256 devices in a mesh: slab: 4 (over y), row: 4 (over x), col: 16 (over z, core).
Axes of the slice: x: 4, y: 4, z: 8, core: 2. Of those that a mesh axis runs over, the one named last changes fastest.
Arguments:
- right_sides: float32 [4, 32, 65536], P('slab', None, ('col', 'row')), may hold values from -6 to 6
- front_tiles: bfloat16 [4, 8192, 128, 128], P('slab', ('col', 'row'))
- tile_rows: int32 [4, 8192], P('slab', ('col', 'row')), may hold values from 0 to 511, as said below
- tile_cols: int32 [4, 8192], P('slab', ('col', 'row')), may hold values from 0 to 511, as said below
- section_blocks: int32 [4], P('slab'), may hold values from 4 to 8, as said below
- plane_map: int32 [4, 16384], P('slab', ('col', 'row')), may hold values from 0 to 511
- interface_coef: float32 [4, 16384], P('slab', ('col', 'row')), may hold values from 0.5 to 1
Outputs:
- solution: float32 [4, 32, 65536], P('slab', None, ('col', 'row'))
The draws below stay inside these ranges and needn't reach their ends.
Inputs may be any that keep to these rules, and one draw needn't show every extreme that they name: `tile_rows`: tile t of a section lies on the device of piece t // 128, which is col index c and row index r with piece c * 4 + r; its row block lies among the 32 blocks of pieces c * 4 to c * 4 + 3, and its column block lies in a piece whose index is r modulo 4. Every block of a device's own piece has a tile with equal row and column block on that device. Several tiles may share a row block and a column block. `tile_cols`: see tile_rows. `section_blocks`: some slab section has all 8 blocks of every piece.
All inputs are finite; a program needn't handle non-finite values.
Results may differ from the reference program's by a relative error of at most 0.0039.
Values may be sent and summed in bfloat16 or wider, within the bound.
No kernel may reach another device: no remote copies, remote signals or barrier semaphores. Data moves between devices by JAX's collectives and lax.ppermute only.
A program may use at most 64 MiB of HBM per device.

```python
import jax
import jax.numpy as jnp
from jax import lax

B = 128
BLK_DEV = 8
TILE_DEV = 128
PLANE_DEV = 256
ROW_DEVS = 4
COL_DEVS = 16
NSLAB = 4
RHS = 32
PIECE = 1024
NB = 512
U = 65536
NTILE = 8192
PLANE = 16384


def tile_pattern(key):
    base_key = jax.random.fold_in(key, 17)
    keys = jax.random.split(base_key, 4)
    devices = ROW_DEVS * COL_DEVS
    dev_index = jnp.arange(devices, dtype=jnp.int32)
    col_of = dev_index // ROW_DEVS
    row_of = dev_index % ROW_DEVS
    own_blocks = dev_index[:, None] * BLK_DEV + jnp.arange(BLK_DEV, dtype=jnp.int32)[None, :]
    own_blocks = jnp.broadcast_to(own_blocks[None, :, :], (NSLAB, devices, BLK_DEV))
    extra = TILE_DEV - BLK_DEV
    out_rows = col_of[None, :, None] * (ROW_DEVS * BLK_DEV) + jax.random.randint(keys[0], (NSLAB, devices, extra), 0, ROW_DEVS * BLK_DEV)
    pick_col = jax.random.randint(keys[1], (NSLAB, devices, extra), 0, COL_DEVS)
    pick_block = jax.random.randint(keys[2], (NSLAB, devices, extra), 0, BLK_DEV)
    in_cols = (pick_col * ROW_DEVS + row_of[None, :, None]) * BLK_DEV + pick_block
    all_rows = jnp.concatenate([own_blocks, out_rows], axis=2)
    all_cols = jnp.concatenate([own_blocks, in_cols], axis=2)
    diagonal = jnp.concatenate([jnp.ones((NSLAB, devices, BLK_DEV), jnp.int32), jnp.zeros((NSLAB, devices, extra), jnp.int32)], axis=2)
    perm_keys = jax.random.split(keys[3], NSLAB * devices)
    orders = jax.vmap(lambda single: jax.random.permutation(single, TILE_DEV))(perm_keys).reshape(NSLAB, devices, TILE_DEV)
    all_rows = jnp.take_along_axis(all_rows, orders, axis=2).reshape(NSLAB, NTILE)
    all_cols = jnp.take_along_axis(all_cols, orders, axis=2).reshape(NSLAB, NTILE)
    diagonal = jnp.take_along_axis(diagonal, orders, axis=2).reshape(NSLAB, NTILE)
    return (all_rows.astype(jnp.int32), all_cols.astype(jnp.int32), diagonal)


def draw_front_tiles(key, part):
    all_rows, all_cols, diagonal = tile_pattern(key)
    noise_key = jax.random.fold_in(key, 29)
    noise = jax.random.normal(noise_key, (NSLAB, NTILE, B, B), jnp.float32)
    off_scale = 0.7 / jnp.sqrt(jnp.float32(B * TILE_DEV / BLK_DEV))
    diag_scale = 0.5 / jnp.sqrt(jnp.float32(B))
    flag = diagonal[:, :, None, None].astype(jnp.float32)
    tiles = noise * (flag * diag_scale + (1.0 - flag) * off_scale) + flag * jnp.eye(B, dtype=jnp.float32)[None, None, :, :]
    return tiles.astype(jnp.bfloat16)


def draw_tile_rows(key, part):
    return tile_pattern(key)[0]


def draw_tile_cols(key, part):
    return tile_pattern(key)[1]


def draw_section_blocks(key, part):
    first_key, second_key = jax.random.split(jax.random.fold_in(key, 41))
    base_blocks = BLK_DEV // 2 + jax.random.randint(first_key, (NSLAB,), 0, BLK_DEV // 2 + 1)
    full_slab = jax.random.randint(second_key, (), 0, NSLAB)
    return jnp.where(jnp.arange(NSLAB) == full_slab, BLK_DEV, base_blocks).astype(jnp.int32)


def with_ends(values, stream_key, low, high):
    dims = values.shape
    place = [jax.random.randint(jax.random.fold_in(stream_key, axis), (), 0, dims[axis]) for axis in range(len(dims))]
    values = values.at[tuple(place)].set(low)
    longest = dims.index(max(dims))
    place[longest] = (place[longest] + 1) % dims[longest]
    return values.at[tuple(place)].set(high)


def shard_levels(key, shape, shards, low, largest):
    level, own = 1.0, jax.random.fold_in(key, 6)
    for axis_at, parts in shards:
        heights = jnp.exp(jax.random.uniform(jax.random.fold_in(own, axis_at), (parts,), jnp.float32, low / len(shards), largest / len(shards)))
        level = level * jnp.repeat(heights, shape[axis_at] // parts).reshape([-1 if axis == axis_at else 1 for axis in range(len(shape))])
    return level


def bell_draw(rng, shape, spread, most, cuts=(), held_as=jnp.bfloat16):
    result = jax.random.normal(rng, shape, jnp.float32) * spread
    if len(cuts) > 0:
        result = shard_levels(rng, shape, cuts, -0.22, 0.18) * result
    return jnp.clip(result, min=-most, max=most).astype(held_as)


def setup_inputs(seed: int = 0) -> dict:
    seeds = jax.random.split(jax.random.key(seed), 8)
    return {
        "right_sides": bell_draw(seeds[0], (NSLAB, RHS, U), 1.0, 6.0, ((0, 4), (2, 64)), jnp.float32),
        "front_tiles": draw_front_tiles(jax.random.fold_in(seeds[7], 71), 0),
        "tile_rows": draw_tile_rows(jax.random.fold_in(seeds[7], 71), 0),
        "tile_cols": draw_tile_cols(jax.random.fold_in(seeds[7], 71), 0),
        "section_blocks": draw_section_blocks(jax.random.fold_in(seeds[7], 71), 0),
        "plane_map": with_ends(jax.random.randint(seeds[5], (NSLAB, PLANE), 0, BLK_DEV // 2 * B), jax.random.fold_in(seeds[5], 1), 0, (BLK_DEV // 2 * B) - 1).astype(jnp.int32),
        "interface_coef": jnp.clip(0.5 + 0.5 * jax.random.uniform(seeds[6], (NSLAB, PLANE), jnp.float32) ** shard_levels(seeds[6], (NSLAB, PLANE), ((0, 4), (1, 64)), -0.2, 0.2), 0.5, 1.0),
    }


def front_apply(front, rows_index, cols_index, vector):
    batch_rows = vector.shape[0]
    blocks = vector.astype(jnp.bfloat16).reshape(batch_rows, NB, B)

    def add_group(summed, members):
        tile_group, row_group, col_group = members
        picked = jnp.take(blocks, col_group, axis=1).astype(jnp.float32)
        products = jnp.einsum("wtk,tjk->wtj", picked, tile_group.astype(jnp.float32))
        return summed.at[:, row_group].add(products), None

    groups = (front.reshape(NTILE // TILE_DEV, TILE_DEV, B, B), rows_index.reshape(NTILE // TILE_DEV, TILE_DEV), cols_index.reshape(NTILE // TILE_DEV, TILE_DEV))
    summed, _ = lax.scan(add_group, jnp.zeros((batch_rows, NB, B), jnp.float32), groups)
    return summed.reshape(batch_rows, U)


def reference(right_sides, front_tiles, tile_rows, tile_cols, section_blocks, plane_map, interface_coef):
    positions = jnp.arange(U, dtype=jnp.int32)
    plane_index = jnp.arange(PLANE, dtype=jnp.int32)
    plane_piece = (plane_index // PLANE_DEV).astype(jnp.int32)
    plane_target = (plane_piece * PIECE + plane_index % PLANE_DEV).astype(jnp.int32)
    swept = []
    actives = []
    previous = None
    for slab_number in range(NSLAB):
        active = ((positions % PIECE) < section_blocks[slab_number] * B).astype(jnp.float32)
        actives.append(active)
        source = right_sides[slab_number]
        if slab_number > 0:
            partner = (plane_piece * PIECE + plane_map[slab_number]).astype(jnp.int32)
            pulled = previous[:, partner] * interface_coef[slab_number][None, :]
            source = source.at[:, plane_target].add(-pulled)
        current = active[None, :] * front_apply(front_tiles[slab_number], tile_rows[slab_number], tile_cols[slab_number], active[None, :] * source)
        swept.append(current)
        previous = current
    solved = [None] * NSLAB
    solved[NSLAB - 1] = swept[NSLAB - 1]
    for slab_number in range(NSLAB - 2, -1, -1):
        upper_sol = solved[slab_number + 1]
        partner = (plane_piece * PIECE + plane_map[slab_number + 1]).astype(jnp.int32)
        weighted = upper_sol[:, plane_target] * interface_coef[slab_number + 1][None, :]
        lifted = jnp.zeros_like(upper_sol).at[:, partner].add(weighted)
        correction = front_apply(front_tiles[slab_number], tile_rows[slab_number], tile_cols[slab_number], lifted)
        solved[slab_number] = swept[slab_number] - actives[slab_number][None, :] * correction
    return jnp.stack(solved)
```

```python
import functools

import jax
import jax.numpy as jnp
from jax import lax
from jax.experimental import pallas as pl
from jax.experimental.pallas import tpu as pltpu
from jax.sharding import PartitionSpec as P

B = 128
BLK = 8
NROW = 4
NCOL = 16
NSLAB = 4
W = 32
NT = 128
UNROLL = 8
TGT = 2
PRT = 4
LST = NT + UNROLL
BF = jnp.bfloat16
F32 = jnp.float32


def whole(shape):
    return pl.BlockSpec(shape, lambda *_: (0,) * len(shape))


def smem():
    return pl.BlockSpec(memory_space=pltpu.SMEM)


def lists_kernel(rows_ref, cols_ref, pos_ref, out_ref):
    base = pos_ref[0] * (NROW * BLK)

    def clear(i, _):
        for k in range(2):
            out_ref[3 * k, i] = 0
            out_ref[3 * k + 1, i] = NROW * BLK
            out_ref[3 * k + 2, i] = 0
        return 0

    lax.fori_loop(0, LST, clear, 0)

    def step(t, counts):
        row = rows_ref[0, t] - base
        col = cols_ref[0, t]
        part = col // (BLK * NROW)
        blk = col % BLK
        slot = (part % 2) * (NCOL // 2) + part // 2
        out_ref[7, t] = row
        out_ref[8, t] = slot * BLK + blk
        new = []
        for k, width in ((0, TGT), (1, PRT)):
            n = counts[k]
            out_ref[3 * k, n] = t
            out_ref[3 * k + 1, n] = row
            out_ref[3 * k + 2, n] = part * width + blk
            new.append(n + (blk < width).astype(jnp.int32))
        return tuple(new)

    counts = lax.fori_loop(0, NT, step, (0, 0))
    for k in range(2):
        n = counts[k]
        out_ref[3 * k, n] = 0
        out_ref[3 * k + 1, n] = NROW * BLK
        out_ref[3 * k + 2, n] = 0
        out_ref[6, k] = (n + UNROLL - 1) // UNROLL


def make_lists(tile_rows, tile_cols, col_index):
    return pl.pallas_call(
        lists_kernel,
        out_shape=jax.ShapeDtypeStruct((9, LST), jnp.int32),
        in_specs=[smem(), smem(), smem()],
        out_specs=smem(),
        name="lists",
    )(tile_rows, tile_cols, col_index)


def product(v, tile):
    return lax.dot_general(v, tile, (((1,), (1,)), ((), ())), preferred_element_type=F32)


def write_message(acc, msg_ref, kind):
    for r in range(NROW):
        if kind == "final":
            for b in range(BLK):
                msg_ref[r, b] = acc[r * BLK + b]
        else:
            for b in range(PRT if kind == "down" else TGT):
                part = acc[r * BLK + b].astype(BF)
                for s in range(NSLAB):
                    msg_ref[s * NROW + r, b] = part


def message_shape(kind):
    if kind == "final":
        return (NROW, BLK, W, B), F32
    return (NSLAB * NROW, PRT if kind == "down" else TGT, W, B), BF


def first_kernel(lst, v_ref, tiles_ref, acc_out, msg_ref, *, kind):
    acc_out[...] = jnp.zeros_like(acc_out)

    def group(g, _):
        base = g * UNROLL
        done = []
        for u in range(UNROLL):
            done.append(product(v_ref[lst[8, base + u]], tiles_ref[base + u]))
        for u in range(UNROLL):
            acc_out[lst[7, base + u]] += done[u]
        return 0

    lax.fori_loop(0, NT // UNROLL, group, 0)
    write_message(acc_out, msg_ref, kind)


def first_apply(lst, gathered, tiles, kind):
    shape, dtype = message_shape(kind)
    return pl.pallas_call(
        functools.partial(first_kernel, kind=kind),
        out_shape=(
            jax.ShapeDtypeStruct((NROW * BLK, W, B), F32),
            jax.ShapeDtypeStruct(shape, dtype),
        ),
        in_specs=[smem(), whole(gathered.shape), whole(tiles.shape)],
        out_specs=(whole((NROW * BLK, W, B)), whole(shape)),
        grid=(1,),
        name="first",
    )(lst, gathered, tiles)


def step_kernel(lst, flag, v_ref, tiles_ref, acc_in, acc_out, msg_ref, acc, buf, sems, *, which, kind):
    groups = lst[6, which] * flag[0]
    count = groups * UNROLL
    first = 3 * which

    def copy(i):
        return pltpu.make_async_copy(tiles_ref.at[lst[first, i]], buf.at[i], sems.at[i])

    def start(i, _):
        copy(i).start()
        return 0

    lax.fori_loop(0, count, start, 0)
    acc[: NROW * BLK] = acc_in[...]

    def group(g, _):
        base = g * UNROLL
        done = []
        for u in range(UNROLL):
            copy(base + u).wait()
        for u in range(UNROLL):
            done.append(product(v_ref[lst[first + 2, base + u]], buf[base + u]))
        for u in range(UNROLL):
            acc[lst[first + 1, base + u]] += done[u]
        return 0

    lax.fori_loop(0, groups, group, 0)
    if kind != "final":
        acc_out[...] = acc[: NROW * BLK]
    write_message(acc, msg_ref, kind)


def step_apply(lst, flag, gathered, tiles, acc, which, kind):
    shape, dtype = message_shape(kind)
    return pl.pallas_call(
        functools.partial(step_kernel, which=which, kind=kind),
        out_shape=(
            jax.ShapeDtypeStruct((NROW * BLK, W, B), F32),
            jax.ShapeDtypeStruct(shape, dtype),
        ),
        in_specs=[
            smem(),
            smem(),
            whole(gathered.shape),
            pl.BlockSpec(memory_space=pl.ANY),
            whole((NROW * BLK, W, B)),
        ],
        out_specs=(whole((NROW * BLK, W, B)), whole(shape)),
        grid=(1,),
        scratch_shapes=[
            pltpu.VMEM((NROW * BLK + 1, W, B), F32),
            pltpu.VMEM((LST, B, B), BF),
            pltpu.SemaphoreType.DMA((LST,)),
        ],
        input_output_aliases={4: 0},
        name="step_" + kind,
    )(lst, flag, gathered, tiles, acc)


def split3(x):
    high = x.astype(BF)
    rest = x - high.astype(F32)
    mid = rest.astype(BF)
    low = (rest - mid.astype(F32)).astype(BF)
    return jnp.concatenate([high, mid, low], axis=0)


def down_kernel(pos, rcv_ref, rhs_ref, coef_ref, hot_ref, out_ref):
    total = jnp.zeros((3 * W, TGT * B), F32)
    for b in range(PRT):
        part = rcv_ref[0, b].astype(F32)
        for r in range(1, NROW):
            part = part + rcv_ref[r, b].astype(F32)
        total = total + jnp.dot(
            split3(part), hot_ref[b * B : (b + 1) * B, :], preferred_element_type=F32
        )
    picked = total[:W] + total[W : 2 * W] + total[2 * W :]
    for b in range(TGT):
        cols = slice(b * B, (b + 1) * B)
        out_ref[b] = (rhs_ref[b] - picked[:, cols] * coef_ref[:, cols]).astype(BF)


def up_kernel(pos, rcv_ref, coef_ref, hot_ref, out_ref):
    total = jnp.zeros((3 * W, PRT * B), F32)
    for b in range(TGT):
        part = rcv_ref[0, b].astype(F32)
        for r in range(1, NROW):
            part = part + rcv_ref[r, b].astype(F32)
        part = part * coef_ref[:, b * B : (b + 1) * B]
        total = total + jnp.dot(
            split3(part), hot_ref[b * B : (b + 1) * B, :], preferred_element_type=F32
        )
    lifted = total[:W] + total[W : 2 * W] + total[2 * W :]
    for b in range(PRT):
        out_ref[b] = (-lifted[:, b * B : (b + 1) * B]).astype(BF)


def combine(kernel, pos, received, others, blocks, name):
    tail = received.shape[1:]
    return pl.pallas_call(
        kernel,
        out_shape=jax.ShapeDtypeStruct((blocks, W, B), BF),
        grid_spec=pltpu.PrefetchScalarGridSpec(
            num_scalar_prefetch=1,
            grid=(1,),
            in_specs=[pl.BlockSpec((NROW, *tail), lambda i, p: (p[0], 0, 0, 0))]
            + [whole(o.shape) for o in others],
            out_specs=whole((blocks, W, B)),
        ),
        name=name,
    )(pos, received, *others)


Z_GROUPS = [[2 * z + k for z in range(NCOL // 2)] for k in range(2)]
CORE_GROUPS = [[2 * z, 2 * z + 1] for z in range(NCOL // 2)]


def gather_first(value):
    copies = jnp.broadcast_to(value[None], (NCOL // 2, *value.shape))
    along = lax.all_to_all(copies, "col", 0, 0, tiled=True, axis_index_groups=Z_GROUPS)
    both = lax.all_gather(along, "col", axis_index_groups=CORE_GROUPS)
    return both.reshape(NCOL * value.shape[0], W, B)


def gather_step(value):
    return lax.all_gather(value, "col").reshape(NCOL * value.shape[0], W, B)


def exchange(message):
    return lax.all_to_all(message, ("slab", "row"), 0, 0, tiled=True)


def body(right_sides, front_tiles, tile_rows, tile_cols, section_blocks, plane_map, interface_coef):
    slab = lax.axis_index("slab").astype(jnp.int32)
    col = lax.axis_index("col").astype(jnp.int32)
    tiles = front_tiles[0]
    pack = jnp.concatenate([interface_coef, plane_map.astype(F32)], axis=0)
    pack_next = lax.ppermute(pack, "slab", [(s + 1, s) for s in range(NSLAB - 1)])
    coef_next = pack_next[0:1]
    map_next = pack_next[1].astype(jnp.int32)
    lst = make_lists(tile_rows, tile_cols, col.reshape(1))

    source = right_sides[0].reshape(W, BLK, B).transpose(1, 0, 2)
    blk = jnp.arange(BLK, dtype=jnp.int32)
    keep = (blk < section_blocks[0]) & ((slab == 0) | (blk >= TGT))
    v0 = jnp.where(keep[:, None, None], source, 0.0).astype(BF)
    rhs_target = source[:TGT]
    partner = jnp.arange(PRT * B, dtype=jnp.int32)
    hot_own = (partner[:, None] == plane_map[0][None, :]).astype(BF)
    hot_next = (map_next[:, None] == partner[None, :]).astype(BF)

    acc, msg = first_apply(lst, gather_first(v0), tiles, "down")
    before = jnp.maximum(slab - 1, 0).reshape(1)
    after = jnp.minimum(slab + 1, NSLAB - 1).reshape(1)
    for s in range(1, NSLAB):
        rcv = exchange(msg)
        v = combine(down_kernel, before, rcv, (rhs_target, interface_coef, hot_own), TGT, "down")
        flag = (slab == s).astype(jnp.int32).reshape(1)
        kind = "down" if s < NSLAB - 1 else "up"
        acc, msg = step_apply(lst, flag, gather_step(v), tiles, acc, 0, kind)
    for s in range(NSLAB - 2, -1, -1):
        rcv = exchange(msg)
        v = combine(up_kernel, after, rcv, (coef_next, hot_next), PRT, "up")
        flag = (slab == s).astype(jnp.int32).reshape(1)
        kind = "up" if s > 0 else "final"
        acc, msg = step_apply(lst, flag, gather_step(v), tiles, acc, 1, kind)
    parts = lax.all_to_all(msg, "row", 0, 0, tiled=True)
    total = jnp.sum(parts, axis=0)
    total = jnp.where((blk < section_blocks[0])[:, None, None], total, 0.0)
    return total.transpose(1, 0, 2).reshape(1, W, BLK * B)


def solution(mesh):
    placed = (
        P("slab", None, ("col", "row")),
        P("slab", ("col", "row"), None, None),
        P("slab", ("col", "row")),
        P("slab", ("col", "row")),
        P("slab"),
        P("slab", ("col", "row")),
        P("slab", ("col", "row")),
    )
    return jax.shard_map(
        body, mesh=mesh, in_specs=placed, out_specs=P("slab", None, ("col", "row")), check_vma=False
    )
```

```python
import functools

import jax
import jax.numpy as jnp
from jax import lax
from jax.experimental import pallas as pl
from jax.experimental.pallas import tpu as pltpu
from jax.sharding import PartitionSpec as P

B = 128
BLK = 8
NROW = 4
NCOL = 16
NSLAB = 4
W = 32
NT = 128
UNROLL = 8
TGT = 2
PRT = 4
LST = NT + UNROLL
BF = jnp.bfloat16
F32 = jnp.float32


def smem():
    return pl.BlockSpec(memory_space=pltpu.SMEM)


def vmem():
    return pl.BlockSpec(memory_space=pltpu.VMEM)


PARAMS = pltpu.CompilerParams(vmem_limit_bytes=24 * 2**20)
ACC = (NROW * BLK + 1, W, B)
LISTS = 4
TAB, TC, LA, LALL = range(LISTS)


def lists_kernel(rows_ref, cols_ref, pos_ref, out_ref):
    base = pos_ref[0] * (NROW * BLK)

    def step(t, counts):
        row = rows_ref[0, t] - base
        col = cols_ref[0, t]
        part = col // (BLK * NROW)
        blk = col % BLK
        out = row % BLK
        head = t + row * NT
        wide = head + (part * PRT + blk) * (64 * NT)
        narrow = head + (part * TGT + blk) * (64 * NT)
        target = blk < TGT
        low = blk < PRT
        member = (
            (narrow, target & (out < PRT)),
            (narrow, target & (out >= PRT)),
            (wide, low & (out < TGT)),
            (wide, low),
        )
        for k in range(LISTS):
            out_ref[k, counts[k]] = member[k][0]
        return tuple(counts[k] + member[k][1].astype(jnp.int32) for k in range(LISTS))

    counts = lax.fori_loop(0, NT, step, (0,) * LISTS)
    for k in range(LISTS):
        for u in range(UNROLL):
            out_ref[k, counts[k] + u] = NROW * BLK * NT
        out_ref[LISTS, k] = (counts[k] + UNROLL - 1) // UNROLL


def make_lists(tile_rows, tile_cols, col_index):
    return pl.pallas_call(
        lists_kernel,
        out_shape=jax.ShapeDtypeStruct((LISTS + 1, LST), jnp.int32),
        in_specs=[smem(), smem(), smem()],
        out_specs=smem(),
        name="lists",
    )(tile_rows, tile_cols, col_index)


def product(v, tile):
    return lax.dot_general(v, tile, (((1,), (1,)), ((), ())), preferred_element_type=F32)


def apply_list(lst, which, v_ref, tiles_ref, acc):
    def group(g, _):
        entries = [lst[which, g * UNROLL + u] for u in range(UNROLL)]
        done = [product(v_ref[e // (64 * NT)], tiles_ref[e % NT]) for e in entries]
        for e, d in zip(entries, done):
            acc[e // NT % 64] += d
        return 0

    lax.fori_loop(0, lst[LISTS, which], group, 0)


def write_message(acc, msg_ref, kind):
    for r in range(NROW):
        if kind == "final":
            for b in range(BLK):
                msg_ref[r, b] = acc[r * BLK + b]
        else:
            for b in range(PRT if kind == "down" else TGT):
                part = acc[r * BLK + b].astype(BF)
                for s in range(NSLAB):
                    msg_ref[s * NROW + r, b] = part


def message_shape(kind):
    if kind == "final":
        return jax.ShapeDtypeStruct((NROW, BLK, W, B), F32)
    return jax.ShapeDtypeStruct((NSLAB * NROW, PRT if kind == "down" else TGT, W, B), BF)


def first_kernel(rows_ref, cols_ref, pos, own_ref, other_ref, tiles_ref, acc, msg_ref):
    acc[...] = jnp.zeros(ACC, F32)
    base = pos[0] * (NROW * BLK)
    core = pos[0] % 2

    def group(g, _):
        rows, done = [], []
        for u in range(UNROLL):
            t = g * UNROLL + u
            col = cols_ref[0, t]
            part = col // (BLK * NROW)
            at = part // 2 * BLK + col % BLK
            v = jnp.where(part % 2 == core, own_ref[at], other_ref[at])
            rows.append(rows_ref[0, t] - base)
            done.append(product(v, tiles_ref[t]))
        for r, d in zip(rows, done):
            acc[r] += d
        return 0

    lax.fori_loop(0, NT // UNROLL, group, 0)
    write_message(acc, msg_ref, "down")


def first_apply(tile_rows, tile_cols, pos, own, other, tiles):
    return pl.pallas_call(
        first_kernel,
        out_shape=(jax.ShapeDtypeStruct(ACC, F32), message_shape("down")),
        in_specs=[smem(), smem(), smem(), vmem(), vmem(), vmem()],
        out_specs=(vmem(), vmem()),
        compiler_params=PARAMS,
        name="first",
    )(tile_rows, tile_cols, pos, own, other, tiles)


def down_step_kernel(lst, flag, v_ref, tiles_ref, acc_in, acc, msg_ref, *, kind):
    @pl.when(flag[0] == 1)
    def _():
        apply_list(lst, TAB, v_ref, tiles_ref, acc)

    write_message(acc, msg_ref, kind)


def down_step(lst, flag, gathered, tiles, acc, kind):
    return pl.pallas_call(
        functools.partial(down_step_kernel, kind=kind),
        out_shape=(jax.ShapeDtypeStruct(ACC, F32), message_shape(kind)),
        in_specs=[smem(), smem(), vmem(), vmem(), vmem()],
        out_specs=(vmem(), vmem()),
        input_output_aliases={4: 0},
        compiler_params=PARAMS,
        name="down_step",
    )(lst, flag, gathered, tiles, acc)


def up_step_kernel(lst, flag, v_ref, tiles_ref, acc_in, msg_ref, acc):
    for r in range(NROW):
        for b in range(TGT):
            acc[r * BLK + b] = acc_in[r * BLK + b]

    @pl.when(flag[0] == 1)
    def _():
        apply_list(lst, LA, v_ref, tiles_ref, acc)

    write_message(acc, msg_ref, "up")


def up_step(lst, flag, gathered, tiles, acc):
    return pl.pallas_call(
        up_step_kernel,
        out_shape=message_shape("up"),
        in_specs=[smem(), smem(), vmem(), vmem(), vmem()],
        out_specs=vmem(),
        scratch_shapes=[pltpu.VMEM(ACC, F32)],
        compiler_params=PARAMS,
        name="up_step",
    )(lst, flag, gathered, tiles, acc)


def last_kernel(lst, pos, tiles_ref, v1, v2, v3, l2, l1, l0, acc_in, acc, msg_ref):
    for s, v_ref in ((1, v1), (2, v2), (3, v3)):
        @pl.when(pos[0] == s)
        def _(v_ref=v_ref):
            apply_list(lst, TC, v_ref, tiles_ref, acc)

    for s, v_ref in ((2, l2), (1, l1), (0, l0)):
        @pl.when(pos[0] == s)
        def _(v_ref=v_ref):
            apply_list(lst, LALL, v_ref, tiles_ref, acc)

    write_message(acc, msg_ref, "final")


def last_apply(lst, slab, tiles, downs, ups, acc):
    return pl.pallas_call(
        last_kernel,
        out_shape=(jax.ShapeDtypeStruct(ACC, F32), message_shape("final")),
        in_specs=[smem(), smem()] + [vmem()] * 8,
        out_specs=(vmem(), vmem()),
        input_output_aliases={9: 0},
        compiler_params=PARAMS,
        name="last",
    )(lst, slab, tiles, *downs, *ups, acc)[1]


def split(x):
    high = x.astype(BF)
    rest = x - high.astype(F32)
    return jnp.concatenate([high, rest.astype(BF)], axis=0)


def row_total(rcv_ref, pos, b):
    part = rcv_ref[pos[0] * NROW, b].astype(F32)
    for r in range(1, NROW):
        part = part + rcv_ref[pos[0] * NROW + r, b].astype(F32)
    return part


def down_kernel(pos, rcv_ref, rhs_ref, coef_ref, hot_ref, out_ref):
    values = jnp.concatenate([split(row_total(rcv_ref, pos, b)) for b in range(PRT)], axis=1)
    total = jnp.dot(values, hot_ref[...], preferred_element_type=F32)
    picked = total[:W] + total[W:]
    for b in range(TGT):
        cols = slice(b * B, (b + 1) * B)
        out_ref[b] = (rhs_ref[b] - picked[:, cols] * coef_ref[:, cols]).astype(BF)


def up_kernel(pos, rcv_ref, coef_ref, hot_ref, out_ref):
    values = jnp.concatenate(
        [
            split(row_total(rcv_ref, pos, b) * coef_ref[:, b * B : (b + 1) * B])
            for b in range(TGT)
        ],
        axis=1,
    )
    total = jnp.dot(values, hot_ref[...], preferred_element_type=F32)
    lifted = total[:W] + total[W:]
    for b in range(PRT):
        out_ref[b] = (-lifted[:, b * B : (b + 1) * B]).astype(BF)


def combine(kernel, pos, received, others, blocks, name):
    return pl.pallas_call(
        kernel,
        out_shape=jax.ShapeDtypeStruct((blocks, W, B), BF),
        in_specs=[smem()] + [vmem()] * (1 + len(others)),
        out_specs=vmem(),
        compiler_params=PARAMS,
        name=name,
    )(pos, received, *others)


Z_GROUPS = [[2 * z + k for z in range(NCOL // 2)] for k in range(2)]


def gather_first(value):
    copies = jnp.broadcast_to(value[None], (NCOL // 2, *value.shape))
    along = lax.all_to_all(copies, "col", 0, 0, tiled=True, axis_index_groups=Z_GROUPS)
    along = along.reshape(NCOL // 2 * value.shape[0], W, B)
    return along, lax.ppermute(along, "col", [(c, c ^ 1) for c in range(NCOL)])


def gather_step(value):
    return lax.all_gather(value, "col").reshape(NCOL * value.shape[0], W, B)


def exchange(message):
    return lax.all_to_all(message, ("slab", "row"), 0, 0, tiled=True)


def body(right_sides, front_tiles, tile_rows, tile_cols, section_blocks, plane_map, interface_coef):
    slab = lax.axis_index("slab").astype(jnp.int32)
    col = lax.axis_index("col").astype(jnp.int32)
    tiles = front_tiles[0]
    pack = jnp.concatenate([interface_coef, plane_map.astype(F32)], axis=0)
    pack_next = lax.ppermute(pack, "slab", [(s + 1, s) for s in range(NSLAB - 1)])
    coef_next = pack_next[0:1]
    map_next = pack_next[1].astype(jnp.int32)
    lst = make_lists(tile_rows, tile_cols, col.reshape(1))

    source = right_sides[0].reshape(W, BLK, B).transpose(1, 0, 2)
    blk = jnp.arange(BLK, dtype=jnp.int32)
    keep = (blk < section_blocks[0]) & ((slab == 0) | (blk >= TGT))
    v0 = jnp.where(keep[:, None, None], source, 0.0).astype(BF)
    rhs_target = source[:TGT]
    partner = jnp.arange(PRT * B, dtype=jnp.int32)
    hot_own = (partner[:, None] == plane_map[0][None, :]).astype(BF)
    hot_next = (map_next[:, None] == partner[None, :]).astype(BF)

    own, other = gather_first(v0)
    acc, msg = first_apply(tile_rows, tile_cols, col.reshape(1), own, other, tiles)
    before = jnp.maximum(slab - 1, 0).reshape(1)
    after = jnp.minimum(slab + 1, NSLAB - 1).reshape(1)
    downs, ups = [], []
    for s in range(1, NSLAB):
        rcv = exchange(msg)
        v = combine(down_kernel, before, rcv, (rhs_target, interface_coef, hot_own), TGT, "down")
        downs.append(gather_step(v))
        flag = (slab == s).astype(jnp.int32).reshape(1)
        kind = "down" if s < NSLAB - 1 else "up"
        acc, msg = down_step(lst, flag, downs[-1], tiles, acc, kind)
    for s in range(NSLAB - 2, -1, -1):
        rcv = exchange(msg)
        v = combine(up_kernel, after, rcv, (coef_next, hot_next), PRT, "up")
        ups.append(gather_step(v))
        if s > 0:
            flag = (slab == s).astype(jnp.int32).reshape(1)
            msg = up_step(lst, flag, ups[-1], tiles, acc)
    msg = last_apply(lst, slab.reshape(1), tiles, downs, ups, acc)
    parts = lax.all_to_all(msg, "row", 0, 0, tiled=True)
    total = jnp.sum(parts, axis=0)
    total = jnp.where((blk < section_blocks[0])[:, None, None], total, 0.0)
    return total.transpose(1, 0, 2).reshape(1, W, BLK * B)


def solution(mesh):
    placed = (
        P("slab", None, ("col", "row")),
        P("slab", ("col", "row"), None, None),
        P("slab", ("col", "row")),
        P("slab", ("col", "row")),
        P("slab"),
        P("slab", ("col", "row")),
        P("slab", ("col", "row")),
    )
    return jax.shard_map(
        body, mesh=mesh, in_specs=placed, out_specs=P("slab", None, ("col", "row")), check_vma=False
    )
```

```python
import functools

import jax
import jax.numpy as jnp
from jax import lax
from jax.experimental import pallas as pl
from jax.experimental.pallas import tpu as pltpu
from jax.sharding import PartitionSpec as P

B = 128
BLK = 8
NROW = 4
NCOL = 16
NSLAB = 4
W = 32
NT = 128
UNROLL = 8
TGT = 2
PRT = 4
LST = NT + UNROLL
BF = jnp.bfloat16
F32 = jnp.float32


def smem():
    return pl.BlockSpec(memory_space=pltpu.SMEM)


def vmem():
    return pl.BlockSpec(memory_space=pltpu.VMEM)


PARAMS = pltpu.CompilerParams(vmem_limit_bytes=24 * 2**20)
ACC = (NROW * BLK + 1, W, B)
LISTS = 4
TAB, TC, LA, LALL = range(LISTS)
HALF = NCOL // 2


def shr(x, n):
    return lax.shift_right_logical(x, jnp.int32(n))


def tile_codes(tile_rows, tile_cols, col_index):
    row = tile_rows - col_index * (NROW * BLK)
    part = tile_cols // (BLK * NROW)
    side = (part % 2 != col_index % 2).astype(jnp.int32)
    return row + 64 * (part // 2) + 512 * side + 1024 * (tile_cols % BLK)


def product(v, tile):
    return lax.dot_general(v, tile, (((1,), (1,)), ((), ())), preferred_element_type=F32)


def picked(side, own_ref, other_ref, at):
    return jnp.where(side == 0, own_ref[at], other_ref[at])


def apply_list(lst, which, pair, tiles_ref, acc):
    def group(g, _):
        rows, done = [], []
        for u in range(UNROLL):
            e = lst[which, g * UNROLL + u]
            v = picked(shr(e, 19), *pair, shr(e, 13) & 63)
            rows.append(shr(e, 7) & 63)
            done.append(product(v, tiles_ref[e & 127]))
        for r, d in zip(rows, done):
            acc[r] += d
        return 0

    lax.fori_loop(0, lst[LISTS, which], group, 0)


def write_down(acc, pos, hot_ref, msg_ref):
    for d in range(NROW):
        r = (pos[1] + d) & (NROW - 1)
        values = jnp.concatenate([acc[r * BLK + b].astype(BF) for b in range(PRT)], axis=1)
        part = jnp.dot(values, hot_ref[d], preferred_element_type=F32).astype(BF)
        for b in range(TGT):
            for s in range(NSLAB):
                msg_ref[s * NROW + r, b] = part[:, b * B : (b + 1) * B]


def write_up(acc, msg_ref):
    for r in range(NROW):
        for b in range(TGT):
            part = acc[r * BLK + b].astype(BF)
            for s in range(NSLAB):
                msg_ref[s * NROW + r, b] = part


MESSAGE = jax.ShapeDtypeStruct((NSLAB * NROW, TGT, W, B), BF)


def first_kernel(codes, pos, own_ref, other_ref, hot_ref, tiles_hbm, acc, tiles_ref, lst, msg_ref, sems):
    def load(g):
        at = pl.ds(pl.multiple_of(g * UNROLL, UNROLL), UNROLL)
        return pltpu.make_async_copy(tiles_hbm.at[at], tiles_ref.at[at], sems.at[g])

    def start(g, _):
        load(g).start()
        return 0

    lax.fori_loop(0, NT // UNROLL, start, 0)
    acc[...] = jnp.zeros(ACC, F32)

    def group(g, counts):
        rows, done = [], []
        load(g).wait()
        for u in range(UNROLL):
            t = g * UNROLL + u
            code = codes[0, t]
            row = code & 63
            half = shr(code, 6) & 7
            side = shr(code, 9) & 1
            blk = shr(code, 10)
            v = picked(side, own_ref, other_ref, half * BLK + blk)
            rows.append(row)
            done.append(product(v, tiles_ref[t]))
            out = row & (BLK - 1)
            head = t + row * NT + side * 2**19
            narrow = head + (half * TGT + blk) * 8192
            wide = head + (half * PRT + blk) * 8192
            target = blk < TGT
            low = blk < PRT
            member = (
                (narrow, target & (out < PRT)),
                (narrow, target & (out >= PRT)),
                (wide, low & (out < TGT)),
                (wide, low),
            )
            for k in range(LISTS):
                lst[k, counts[k]] = member[k][0]
            counts = tuple(
                counts[k] + jnp.where(member[k][1], jnp.int32(1), jnp.int32(0))
                for k in range(LISTS)
            )
        for r, d in zip(rows, done):
            acc[r] += d
        return counts

    counts = lax.fori_loop(0, NT // UNROLL, group, (jnp.int32(0),) * LISTS)
    for k in range(LISTS):
        for u in range(UNROLL):
            lst[k, counts[k] + u] = NROW * BLK * NT
        lst[LISTS, k] = shr(counts[k] + UNROLL - 1, 3)
    write_down(acc, pos, hot_ref, msg_ref)


def first_apply(codes, pos, pair, hots, tiles):
    return pl.pallas_call(
        first_kernel,
        out_shape=(
            jax.ShapeDtypeStruct(ACC, F32),
            jax.ShapeDtypeStruct(tiles.shape, BF),
            jax.ShapeDtypeStruct((LISTS + 1, LST), jnp.int32),
            MESSAGE,
        ),
        in_specs=[smem(), smem(), vmem(), vmem(), vmem(), pl.BlockSpec(memory_space=pltpu.HBM)],
        out_specs=(vmem(), vmem(), smem(), vmem()),
        scratch_shapes=[pltpu.SemaphoreType.DMA((NT // UNROLL,))],
        compiler_params=PARAMS,
        name="first",
    )(codes, pos, *pair, hots, pltpu.with_memory_space_constraint(tiles, pltpu.HBM))


def down_step_kernel(lst, pos, own_ref, other_ref, hot_ref, tiles_ref, acc_in, acc, msg_ref, *, section):
    @pl.when(pos[0] == section)
    def _():
        apply_list(lst, TAB, (own_ref, other_ref), tiles_ref, acc)

    if section < NSLAB - 1:
        write_down(acc, pos, hot_ref, msg_ref)
    else:
        write_up(acc, msg_ref)


def down_step(lst, pos, pair, hots, tiles, acc, section):
    return pl.pallas_call(
        functools.partial(down_step_kernel, section=section),
        out_shape=(jax.ShapeDtypeStruct(ACC, F32), MESSAGE),
        in_specs=[smem(), smem()] + [vmem()] * 5,
        out_specs=(vmem(), vmem()),
        input_output_aliases={6: 0},
        compiler_params=PARAMS,
        name="down_step",
    )(lst, pos, *pair, hots, tiles, acc)


def up_step_kernel(lst, pos, own_ref, other_ref, tiles_ref, acc_in, msg_ref, acc, *, section):
    for r in range(NROW):
        for b in range(TGT):
            acc[r * BLK + b] = acc_in[r * BLK + b]

    @pl.when(pos[0] == section)
    def _():
        apply_list(lst, LA, (own_ref, other_ref), tiles_ref, acc)

    write_up(acc, msg_ref)


def up_step(lst, pos, pair, tiles, acc, section):
    return pl.pallas_call(
        functools.partial(up_step_kernel, section=section),
        out_shape=MESSAGE,
        in_specs=[smem(), smem()] + [vmem()] * 4,
        out_specs=vmem(),
        scratch_shapes=[pltpu.VMEM(ACC, F32)],
        compiler_params=PARAMS,
        name="up_step",
    )(lst, pos, *pair, tiles, acc)


def last_kernel(lst, pos, tiles_ref, *refs):
    gathered, acc, msg_ref = refs[:12], refs[13], refs[14]
    for k, s in enumerate((1, 2, 3, 2, 1, 0)):
        @pl.when(pos[0] == s)
        def _(k=k):
            pair = gathered[2 * k], gathered[2 * k + 1]
            apply_list(lst, TC if k < NSLAB - 1 else LALL, pair, tiles_ref, acc)

    for r in range(NROW):
        for b in range(BLK):
            msg_ref[r, b] = acc[r * BLK + b]


def last_apply(lst, pos, tiles, pairs, acc):
    flat = [ref for pair in pairs for ref in pair]
    return pl.pallas_call(
        last_kernel,
        out_shape=(
            jax.ShapeDtypeStruct(ACC, F32),
            jax.ShapeDtypeStruct((NROW, BLK, W, B), F32),
        ),
        in_specs=[smem(), smem()] + [vmem()] * 14,
        out_specs=(vmem(), vmem()),
        input_output_aliases={15: 0},
        compiler_params=PARAMS,
        name="last",
    )(lst, pos, tiles, *flat, acc)[1]


def split(x):
    high = x.astype(BF)
    rest = x - high.astype(F32)
    return jnp.concatenate([high, rest.astype(BF)], axis=0)


def row_total(rcv_ref, section, b):
    part = rcv_ref[section * NROW, b].astype(F32)
    for r in range(1, NROW):
        part = part + rcv_ref[section * NROW + r, b].astype(F32)
    return part


def down_kernel(pos, rcv_ref, rhs_ref, coef_ref, out_ref):
    before = jnp.maximum(pos[0] - 1, 0)
    for b in range(TGT):
        pulled = row_total(rcv_ref, before, b) * coef_ref[:, b * B : (b + 1) * B]
        value = (rhs_ref[b] - pulled).astype(BF)
        for z in range(HALF):
            out_ref[z, b] = value


def up_kernel(pos, rcv_ref, coef_ref, hot_ref, out_ref):
    after = jnp.minimum(pos[0] + 1, NSLAB - 1)
    values = jnp.concatenate(
        [
            split(row_total(rcv_ref, after, b) * coef_ref[:, b * B : (b + 1) * B])
            for b in range(TGT)
        ],
        axis=1,
    )
    total = jnp.dot(values, hot_ref[...], preferred_element_type=F32)
    lifted = -(total[:W] + total[W:])
    for b in range(PRT):
        value = lifted[:, b * B : (b + 1) * B].astype(BF)
        for z in range(HALF):
            out_ref[z, b] = value


def combine(kernel, pos, received, others, blocks, name):
    return pl.pallas_call(
        kernel,
        out_shape=jax.ShapeDtypeStruct((HALF, blocks, W, B), BF),
        in_specs=[smem()] + [vmem()] * (1 + len(others)),
        out_specs=vmem(),
        compiler_params=PARAMS,
        name=name,
    )(pos, received, *others)


def finish_kernel(count, parts_ref, out_ref):
    for b in range(BLK):
        total = parts_ref[0, b]
        for r in range(1, NROW):
            total = total + parts_ref[r, b]
        out_ref[0, :, b * B : (b + 1) * B] = jnp.where(b < count[0], total, 0.0)


def finish(section_blocks, parts):
    return pl.pallas_call(
        finish_kernel,
        out_shape=jax.ShapeDtypeStruct((1, W, BLK * B), F32),
        in_specs=[smem(), vmem()],
        out_specs=vmem(),
        compiler_params=PARAMS,
        name="finish",
    )(section_blocks, parts)


Z_GROUPS = [[2 * z + k for z in range(HALF)] for k in range(2)]


def gather(copies):
    own = lax.all_to_all(copies, "col", 0, 0, tiled=True, axis_index_groups=Z_GROUPS)
    own = own.reshape(HALF * copies.shape[1], W, B)
    return own, lax.ppermute(own, "col", [(c, c ^ 1) for c in range(NCOL)])


def exchange(message):
    return lax.all_to_all(message, ("slab", "row"), 0, 0, tiled=True)


def from_next(value, turn):
    pairs = [
        ((s + 1) * NROW + (r + turn) % NROW, s * NROW + r)
        for s in range(NSLAB - 1)
        for r in range(NROW)
    ]
    return lax.ppermute(value, ("slab", "row"), pairs)


def body(right_sides, front_tiles, tile_rows, tile_cols, section_blocks, plane_map, interface_coef):
    slab = lax.axis_index("slab").astype(jnp.int32)
    row = lax.axis_index("row").astype(jnp.int32)
    col = lax.axis_index("col").astype(jnp.int32)
    pos = jnp.stack([slab, row])
    codes = tile_codes(tile_rows, tile_cols, col)
    map_own = plane_map.astype(F32)
    pack_next = from_next(jnp.concatenate([map_own, interface_coef], axis=0), 0)
    coef_next = pack_next[1:2]
    maps_next = jnp.concatenate(
        [pack_next[0:1]] + [from_next(map_own, d) for d in range(1, NROW)], axis=0
    ).astype(jnp.int32)

    source = right_sides[0].reshape(W, BLK, B).transpose(1, 0, 2)
    blk = jnp.arange(BLK, dtype=jnp.int32)
    keep = (blk < section_blocks[0]) & ((slab == 0) | (blk >= TGT))
    v0 = jnp.where(keep[:, None, None], source, 0.0).astype(BF)
    rhs_target = source[:TGT]
    partner = jnp.arange(PRT * B, dtype=jnp.int32)
    hots = (partner[None, :, None] == maps_next[:, None, :]).astype(BF)
    hot_next = (maps_next[0][:, None] == partner[None, :]).astype(BF)

    pair = gather(jnp.broadcast_to(v0[None], (HALF, *v0.shape)))
    pair, hots, hot_next, coef_next, rhs_target, codes, pos = lax.optimization_barrier(
        (pair, hots, hot_next, coef_next, rhs_target, codes, pos)
    )
    acc, tiles, lst, msg = first_apply(codes, pos, pair, hots, front_tiles[0])
    pairs = []
    for s in range(1, NSLAB):
        rcv = exchange(msg)
        pairs.append(gather(combine(down_kernel, pos, rcv, (rhs_target, interface_coef), TGT, "down")))
        acc, msg = down_step(lst, pos, pairs[-1], hots, tiles, acc, s)
    for s in range(NSLAB - 2, -1, -1):
        rcv = exchange(msg)
        pairs.append(gather(combine(up_kernel, pos, rcv, (coef_next, hot_next), PRT, "up")))
        if s > 0:
            msg = up_step(lst, pos, pairs[-1], tiles, acc, s)
    msg = last_apply(lst, pos, tiles, pairs, acc)
    parts = lax.all_to_all(msg, "row", 0, 0, tiled=True)
    return finish(section_blocks, parts)


def solution(mesh):
    placed = (
        P("slab", None, ("col", "row")),
        P("slab", ("col", "row"), None, None),
        P("slab", ("col", "row")),
        P("slab", ("col", "row")),
        P("slab"),
        P("slab", ("col", "row")),
        P("slab", ("col", "row")),
    )
    return jax.shard_map(
        body, mesh=mesh, in_specs=placed, out_specs=P("slab", None, ("col", "row")), check_vma=False
    )
```

```python
import functools

import jax
import jax.numpy as jnp
from jax import lax
from jax.experimental import pallas as pl
from jax.experimental.pallas import tpu as pltpu
from jax.sharding import PartitionSpec as P

B = 128
BLK = 8
NROW = 4
NCOL = 16
NSLAB = 4
W = 32
NT = 128
UNROLL = 8
TGT = 2
PRT = 4
LST = NT + UNROLL
BF = jnp.bfloat16
F32 = jnp.float32


def smem():
    return pl.BlockSpec(memory_space=pltpu.SMEM)


def vmem():
    return pl.BlockSpec(memory_space=pltpu.VMEM)


PARAMS = pltpu.CompilerParams(vmem_limit_bytes=24 * 2**20)
ACC = (NROW * BLK + 1, W, B)
LISTS = 4
TAB, TC, LA, LALL = range(LISTS)
HALF = NCOL // 2


def shr(x, n):
    return lax.shift_right_logical(x, jnp.int32(n))


def tile_codes(tile_rows, tile_cols, col_index):
    row = tile_rows - col_index * (NROW * BLK)
    part = tile_cols // (BLK * NROW)
    side = (part % 2 != col_index % 2).astype(jnp.int32)
    return row + 64 * (part // 2) + 512 * side + 1024 * (tile_cols % BLK)


def product(v, tile):
    return lax.dot_general(v, tile, (((1,), (1,)), ((), ())), preferred_element_type=F32)


def picked(side, own_ref, other_ref, at):
    return jnp.where(side == 0, own_ref[at], other_ref[at])


def apply_list(lst, which, pair, tiles_ref, acc):
    def group(g, _):
        rows, done = [], []
        for u in range(UNROLL):
            e = lst[which, g * UNROLL + u]
            v = picked(shr(e, 19), *pair, shr(e, 13) & 63)
            rows.append(shr(e, 7) & 63)
            done.append(product(v, tiles_ref[e & 127]))
        for r, d in zip(rows, done):
            acc[r] += d
        return 0

    lax.fori_loop(0, lst[LISTS, which], group, 0)


def write_down(acc, row, hot_ref, msg_ref):
    for d in range(NROW):
        r = (row[0] + d) & (NROW - 1)
        values = jnp.concatenate([acc[r * BLK + b].astype(BF) for b in range(PRT)], axis=1)
        part = jnp.dot(values, hot_ref[d], preferred_element_type=F32).astype(BF)
        for b in range(TGT):
            for s in range(2):
                msg_ref[s * NROW + r, b] = part[:, b * B : (b + 1) * B]


def write_up(acc, msg_ref):
    for r in range(NROW):
        for b in range(TGT):
            part = acc[r * BLK + b].astype(BF)
            for s in range(2):
                msg_ref[s * NROW + r, b] = part


MESSAGE = jax.ShapeDtypeStruct((2 * NROW, TGT, W, B), BF)


def first_kernel(codes, row_index, own_ref, other_ref, hot_ref, tiles_hbm, acc, tiles_ref, lst, msg_ref, sems):
    def load(g):
        at = pl.ds(pl.multiple_of(g * UNROLL, UNROLL), UNROLL)
        return pltpu.make_async_copy(tiles_hbm.at[at], tiles_ref.at[at], sems.at[g])

    def start(g, _):
        load(g).start()
        return 0

    lax.fori_loop(0, NT // UNROLL, start, 0)
    acc[...] = jnp.zeros(ACC, F32)

    def group(g, counts):
        rows, done = [], []
        load(g).wait()
        for u in range(UNROLL):
            t = g * UNROLL + u
            code = codes[0, t]
            row = code & 63
            half = shr(code, 6) & 7
            side = shr(code, 9) & 1
            blk = shr(code, 10)
            v = picked(side, own_ref, other_ref, half * BLK + blk)
            rows.append(row)
            done.append(product(v, tiles_ref[t]))
            out = row & (BLK - 1)
            head = t + row * NT + side * 2**19
            narrow = head + (half * TGT + blk) * 8192
            wide = head + (half * PRT + blk) * 8192
            target = blk < TGT
            low = blk < PRT
            member = (
                (narrow, target & (out < PRT)),
                (narrow, target & (out >= PRT)),
                (wide, low & (out < TGT)),
                (wide, low),
            )
            for k in range(LISTS):
                lst[k, counts[k]] = member[k][0]
            counts = tuple(
                counts[k] + jnp.where(member[k][1], jnp.int32(1), jnp.int32(0))
                for k in range(LISTS)
            )
        for r, d in zip(rows, done):
            acc[r] += d
        return counts

    counts = lax.fori_loop(0, NT // UNROLL, group, (jnp.int32(0),) * LISTS)
    for k in range(LISTS):
        for u in range(UNROLL):
            lst[k, counts[k] + u] = NROW * BLK * NT
        lst[LISTS, k] = shr(counts[k] + UNROLL - 1, 3)
    write_down(acc, row_index, hot_ref, msg_ref)


def first_apply(codes, row_index, pair, hots, tiles):
    return pl.pallas_call(
        first_kernel,
        out_shape=(
            jax.ShapeDtypeStruct(ACC, F32),
            jax.ShapeDtypeStruct(tiles.shape, BF),
            jax.ShapeDtypeStruct((LISTS + 1, LST), jnp.int32),
            MESSAGE,
        ),
        in_specs=[smem(), smem(), vmem(), vmem(), vmem(), pl.BlockSpec(memory_space=pltpu.HBM)],
        out_specs=(vmem(), vmem(), smem(), vmem()),
        scratch_shapes=[pltpu.SemaphoreType.DMA((NT // UNROLL,))],
        compiler_params=PARAMS,
        name="first",
    )(codes, row_index, *pair, hots, pltpu.with_memory_space_constraint(tiles, pltpu.HBM))


def down_step_kernel(lst, slab, row, own_ref, other_ref, hot_ref, tiles_ref, acc_in, acc, msg_ref, *, section):
    @pl.when(slab[0] == section)
    def _():
        apply_list(lst, TAB, (own_ref, other_ref), tiles_ref, acc)

    if section < NSLAB - 1:
        write_down(acc, row, hot_ref, msg_ref)
    else:
        write_up(acc, msg_ref)


def down_step(lst, slab, row, pair, hots, tiles, acc, section):
    return pl.pallas_call(
        functools.partial(down_step_kernel, section=section),
        out_shape=(jax.ShapeDtypeStruct(ACC, F32), MESSAGE),
        in_specs=[smem(), smem(), smem()] + [vmem()] * 5,
        out_specs=(vmem(), vmem()),
        input_output_aliases={7: 0},
        compiler_params=PARAMS,
        name="down_step",
    )(lst, slab, row, *pair, hots, tiles, acc)


def up_step_kernel(lst, slab, own_ref, other_ref, tiles_ref, acc_in, msg_ref, acc, *, section):
    for r in range(NROW):
        for b in range(TGT):
            acc[r * BLK + b] = acc_in[r * BLK + b]

    @pl.when(slab[0] == section)
    def _():
        apply_list(lst, LA, (own_ref, other_ref), tiles_ref, acc)

    write_up(acc, msg_ref)


def up_step(lst, slab, pair, tiles, acc, section):
    return pl.pallas_call(
        functools.partial(up_step_kernel, section=section),
        out_shape=MESSAGE,
        in_specs=[smem(), smem()] + [vmem()] * 4,
        out_specs=vmem(),
        scratch_shapes=[pltpu.VMEM(ACC, F32)],
        compiler_params=PARAMS,
        name="up_step",
    )(lst, slab, *pair, tiles, acc)


def last_kernel(lst, slab, tiles_ref, *refs):
    gathered, acc, msg_ref = refs[:12], refs[13], refs[14]
    for k, s in enumerate((1, 2, 3, 2, 1, 0)):
        @pl.when(slab[0] == s)
        def _(k=k):
            pair = gathered[2 * k], gathered[2 * k + 1]
            apply_list(lst, TC if k < NSLAB - 1 else LALL, pair, tiles_ref, acc)

    for r in range(NROW):
        for b in range(BLK):
            msg_ref[r, b] = acc[r * BLK + b].astype(BF)


def last_apply(lst, slab, tiles, pairs, acc):
    flat = [ref for pair in pairs for ref in pair]
    return pl.pallas_call(
        last_kernel,
        out_shape=(
            jax.ShapeDtypeStruct(ACC, F32),
            jax.ShapeDtypeStruct((NROW, BLK, W, B), BF),
        ),
        in_specs=[smem(), smem()] + [vmem()] * 14,
        out_specs=(vmem(), vmem()),
        input_output_aliases={15: 0},
        compiler_params=PARAMS,
        name="last",
    )(lst, slab, tiles, *flat, acc)[1]


def split(x):
    high = x.astype(BF)
    rest = x - high.astype(F32)
    return jnp.concatenate([high, rest.astype(BF)], axis=0)


def row_total(rcv_ref, place, b):
    part = rcv_ref[place * NROW, b].astype(F32)
    for r in range(1, NROW):
        part = part + rcv_ref[place * NROW + r, b].astype(F32)
    return part


def down_kernel(rcv_ref, rhs_ref, coef_ref, out_ref):
    for b in range(TGT):
        pulled = row_total(rcv_ref, 0, b) * coef_ref[:, b * B : (b + 1) * B]
        value = (rhs_ref[b] - pulled).astype(BF)
        for z in range(HALF):
            out_ref[z, b] = value


def up_kernel(rcv_ref, coef_ref, hot_ref, out_ref):
    values = jnp.concatenate(
        [
            split(row_total(rcv_ref, 1, b) * coef_ref[:, b * B : (b + 1) * B])
            for b in range(TGT)
        ],
        axis=1,
    )
    total = jnp.dot(values, hot_ref[...], preferred_element_type=F32)
    lifted = -(total[:W] + total[W:])
    for b in range(PRT):
        value = lifted[:, b * B : (b + 1) * B].astype(BF)
        for z in range(HALF):
            out_ref[z, b] = value


def combine(kernel, received, others, blocks, name):
    return pl.pallas_call(
        kernel,
        out_shape=jax.ShapeDtypeStruct((HALF, blocks, W, B), BF),
        in_specs=[vmem()] * (1 + len(others)),
        out_specs=vmem(),
        compiler_params=PARAMS,
        name=name,
    )(received, *others)


def prepare_kernel(count, slab, rhs_ref, out_ref, target_ref):
    for b in range(BLK):
        value = rhs_ref[0, :, b * B : (b + 1) * B]
        if b < TGT:
            target_ref[b] = value
            value = jnp.where(slab[0] == 0, value, 0.0)
        value = jnp.where(b < count[0], value, 0.0).astype(BF)
        for z in range(HALF):
            out_ref[z, b] = value


def prepare(right_sides, section_blocks, slab):
    return pl.pallas_call(
        prepare_kernel,
        out_shape=(
            jax.ShapeDtypeStruct((HALF, BLK, W, B), BF),
            jax.ShapeDtypeStruct((TGT, W, B), F32),
        ),
        in_specs=[smem(), smem(), vmem()],
        out_specs=(vmem(), vmem()),
        compiler_params=PARAMS,
        name="prepare",
    )(section_blocks, slab, right_sides)


def finish_kernel(count, parts_ref, out_ref):
    for b in range(BLK):
        total = parts_ref[0, b].astype(F32)
        for r in range(1, NROW):
            total = total + parts_ref[r, b].astype(F32)
        out_ref[0, :, b * B : (b + 1) * B] = jnp.where(b < count[0], total, 0.0)


def finish(section_blocks, parts):
    return pl.pallas_call(
        finish_kernel,
        out_shape=jax.ShapeDtypeStruct((1, W, BLK * B), F32),
        in_specs=[smem(), vmem()],
        out_specs=vmem(),
        compiler_params=PARAMS,
        name="finish",
    )(section_blocks, parts)


Z_GROUPS = [[2 * z + k for z in range(HALF)] for k in range(2)]


def gather(copies):
    own = lax.all_to_all(copies, "col", 0, 0, tiled=True, axis_index_groups=Z_GROUPS)
    own = own.reshape(HALF * copies.shape[1], W, B)
    return own, lax.ppermute(own, "col", [(c, c ^ 1) for c in range(NCOL)])


def exchange(message, low):
    groups = [
        [(s + k) % NSLAB * NROW + r for k in range(2) for r in range(NROW)]
        for s in (low, low + 2)
    ]
    return lax.all_to_all(message, ("slab", "row"), 0, 0, tiled=True, axis_index_groups=groups)


def from_next(value, turn):
    pairs = [
        ((s + 1) * NROW + (r + turn) % NROW, s * NROW + r)
        for s in range(NSLAB - 1)
        for r in range(NROW)
    ]
    return lax.ppermute(value, ("slab", "row"), pairs)


def body(right_sides, front_tiles, tile_rows, tile_cols, section_blocks, plane_map, interface_coef):
    slab = lax.axis_index("slab").astype(jnp.int32)
    row = lax.axis_index("row").astype(jnp.int32)
    col = lax.axis_index("col").astype(jnp.int32)
    slab = slab.reshape(1)
    row = row.reshape(1)
    codes = tile_codes(tile_rows, tile_cols, col)
    map_own = plane_map.astype(F32)
    pack_next = from_next(jnp.concatenate([map_own, interface_coef], axis=0), 0)
    coef_next = pack_next[1:2]
    maps_next = jnp.concatenate(
        [pack_next[0:1]] + [from_next(map_own, d) for d in range(1, NROW)], axis=0
    ).astype(jnp.int32)

    copies, rhs_target = prepare(right_sides, section_blocks, slab)
    partner = jnp.arange(PRT * B, dtype=jnp.int32)
    hots = (partner[None, :, None] == maps_next[:, None, :]).astype(BF)
    hot_next = (maps_next[0][:, None] == partner[None, :]).astype(BF)

    pair = gather(copies)
    pair, hots, hot_next, coef_next, rhs_target, codes = lax.optimization_barrier(
        (pair, hots, hot_next, coef_next, rhs_target, codes)
    )
    acc, tiles, lst, msg = first_apply(codes, row, pair, hots, front_tiles[0])
    pairs = []
    for s in range(1, NSLAB):
        rcv = exchange(msg, s - 1)
        pairs.append(gather(combine(down_kernel, rcv, (rhs_target, interface_coef), TGT, "down")))
        acc, msg = down_step(lst, slab, row, pairs[-1], hots, tiles, acc, s)
    for s in range(NSLAB - 2, -1, -1):
        rcv = exchange(msg, s)
        pairs.append(gather(combine(up_kernel, rcv, (coef_next, hot_next), PRT, "up")))
        if s > 0:
            msg = up_step(lst, slab, pairs[-1], tiles, acc, s)
    msg = last_apply(lst, slab, tiles, pairs, acc)
    return finish(section_blocks, lax.all_to_all(msg, "row", 0, 0, tiled=True))


def solution(mesh):
    placed = (
        P("slab", None, ("col", "row")),
        P("slab", ("col", "row"), None, None),
        P("slab", ("col", "row")),
        P("slab", ("col", "row")),
        P("slab"),
        P("slab", ("col", "row")),
        P("slab", ("col", "row")),
    )
    return jax.shard_map(
        body, mesh=mesh, in_specs=placed, out_specs=P("slab", None, ("col", "row")), check_vma=False
    )
```

```python
import functools

import jax
import jax.numpy as jnp
from jax import lax
from jax.experimental import pallas as pl
from jax.experimental.pallas import tpu as pltpu
from jax.sharding import PartitionSpec as P

B = 128
BLK = 8
NROW = 4
NCOL = 16
NSLAB = 4
W = 32
NT = 128
UNROLL = 8
TGT = 2
PRT = 4
LST = NT + UNROLL
BF = jnp.bfloat16
F32 = jnp.float32


def smem():
    return pl.BlockSpec(memory_space=pltpu.SMEM)


def vmem():
    return pl.BlockSpec(memory_space=pltpu.VMEM)


PARAMS = pltpu.CompilerParams(vmem_limit_bytes=24 * 2**20)
ACC = (NROW * BLK + 1, W, B)
LISTS = 6
V0AB, V0C, TAB, TC, LA, LBC = range(LISTS)
CHUNK = 3
ORDER = (1, 2, 3, 2, 1)
HALF = NCOL // 2


def shr(x, n):
    return lax.shift_right_logical(x, jnp.int32(n))


def tile_codes(tile_rows, tile_cols, col_index):
    row = tile_rows - col_index * (NROW * BLK)
    part = tile_cols // (BLK * NROW)
    side = (part % 2 != col_index % 2).astype(jnp.int32)
    return row + 64 * (part // 2) + 512 * side + 1024 * (tile_cols % BLK)


def product(v, tile):
    return lax.dot_general(v, tile, (((1,), (1,)), ((), ())), preferred_element_type=F32)


def picked(side, own_ref, other_ref, at):
    return jnp.where(side == 0, own_ref[at], other_ref[at])


def lists_kernel(codes, lst):
    def step(t, counts):
        code = codes[0, t]
        row = code & 63
        half = shr(code, 6) & 7
        side = shr(code, 9) & 1
        blk = shr(code, 10)
        out = row & (BLK - 1)
        head = t + row * NT + side * 2**19
        early = out < PRT
        target = blk < TGT
        low = blk < PRT
        member = (
            (BLK, early),
            (BLK, out >= PRT),
            (TGT, target & early),
            (TGT, target & (out >= PRT)),
            (PRT, low & (out < TGT)),
            (PRT, low & (out >= TGT)),
        )
        entry = {n: head + (half * n + blk) * 8192 for n in (BLK, TGT, PRT)}
        for k in range(LISTS):
            lst[k, counts[k]] = entry[member[k][0]]
        return tuple(
            counts[k] + jnp.where(member[k][1], jnp.int32(1), jnp.int32(0)) for k in range(LISTS)
        )

    counts = lax.fori_loop(0, NT, step, (jnp.int32(0),) * LISTS)
    for k in range(LISTS):
        for u in range(UNROLL):
            lst[k, counts[k] + u] = NROW * BLK * NT
        lst[LISTS, k] = shr(counts[k] + UNROLL - 1, 3)


def make_lists(codes):
    return pl.pallas_call(
        lists_kernel,
        out_shape=jax.ShapeDtypeStruct((LISTS + 1, LST), jnp.int32),
        in_specs=[smem()],
        out_specs=smem(),
        name="lists",
    )(codes)


def apply_group(lst, which, g, pair, tiles_ref, acc):
    rows, done = [], []
    for u in range(UNROLL):
        e = lst[which, g * UNROLL + u]
        v = picked(shr(e, 19), *pair, shr(e, 13) & 63)
        rows.append(shr(e, 7) & 63)
        done.append(product(v, tiles_ref[e & 127]))
    for r, d in zip(rows, done):
        acc[r] += d


def apply_list(lst, which, pair, tiles_ref, acc, low=0, most=NT):
    def group(g, _):
        apply_group(lst, which, g, pair, tiles_ref, acc)
        return 0

    groups = lst[LISTS, which]
    lax.fori_loop(low, jnp.minimum(groups, low + most), group, 0)


def late_start(slab, step):
    used = jnp.int32(step)
    for active in ORDER[:step]:
        used = used - jnp.where(slab[0] == active, jnp.int32(1), jnp.int32(0))
    return used * CHUNK


def step_work(lst, slab, which, pair, first_pair, tiles_ref, acc, step):
    @pl.when(slab[0] == ORDER[step])
    def _():
        apply_list(lst, which, pair, tiles_ref, acc)

    @pl.when(slab[0] != ORDER[step])
    def _():
        apply_list(lst, V0C, first_pair, tiles_ref, acc, late_start(slab, step), CHUNK)


def write_down(acc, row, hot_ref, msg_ref):
    for d in range(NROW):
        r = (row[0] + d) & (NROW - 1)
        values = jnp.concatenate([acc[r * BLK + b].astype(BF) for b in range(PRT)], axis=1)
        part = jnp.dot(values, hot_ref[d], preferred_element_type=F32).astype(BF)
        for b in range(TGT):
            for s in range(2):
                msg_ref[s * NROW + r, b] = part[:, b * B : (b + 1) * B]


def write_up(acc, msg_ref):
    for r in range(NROW):
        for b in range(TGT):
            part = acc[r * BLK + b].astype(BF)
            for s in range(2):
                msg_ref[s * NROW + r, b] = part


MESSAGE = jax.ShapeDtypeStruct((2 * NROW, TGT, W, B), BF)


def first_kernel(lst, row, own_ref, other_ref, hot_ref, tiles_hbm, acc, tiles_ref, msg_ref, sems):
    def load(g):
        at = pl.ds(pl.multiple_of(g * UNROLL, UNROLL), UNROLL)
        return pltpu.make_async_copy(tiles_hbm.at[at], tiles_ref.at[at], sems.at[g])

    def start(g, _):
        load(g).start()
        return 0

    def wait(g, _):
        load(g).wait()
        return 0

    lax.fori_loop(0, NT // UNROLL, start, 0)
    acc[...] = jnp.zeros(ACC, F32)

    def group(g, loaded):
        need = loaded
        for u in range(UNROLL):
            need = jnp.maximum(need, shr(lst[V0AB, g * UNROLL + u] & 127, 3) + 1)
        lax.fori_loop(loaded, need, wait, 0)
        apply_group(lst, V0AB, g, (own_ref, other_ref), tiles_ref, acc)
        return need

    loaded = lax.fori_loop(0, lst[LISTS, V0AB], group, jnp.int32(0))
    write_down(acc, row, hot_ref, msg_ref)
    lax.fori_loop(loaded, NT // UNROLL, wait, 0)


def first_apply(lst, row, pair, hots, tiles):
    return pl.pallas_call(
        first_kernel,
        out_shape=(
            jax.ShapeDtypeStruct(ACC, F32),
            jax.ShapeDtypeStruct(tiles.shape, BF),
            MESSAGE,
        ),
        in_specs=[smem(), smem(), vmem(), vmem(), vmem(), pl.BlockSpec(memory_space=pltpu.HBM)],
        out_specs=(vmem(), vmem(), vmem()),
        scratch_shapes=[pltpu.SemaphoreType.DMA((NT // UNROLL,))],
        compiler_params=PARAMS,
        name="first",
    )(lst, row, *pair, hots, pltpu.with_memory_space_constraint(tiles, pltpu.HBM))


def down_step_kernel(
    lst, slab, row, own_ref, other_ref, own0, other0, hot_ref, tiles_ref, acc_in, acc, msg_ref, *, step
):
    step_work(lst, slab, TAB, (own_ref, other_ref), (own0, other0), tiles_ref, acc, step)
    if ORDER[step] < NSLAB - 1:
        write_down(acc, row, hot_ref, msg_ref)
    else:
        write_up(acc, msg_ref)


def down_step(lst, slab, row, pair, first_pair, hots, tiles, acc, step):
    return pl.pallas_call(
        functools.partial(down_step_kernel, step=step),
        out_shape=(jax.ShapeDtypeStruct(ACC, F32), MESSAGE),
        in_specs=[smem(), smem(), smem()] + [vmem()] * 7,
        out_specs=(vmem(), vmem()),
        input_output_aliases={9: 0},
        compiler_params=PARAMS,
        name="down_step",
    )(lst, slab, row, *pair, *first_pair, hots, tiles, acc)


def up_step_kernel(
    lst, slab, own_ref, other_ref, own0, other0, tiles_ref, acc_in, acc, msg_ref, *, step
):
    step_work(lst, slab, LA, (own_ref, other_ref), (own0, other0), tiles_ref, acc, step)
    write_up(acc, msg_ref)


def up_step(lst, slab, pair, first_pair, tiles, acc, step):
    return pl.pallas_call(
        functools.partial(up_step_kernel, step=step),
        out_shape=(jax.ShapeDtypeStruct(ACC, F32), MESSAGE),
        in_specs=[smem(), smem()] + [vmem()] * 6,
        out_specs=(vmem(), vmem()),
        input_output_aliases={7: 0},
        compiler_params=PARAMS,
        name="up_step",
    )(lst, slab, *pair, *first_pair, tiles, acc)


def last_kernel(lst, slab, tiles_ref, own0, other0, *refs):
    gathered, acc, msg_ref = refs[:12], refs[13], refs[14]
    for k, s in enumerate((1, 2, 3, 2, 1, 0)):
        pair = gathered[2 * k], gathered[2 * k + 1]

        @pl.when(slab[0] == s)
        def _(k=k, s=s, pair=pair):
            if s == 0:
                apply_list(lst, LA, pair, tiles_ref, acc)
            apply_list(lst, TC if k < NSLAB - 1 else LBC, pair, tiles_ref, acc)

    apply_list(lst, V0C, (own0, other0), tiles_ref, acc, late_start(slab, len(ORDER)))
    for r in range(NROW):
        for b in range(BLK):
            msg_ref[r, b] = acc[r * BLK + b].astype(BF)


def last_apply(lst, slab, tiles, first_pair, pairs, acc):
    flat = [ref for pair in pairs for ref in pair]
    return pl.pallas_call(
        last_kernel,
        out_shape=(
            jax.ShapeDtypeStruct(ACC, F32),
            jax.ShapeDtypeStruct((NROW, BLK, W, B), BF),
        ),
        in_specs=[smem(), smem()] + [vmem()] * 16,
        out_specs=(vmem(), vmem()),
        input_output_aliases={17: 0},
        compiler_params=PARAMS,
        name="last",
    )(lst, slab, tiles, *first_pair, *flat, acc)[1]


def split(x):
    high = x.astype(BF)
    rest = x - high.astype(F32)
    return jnp.concatenate([high, rest.astype(BF)], axis=0)


def row_total(rcv_ref, place, b):
    part = rcv_ref[place * NROW, b].astype(F32)
    for r in range(1, NROW):
        part = part + rcv_ref[place * NROW + r, b].astype(F32)
    return part


def down_kernel(rcv_ref, rhs_ref, coef_ref, out_ref):
    for b in range(TGT):
        pulled = row_total(rcv_ref, 0, b) * coef_ref[:, b * B : (b + 1) * B]
        value = (rhs_ref[b] - pulled).astype(BF)
        for z in range(HALF):
            out_ref[z, b] = value


def up_kernel(rcv_ref, coef_ref, hot_ref, out_ref):
    values = jnp.concatenate(
        [
            split(row_total(rcv_ref, 1, b) * coef_ref[:, b * B : (b + 1) * B])
            for b in range(TGT)
        ],
        axis=1,
    )
    total = jnp.dot(values, hot_ref[...], preferred_element_type=F32)
    lifted = -(total[:W] + total[W:])
    for b in range(PRT):
        value = lifted[:, b * B : (b + 1) * B].astype(BF)
        for z in range(HALF):
            out_ref[z, b] = value


def combine(kernel, received, others, blocks, name):
    return pl.pallas_call(
        kernel,
        out_shape=jax.ShapeDtypeStruct((HALF, blocks, W, B), BF),
        in_specs=[vmem()] * (1 + len(others)),
        out_specs=vmem(),
        compiler_params=PARAMS,
        name=name,
    )(received, *others)


def prepare_kernel(count, slab, rhs_ref, out_ref, target_ref):
    for b in range(BLK):
        value = rhs_ref[0, :, b * B : (b + 1) * B]
        if b < TGT:
            target_ref[b] = value
            value = jnp.where(slab[0] == 0, value, 0.0)
        value = jnp.where(b < count[0], value, 0.0).astype(BF)
        for z in range(HALF):
            out_ref[z, b] = value


def prepare(right_sides, section_blocks, slab):
    return pl.pallas_call(
        prepare_kernel,
        out_shape=(
            jax.ShapeDtypeStruct((HALF, BLK, W, B), BF),
            jax.ShapeDtypeStruct((TGT, W, B), F32),
        ),
        in_specs=[smem(), smem(), vmem()],
        out_specs=(vmem(), vmem()),
        compiler_params=PARAMS,
        name="prepare",
    )(section_blocks, slab, right_sides)


def finish_kernel(count, parts_ref, out_ref):
    for b in range(BLK):
        total = parts_ref[0, b].astype(F32)
        for r in range(1, NROW):
            total = total + parts_ref[r, b].astype(F32)
        out_ref[0, :, b * B : (b + 1) * B] = jnp.where(b < count[0], total, 0.0)


def finish(section_blocks, parts):
    return pl.pallas_call(
        finish_kernel,
        out_shape=jax.ShapeDtypeStruct((1, W, BLK * B), F32),
        in_specs=[smem(), vmem()],
        out_specs=vmem(),
        compiler_params=PARAMS,
        name="finish",
    )(section_blocks, parts)


Z_GROUPS = [[2 * z + k for z in range(HALF)] for k in range(2)]


def gather(copies):
    own = lax.all_to_all(copies, "col", 0, 0, tiled=True, axis_index_groups=Z_GROUPS)
    own = own.reshape(HALF * copies.shape[1], W, B)
    return own, lax.ppermute(own, "col", [(c, c ^ 1) for c in range(NCOL)])


def exchange(message, low):
    groups = [
        [(s + k) % NSLAB * NROW + r for k in range(2) for r in range(NROW)]
        for s in (low, low + 2)
    ]
    return lax.all_to_all(message, ("slab", "row"), 0, 0, tiled=True, axis_index_groups=groups)


def from_next(value, turn):
    pairs = [
        ((s + 1) * NROW + (r + turn) % NROW, s * NROW + r)
        for s in range(NSLAB - 1)
        for r in range(NROW)
    ]
    return lax.ppermute(value, ("slab", "row"), pairs)


def body(right_sides, front_tiles, tile_rows, tile_cols, section_blocks, plane_map, interface_coef):
    slab = lax.axis_index("slab").astype(jnp.int32)
    row = lax.axis_index("row").astype(jnp.int32)
    col = lax.axis_index("col").astype(jnp.int32)
    slab = slab.reshape(1)
    row = row.reshape(1)
    codes = tile_codes(tile_rows, tile_cols, col)
    map_own = plane_map.astype(F32)
    pack_next = from_next(jnp.concatenate([map_own, interface_coef], axis=0), 0)
    coef_next = pack_next[1:2]
    maps_next = jnp.concatenate(
        [pack_next[0:1]] + [from_next(map_own, d) for d in range(1, NROW)], axis=0
    ).astype(jnp.int32)

    copies, rhs_target = prepare(right_sides, section_blocks, slab)
    partner = jnp.arange(PRT * B, dtype=jnp.int32)
    hots = (partner[None, :, None] == maps_next[:, None, :]).astype(BF)
    hot_next = (maps_next[0][:, None] == partner[None, :]).astype(BF)

    start = gather(copies)
    start, hots, hot_next, coef_next, rhs_target, lst = lax.optimization_barrier(
        (start, hots, hot_next, coef_next, rhs_target, make_lists(codes))
    )
    acc, tiles, msg = first_apply(lst, row, start, hots, front_tiles[0])
    pairs = []
    for step, active in enumerate(ORDER[: NSLAB - 1]):
        rcv = exchange(msg, active - 1)
        pairs.append(gather(combine(down_kernel, rcv, (rhs_target, interface_coef), TGT, "down")))
        acc, msg = down_step(lst, slab, row, pairs[-1], start, hots, tiles, acc, step)
    for s in range(NSLAB - 2, -1, -1):
        rcv = exchange(msg, s)
        pairs.append(gather(combine(up_kernel, rcv, (coef_next, hot_next), PRT, "up")))
        if s > 0:
            acc, msg = up_step(lst, slab, pairs[-1], start, tiles, acc, 2 * NSLAB - 3 - s)
    msg = last_apply(lst, slab, tiles, start, pairs, acc)
    return finish(section_blocks, lax.all_to_all(msg, "row", 0, 0, tiled=True))


def solution(mesh):
    placed = (
        P("slab", None, ("col", "row")),
        P("slab", ("col", "row"), None, None),
        P("slab", ("col", "row")),
        P("slab", ("col", "row")),
        P("slab"),
        P("slab", ("col", "row")),
        P("slab", ("col", "row")),
    )
    return jax.shard_map(
        body, mesh=mesh, in_specs=placed, out_specs=P("slab", None, ("col", "row")), check_vma=False
    )
```

```python
import functools

import jax
import jax.numpy as jnp
from jax import lax
from jax.experimental import pallas as pl
from jax.experimental.pallas import tpu as pltpu
from jax.sharding import PartitionSpec as P

B = 128
BLK = 8
NROW = 4
NCOL = 16
NSLAB = 4
W = 32
NT = 128
UNROLL = 8
TGT = 2
PRT = 4
LST = NT + UNROLL
BF = jnp.bfloat16
F32 = jnp.float32


def smem():
    return pl.BlockSpec(memory_space=pltpu.SMEM)


def vmem():
    return pl.BlockSpec(memory_space=pltpu.VMEM)


PARAMS = pltpu.CompilerParams(vmem_limit_bytes=24 * 2**20)
ACC = (NROW * BLK + 1, W, B)
LISTS = 6
V0AB, V0C, TAB, TC, LA, LBC = range(LISTS)
CHUNK = 3
ORDER = (1, 2, 3, 2, 1)
HALF = NCOL // 2


def shr(x, n):
    return lax.shift_right_logical(x, jnp.int32(n))


def product(v, tile):
    return lax.dot_general(v, tile, (((1,), (1,)), ((), ())), preferred_element_type=F32)


def picked(side, own_ref, other_ref, at):
    return jnp.where(side == 0, own_ref[at], other_ref[at])


def lists_kernel(rows, cols, col_index, lst):
    base = col_index[0] * (NROW * BLK)
    core = col_index[0] & 1

    def step(t, ends):
        row = rows[0, t] - base
        col = cols[0, t]
        part = shr(col, 5)
        half = shr(part, 1)
        blk = col & (BLK - 1)
        out = row & (BLK - 1)
        head = t + row * NT + ((part & 1) ^ core) * 2**19
        early = out < PRT
        target = blk < TGT
        low = blk < PRT
        member = (
            (BLK, early),
            (BLK, out >= PRT),
            (TGT, target & early),
            (TGT, target & (out >= PRT)),
            (PRT, low & (out < TGT)),
            (PRT, low & (out >= TGT)),
        )
        entry = {n: head + (half * n + blk) * 8192 for n in (BLK, TGT, PRT)}
        for k in range(LISTS):
            lst[ends[k]] = entry[member[k][0]]
        return tuple(
            ends[k] + jnp.where(member[k][1], jnp.int32(1), jnp.int32(0)) for k in range(LISTS)
        )

    ends = lax.fori_loop(0, NT, step, tuple(jnp.int32(k * LST) for k in range(LISTS)))
    for k in range(LISTS):
        for u in range(UNROLL):
            lst[ends[k] + u] = NROW * BLK * NT
        lst[LISTS * LST + k] = shr(ends[k] - k * LST + UNROLL - 1, 3)


def make_lists(tile_rows, tile_cols, col_index):
    return pl.pallas_call(
        lists_kernel,
        out_shape=jax.ShapeDtypeStruct((LISTS * LST + UNROLL,), jnp.int32),
        in_specs=[smem(), smem(), smem()],
        out_specs=smem(),
        name="lists",
    )(tile_rows, tile_cols, col_index)


def apply_group(lst, which, g, pair, tiles_ref, acc):
    rows, done = [], []
    for u in range(UNROLL):
        e = lst[which * LST + g * UNROLL + u]
        v = picked(shr(e, 19), *pair, shr(e, 13) & 63)
        rows.append(shr(e, 7) & 63)
        done.append(product(v, tiles_ref[e & 127]))
    for r, d in zip(rows, done):
        acc[r] += d


def apply_list(lst, which, pair, tiles_ref, acc, low=0, most=NT):
    def group(g, _):
        apply_group(lst, which, g, pair, tiles_ref, acc)
        return 0

    groups = lst[LISTS * LST + which]
    lax.fori_loop(low, jnp.minimum(groups, low + most), group, 0)


def late_start(slab, step):
    used = jnp.int32(step)
    for active in ORDER[:step]:
        used = used - jnp.where(slab[0] == active, jnp.int32(1), jnp.int32(0))
    return used * CHUNK


def step_work(lst, slab, which, pair, first_pair, tiles_ref, acc, step):
    @pl.when(slab[0] == ORDER[step])
    def _():
        apply_list(lst, which, pair, tiles_ref, acc)

    @pl.when(slab[0] != ORDER[step])
    def _():
        apply_list(lst, V0C, first_pair, tiles_ref, acc, late_start(slab, step), CHUNK)


def write_message(acc, msg_ref):
    for r in range(NROW):
        for b in range(msg_ref.shape[1]):
            part = acc[r * BLK + b].astype(BF)
            for s in range(2):
                msg_ref[s * NROW + r, b] = part


def message(blocks):
    return jax.ShapeDtypeStruct((2 * NROW, blocks, W, B), BF)


def first_kernel(lst, own_ref, other_ref, tiles_hbm, acc, tiles_ref, msg_ref, sems):
    def load(g):
        at = pl.ds(pl.multiple_of(g * UNROLL, UNROLL), UNROLL)
        return pltpu.make_async_copy(tiles_hbm.at[at], tiles_ref.at[at], sems.at[g])

    def start(g, _):
        load(g).start()
        return 0

    def wait(g, _):
        load(g).wait()
        return 0

    lax.fori_loop(0, NT // UNROLL, start, 0)
    acc[...] = jnp.zeros(ACC, F32)

    def group(g, loaded):
        need = loaded
        for u in range(UNROLL):
            need = jnp.maximum(need, shr(lst[V0AB * LST + g * UNROLL + u] & 127, 3) + 1)
        lax.fori_loop(loaded, need, wait, 0)
        apply_group(lst, V0AB, g, (own_ref, other_ref), tiles_ref, acc)
        return need

    loaded = lax.fori_loop(0, lst[LISTS * LST + V0AB], group, jnp.int32(0))
    write_message(acc, msg_ref)
    lax.fori_loop(loaded, NT // UNROLL, wait, 0)


def first_apply(lst, pair, tiles):
    return pl.pallas_call(
        first_kernel,
        out_shape=(
            jax.ShapeDtypeStruct(ACC, F32),
            jax.ShapeDtypeStruct(tiles.shape, BF),
            message(PRT),
        ),
        in_specs=[smem(), vmem(), vmem(), pl.BlockSpec(memory_space=pltpu.HBM)],
        out_specs=(vmem(), vmem(), vmem()),
        scratch_shapes=[pltpu.SemaphoreType.DMA((NT // UNROLL,))],
        compiler_params=PARAMS,
        name="first",
    )(lst, *pair, pltpu.with_memory_space_constraint(tiles, pltpu.HBM))


def step_kernel(
    lst, slab, own_ref, other_ref, own0, other0, tiles_ref, acc_in, acc, msg_ref, *, which, step
):
    step_work(lst, slab, which, (own_ref, other_ref), (own0, other0), tiles_ref, acc, step)
    write_message(acc, msg_ref)


def step_apply(lst, slab, which, pair, first_pair, tiles, acc, step):
    blocks = PRT if ORDER[step + 1 :] and ORDER[step] < ORDER[step + 1] else TGT
    return pl.pallas_call(
        functools.partial(step_kernel, which=which, step=step),
        out_shape=(jax.ShapeDtypeStruct(ACC, F32), message(blocks)),
        in_specs=[smem(), smem()] + [vmem()] * 6,
        out_specs=(vmem(), vmem()),
        input_output_aliases={7: 0},
        compiler_params=PARAMS,
        name="step",
    )(lst, slab, *pair, *first_pair, tiles, acc)


def last_kernel(lst, slab, tiles_ref, own0, other0, *refs):
    gathered, acc, msg_ref = refs[:12], refs[13], refs[14]
    for k, s in enumerate((1, 2, 3, 2, 1, 0)):
        pair = gathered[2 * k], gathered[2 * k + 1]

        @pl.when(slab[0] == s)
        def _(k=k, s=s, pair=pair):
            if s == 0:
                apply_list(lst, LA, pair, tiles_ref, acc)
            apply_list(lst, TC if k < NSLAB - 1 else LBC, pair, tiles_ref, acc)

    apply_list(lst, V0C, (own0, other0), tiles_ref, acc, late_start(slab, len(ORDER)))
    for r in range(NROW):
        for b in range(BLK):
            msg_ref[r, b] = acc[r * BLK + b].astype(BF)


def last_apply(lst, slab, tiles, first_pair, pairs, acc):
    flat = [ref for pair in pairs for ref in pair]
    return pl.pallas_call(
        last_kernel,
        out_shape=(
            jax.ShapeDtypeStruct(ACC, F32),
            jax.ShapeDtypeStruct((NROW, BLK, W, B), BF),
        ),
        in_specs=[smem(), smem()] + [vmem()] * 16,
        out_specs=(vmem(), vmem()),
        input_output_aliases={17: 0},
        compiler_params=PARAMS,
        name="last",
    )(lst, slab, tiles, *first_pair, *flat, acc)[1]


def split(x):
    high = x.astype(BF)
    rest = x - high.astype(F32)
    return jnp.concatenate([high, rest.astype(BF)], axis=0)


def row_total(rcv_ref, place, b):
    part = rcv_ref[place * NROW, b].astype(F32)
    for r in range(1, NROW):
        part = part + rcv_ref[place * NROW + r, b].astype(F32)
    return part


def down_kernel(rcv_ref, rhs_ref, coef_ref, hot_ref, out_ref):
    values = jnp.concatenate([split(row_total(rcv_ref, 0, b)) for b in range(PRT)], axis=1)
    total = jnp.dot(values, hot_ref[...], preferred_element_type=F32)
    chosen = (total[:W] + total[W:]) * coef_ref[...]
    for b in range(TGT):
        value = (rhs_ref[b] - chosen[:, b * B : (b + 1) * B]).astype(BF)
        for z in range(HALF):
            out_ref[z, b] = value


def up_kernel(rcv_ref, coef_ref, hot_ref, out_ref):
    values = jnp.concatenate(
        [
            split(row_total(rcv_ref, 1, b) * coef_ref[:, b * B : (b + 1) * B])
            for b in range(TGT)
        ],
        axis=1,
    )
    total = jnp.dot(values, hot_ref[...], preferred_element_type=F32)
    lifted = -(total[:W] + total[W:])
    for b in range(PRT):
        value = lifted[:, b * B : (b + 1) * B].astype(BF)
        for z in range(HALF):
            out_ref[z, b] = value


def combine(kernel, received, others, blocks, name):
    return pl.pallas_call(
        kernel,
        out_shape=jax.ShapeDtypeStruct((HALF, blocks, W, B), BF),
        in_specs=[vmem()] * (1 + len(others)),
        out_specs=vmem(),
        compiler_params=PARAMS,
        name=name,
    )(received, *others)


def prepare_kernel(count, slab, rhs_ref, out_ref, target_ref):
    for b in range(BLK):
        value = rhs_ref[0, :, b * B : (b + 1) * B]
        if b < TGT:
            target_ref[b] = value
            value = jnp.where(slab[0] == 0, value, 0.0)
        value = jnp.where(b < count[0], value, 0.0).astype(BF)
        for z in range(HALF):
            out_ref[z, b] = value


def prepare(right_sides, section_blocks, slab):
    return pl.pallas_call(
        prepare_kernel,
        out_shape=(
            jax.ShapeDtypeStruct((HALF, BLK, W, B), BF),
            jax.ShapeDtypeStruct((TGT, W, B), F32),
        ),
        in_specs=[smem(), smem(), vmem()],
        out_specs=(vmem(), vmem()),
        compiler_params=PARAMS,
        name="prepare",
    )(section_blocks, slab, right_sides)


def finish_kernel(count, parts_ref, out_ref):
    for b in range(BLK):
        total = parts_ref[0, b].astype(F32)
        for r in range(1, NROW):
            total = total + parts_ref[r, b].astype(F32)
        out_ref[0, :, b * B : (b + 1) * B] = jnp.where(b < count[0], total, 0.0)


def finish(section_blocks, parts):
    return pl.pallas_call(
        finish_kernel,
        out_shape=jax.ShapeDtypeStruct((1, W, BLK * B), F32),
        in_specs=[smem(), vmem()],
        out_specs=vmem(),
        compiler_params=PARAMS,
        name="finish",
    )(section_blocks, parts)


Z_GROUPS = [[2 * z + k for z in range(HALF)] for k in range(2)]


def gather(copies):
    own = lax.all_to_all(copies, "col", 0, 0, tiled=True, axis_index_groups=Z_GROUPS)
    own = own.reshape(HALF * copies.shape[1], W, B)
    return own, lax.ppermute(own, "col", [(c, c ^ 1) for c in range(NCOL)])


def exchange(message, low):
    groups = [
        [(s + k) % NSLAB * NROW + r for k in range(2) for r in range(NROW)]
        for s in (low, low + 2)
    ]
    return lax.all_to_all(message, ("slab", "row"), 0, 0, tiled=True, axis_index_groups=groups)


def body(right_sides, front_tiles, tile_rows, tile_cols, section_blocks, plane_map, interface_coef):
    slab = lax.axis_index("slab").astype(jnp.int32).reshape(1)
    col = lax.axis_index("col").astype(jnp.int32).reshape(1)
    pack = jnp.concatenate([plane_map.astype(F32), interface_coef], axis=0)
    pack_next = lax.ppermute(pack, "slab", [(s + 1, s) for s in range(NSLAB - 1)])
    map_next = pack_next[0].astype(jnp.int32)
    coef_next = pack_next[1:2]
    partner = jnp.arange(PRT * B, dtype=jnp.int32)
    hot_own = (partner[:, None] == plane_map[0][None, :]).astype(BF)
    hot_next = (map_next[:, None] == partner[None, :]).astype(BF)

    copies, rhs_target = prepare(right_sides, section_blocks, slab)
    start = gather(copies)
    lst = make_lists(tile_rows, tile_cols, col)
    start, hot_own, hot_next, coef_next, rhs_target, lst = lax.optimization_barrier(
        (start, hot_own, hot_next, coef_next, rhs_target, lst)
    )
    acc, tiles, msg = first_apply(lst, start, front_tiles[0])
    pairs = []
    for step in range(NSLAB - 1):
        rcv = exchange(msg, step)
        value = combine(down_kernel, rcv, (rhs_target, interface_coef, hot_own), TGT, "down")
        pairs.append(gather(value))
        acc, msg = step_apply(lst, slab, TAB, pairs[-1], start, tiles, acc, step)
    for step in range(NSLAB - 1, 2 * NSLAB - 2):
        rcv = exchange(msg, 2 * NSLAB - 3 - step)
        pairs.append(gather(combine(up_kernel, rcv, (coef_next, hot_next), PRT, "up")))
        if step < len(ORDER):
            acc, msg = step_apply(lst, slab, LA, pairs[-1], start, tiles, acc, step)
    msg = last_apply(lst, slab, tiles, start, pairs, acc)
    return finish(section_blocks, lax.all_to_all(msg, "row", 0, 0, tiled=True))


def solution(mesh):
    placed = (
        P("slab", None, ("col", "row")),
        P("slab", ("col", "row"), None, None),
        P("slab", ("col", "row")),
        P("slab", ("col", "row")),
        P("slab"),
        P("slab", ("col", "row")),
        P("slab", ("col", "row")),
    )
    return jax.shard_map(
        body, mesh=mesh, in_specs=placed, out_specs=P("slab", None, ("col", "row")), check_vma=False
    )
```

```python
import functools

import jax
import jax.numpy as jnp
from jax import lax
from jax.experimental import pallas as pl
from jax.experimental.pallas import tpu as pltpu
from jax.sharding import PartitionSpec as P

B = 128
BLK = 8
NROW = 4
NCOL = 16
NSLAB = 4
W = 32
NT = 128
UNROLL = 8
TGT = 2
PRT = 4
BF = jnp.bfloat16
F32 = jnp.float32


def smem():
    return pl.BlockSpec(memory_space=pltpu.SMEM)


def vmem():
    return pl.BlockSpec(memory_space=pltpu.VMEM)


PARAMS = pltpu.CompilerParams(vmem_limit_bytes=24 * 2**20)
ACC = (NROW * BLK + 1, W, B)
LISTS = 6
V0AB, V0C, TAB, TC, LA, LBC = range(LISTS)
CHUNK = 3
ORDER = (1, 2, 3, 2, 1)
HALF = NCOL // 2


def shr(x, n):
    return lax.shift_right_logical(x, jnp.int32(n))


def product(v, tile):
    return lax.dot_general(v, tile, (((1,), (1,)), ((), ())), preferred_element_type=F32)


def picked(side, own_ref, other_ref, at):
    return jnp.where(side == 0, own_ref[at], other_ref[at])


def lists_kernel(col_index, rows_ref, cols_ref, out_ref):
    lane = lax.broadcasted_iota(jnp.int32, (1, NT), 1)
    down = lax.broadcasted_iota(jnp.int32, (NT, NT), 0)
    across = lax.broadcasted_iota(jnp.int32, (NT, NT), 1)
    before = jnp.where(down < across, 1.0, 0.0).astype(BF)
    row = rows_ref[...] - col_index[0] * (NROW * BLK)
    col = cols_ref[...]
    part = shr(col, 5)
    half = shr(part, 1)
    side = (part & 1) ^ (col_index[0] & 1)
    blk = col & (BLK - 1)
    out = row & (BLK - 1)
    early = out < PRT
    target = blk < TGT
    low = blk < PRT
    member = (
        (BLK, early),
        (BLK, out >= PRT),
        (TGT, target & early),
        (TGT, target & (out >= PRT)),
        (PRT, low & (out < TGT)),
        (PRT, low & (out >= TGT)),
    )
    sizes = jnp.zeros((1, NT), jnp.int32)
    for k, (width, belongs) in enumerate(member):
        one = jnp.where(belongs, 1.0, 0.0)
        count = jnp.sum(one, axis=1, keepdims=True).astype(jnp.int32)
        rank = jnp.dot(
            jnp.broadcast_to(one, (8, NT)).astype(BF), before, preferred_element_type=F32
        )[0:1].astype(jnp.int32)
        rank = jnp.where(belongs, rank, -1)
        place = jnp.where(jnp.broadcast_to(rank, (NT, NT)) == down, 1.0, 0.0).astype(BF)
        upper = half * width + blk + side * 64
        digits = jnp.concatenate(
            [x.astype(F32) for x in (lane, row, upper, upper, upper, upper, upper, upper)], axis=0
        ).astype(BF)
        moved = lax.dot_general(
            digits, place, (((1,), (1,)), ((), ())), preferred_element_type=F32
        ).astype(jnp.int32)
        entry = moved[0:1] + moved[1:2] * NT + moved[2:3] * 8192
        out_ref[k : k + 1, :] = jnp.where(lane < count, entry, NROW * BLK * NT)
        sizes = jnp.where(lane == k, shr(count + UNROLL - 1, 3), sizes)
    out_ref[LISTS : LISTS + 1, :] = sizes
    out_ref[LISTS + 1 : LISTS + 2, :] = sizes


def make_lists(tile_rows, tile_cols, col_index):
    return pl.pallas_call(
        lists_kernel,
        out_shape=jax.ShapeDtypeStruct((LISTS + 2, NT), jnp.int32),
        in_specs=[smem(), vmem(), vmem()],
        out_specs=vmem(),
        compiler_params=PARAMS,
        name="lists",
    )(col_index, tile_rows, tile_cols)


def load_kernel(tiles_hbm, own_ref, tiles_ref, sem):
    copy = pltpu.make_async_copy(tiles_hbm, tiles_ref, sem)
    copy.start()
    copy.wait()


def load_tiles(tiles, own):
    return pl.pallas_call(
        load_kernel,
        out_shape=jax.ShapeDtypeStruct(tiles.shape, BF),
        in_specs=[pl.BlockSpec(memory_space=pltpu.HBM), vmem()],
        out_specs=vmem(),
        scratch_shapes=[pltpu.SemaphoreType.DMA],
        compiler_params=PARAMS,
        name="load",
    )(pltpu.with_memory_space_constraint(tiles, pltpu.HBM), own)


def apply_group(lst, which, g, pair, tiles_ref, acc):
    rows, done = [], []
    for u in range(UNROLL):
        e = lst[which, g * UNROLL + u]
        v = picked(shr(e, 19), *pair, shr(e, 13) & 63)
        rows.append(shr(e, 7) & 63)
        done.append(product(v, tiles_ref[e & 127]))
    for r, d in zip(rows, done):
        acc[r] += d


def apply_list(lst, which, pair, tiles_ref, acc, low=0, most=NT):
    def group(g, _):
        apply_group(lst, which, g, pair, tiles_ref, acc)
        return 0

    groups = lst[LISTS, which]
    lax.fori_loop(low, jnp.minimum(groups, low + most), group, 0)


def late_start(slab, step):
    used = jnp.int32(step)
    for active in ORDER[:step]:
        used = used - jnp.where(slab[0] == active, jnp.int32(1), jnp.int32(0))
    return used * CHUNK


def step_work(lst, slab, which, pair, first_pair, tiles_ref, acc, step):
    @pl.when(slab[0] == ORDER[step])
    def _():
        apply_list(lst, which, pair, tiles_ref, acc)

    @pl.when(slab[0] != ORDER[step])
    def _():
        apply_list(lst, V0C, first_pair, tiles_ref, acc, late_start(slab, step), CHUNK)


def write_down(acc, row, hot_ref, msg_ref):
    for d in range(NROW):
        r = (row[0] + d) & (NROW - 1)
        values = jnp.concatenate([acc[r * BLK + b].astype(BF) for b in range(PRT)], axis=1)
        part = jnp.dot(values, hot_ref[d], preferred_element_type=F32).astype(BF)
        for b in range(TGT):
            for s in range(2):
                msg_ref[s * NROW + r, b] = part[:, b * B : (b + 1) * B]


def write_up(acc, msg_ref):
    for r in range(NROW):
        for b in range(TGT):
            part = acc[r * BLK + b].astype(BF)
            for s in range(2):
                msg_ref[s * NROW + r, b] = part


MESSAGE = jax.ShapeDtypeStruct((2 * NROW, TGT, W, B), BF)


def first_kernel(lst, row, own_ref, other_ref, hot_ref, tiles_ref, acc, msg_ref):
    acc[...] = jnp.zeros(ACC, F32)
    apply_list(lst, V0AB, (own_ref, other_ref), tiles_ref, acc)
    write_down(acc, row, hot_ref, msg_ref)


def first_apply(lst, row, pair, hots, tiles):
    return pl.pallas_call(
        first_kernel,
        out_shape=(jax.ShapeDtypeStruct(ACC, F32), MESSAGE),
        in_specs=[smem(), smem()] + [vmem()] * 4,
        out_specs=(vmem(), vmem()),
        compiler_params=PARAMS,
        name="first",
    )(lst, row, *pair, hots, tiles)


def down_step_kernel(
    lst, slab, row, own_ref, other_ref, own0, other0, hot_ref, tiles_ref, acc_in, acc, msg_ref, *, step
):
    step_work(lst, slab, TAB, (own_ref, other_ref), (own0, other0), tiles_ref, acc, step)
    if ORDER[step] < NSLAB - 1:
        write_down(acc, row, hot_ref, msg_ref)
    else:
        write_up(acc, msg_ref)


def down_step(lst, slab, row, pair, first_pair, hots, tiles, acc, step):
    return pl.pallas_call(
        functools.partial(down_step_kernel, step=step),
        out_shape=(jax.ShapeDtypeStruct(ACC, F32), MESSAGE),
        in_specs=[smem(), smem(), smem()] + [vmem()] * 7,
        out_specs=(vmem(), vmem()),
        input_output_aliases={9: 0},
        compiler_params=PARAMS,
        name="down_step",
    )(lst, slab, row, *pair, *first_pair, hots, tiles, acc)


def up_step_kernel(
    lst, slab, own_ref, other_ref, own0, other0, tiles_ref, acc_in, acc, msg_ref, *, step
):
    step_work(lst, slab, LA, (own_ref, other_ref), (own0, other0), tiles_ref, acc, step)
    write_up(acc, msg_ref)


def up_step(lst, slab, pair, first_pair, tiles, acc, step):
    return pl.pallas_call(
        functools.partial(up_step_kernel, step=step),
        out_shape=(jax.ShapeDtypeStruct(ACC, F32), MESSAGE),
        in_specs=[smem(), smem()] + [vmem()] * 6,
        out_specs=(vmem(), vmem()),
        input_output_aliases={7: 0},
        compiler_params=PARAMS,
        name="up_step",
    )(lst, slab, *pair, *first_pair, tiles, acc)


def last_kernel(lst, slab, tiles_ref, own0, other0, *refs):
    gathered, acc, msg_ref = refs[:12], refs[13], refs[14]
    for k, s in enumerate((1, 2, 3, 2, 1, 0)):
        pair = gathered[2 * k], gathered[2 * k + 1]

        @pl.when(slab[0] == s)
        def _(k=k, s=s, pair=pair):
            if s == 0:
                apply_list(lst, LA, pair, tiles_ref, acc)
            apply_list(lst, TC if k < NSLAB - 1 else LBC, pair, tiles_ref, acc)

    apply_list(lst, V0C, (own0, other0), tiles_ref, acc, late_start(slab, len(ORDER)))
    for r in range(NROW):
        for b in range(BLK):
            msg_ref[r, b] = acc[r * BLK + b].astype(BF)


def last_apply(lst, slab, tiles, first_pair, pairs, acc):
    flat = [ref for pair in pairs for ref in pair]
    return pl.pallas_call(
        last_kernel,
        out_shape=(
            jax.ShapeDtypeStruct(ACC, F32),
            jax.ShapeDtypeStruct((NROW, BLK, W, B), BF),
        ),
        in_specs=[smem(), smem()] + [vmem()] * 16,
        out_specs=(vmem(), vmem()),
        input_output_aliases={17: 0},
        compiler_params=PARAMS,
        name="last",
    )(lst, slab, tiles, *first_pair, *flat, acc)[1]


def split(x):
    high = x.astype(BF)
    rest = x - high.astype(F32)
    return jnp.concatenate([high, rest.astype(BF)], axis=0)


def row_total(rcv_ref, place, b):
    part = rcv_ref[place * NROW, b].astype(F32)
    for r in range(1, NROW):
        part = part + rcv_ref[place * NROW + r, b].astype(F32)
    return part


def down_kernel(rcv_ref, rhs_ref, coef_ref, out_ref):
    for b in range(TGT):
        pulled = row_total(rcv_ref, 0, b) * coef_ref[:, b * B : (b + 1) * B]
        value = (rhs_ref[b] - pulled).astype(BF)
        for z in range(HALF):
            out_ref[z, b] = value


def up_kernel(rcv_ref, coef_ref, hot_ref, out_ref):
    values = jnp.concatenate(
        [
            split(row_total(rcv_ref, 1, b) * coef_ref[:, b * B : (b + 1) * B])
            for b in range(TGT)
        ],
        axis=1,
    )
    total = jnp.dot(values, hot_ref[...], preferred_element_type=F32)
    lifted = -(total[:W] + total[W:])
    for b in range(PRT):
        value = lifted[:, b * B : (b + 1) * B].astype(BF)
        for z in range(HALF):
            out_ref[z, b] = value


def combine(kernel, received, others, blocks, name):
    return pl.pallas_call(
        kernel,
        out_shape=jax.ShapeDtypeStruct((HALF, blocks, W, B), BF),
        in_specs=[vmem()] * (1 + len(others)),
        out_specs=vmem(),
        compiler_params=PARAMS,
        name=name,
    )(received, *others)


def prepare_kernel(count, slab, rhs_ref, out_ref, target_ref):
    for b in range(BLK):
        value = rhs_ref[0, :, b * B : (b + 1) * B]
        if b < TGT:
            target_ref[b] = value
            value = jnp.where(slab[0] == 0, value, 0.0)
        value = jnp.where(b < count[0], value, 0.0).astype(BF)
        for z in range(HALF):
            out_ref[z, b] = value


def prepare(right_sides, section_blocks, slab):
    return pl.pallas_call(
        prepare_kernel,
        out_shape=(
            jax.ShapeDtypeStruct((HALF, BLK, W, B), BF),
            jax.ShapeDtypeStruct((TGT, W, B), F32),
        ),
        in_specs=[smem(), smem(), vmem()],
        out_specs=(vmem(), vmem()),
        compiler_params=PARAMS,
        name="prepare",
    )(section_blocks, slab, right_sides)


def finish_kernel(count, parts_ref, out_ref):
    for b in range(BLK):
        total = parts_ref[0, b].astype(F32)
        for r in range(1, NROW):
            total = total + parts_ref[r, b].astype(F32)
        out_ref[0, :, b * B : (b + 1) * B] = jnp.where(b < count[0], total, 0.0)


def finish(section_blocks, parts):
    return pl.pallas_call(
        finish_kernel,
        out_shape=jax.ShapeDtypeStruct((1, W, BLK * B), F32),
        in_specs=[smem(), vmem()],
        out_specs=vmem(),
        compiler_params=PARAMS,
        name="finish",
    )(section_blocks, parts)


Z_GROUPS = [[2 * z + k for z in range(HALF)] for k in range(2)]


def gather(copies):
    own = lax.all_to_all(copies, "col", 0, 0, tiled=True, axis_index_groups=Z_GROUPS)
    own = own.reshape(HALF * copies.shape[1], W, B)
    return own, lax.ppermute(own, "col", [(c, c ^ 1) for c in range(NCOL)])


def exchange(message, low):
    groups = [
        [(s + k) % NSLAB * NROW + r for k in range(2) for r in range(NROW)]
        for s in (low, low + 2)
    ]
    return lax.all_to_all(message, ("slab", "row"), 0, 0, tiled=True, axis_index_groups=groups)


def from_next(value, turn):
    pairs = [
        ((s + 1) * NROW + (r + turn) % NROW, s * NROW + r)
        for s in range(NSLAB - 1)
        for r in range(NROW)
    ]
    return lax.ppermute(value, ("slab", "row"), pairs)


def body(right_sides, front_tiles, tile_rows, tile_cols, section_blocks, plane_map, interface_coef):
    slab = lax.axis_index("slab").astype(jnp.int32)
    row = lax.axis_index("row").astype(jnp.int32)
    col = lax.axis_index("col").astype(jnp.int32)
    slab = slab.reshape(1)
    row = row.reshape(1)
    col = col.reshape(1)
    map_own = plane_map.astype(F32)
    pack_next = from_next(jnp.concatenate([map_own, interface_coef], axis=0), 0)
    coef_next = pack_next[1:2]
    maps_next = jnp.concatenate(
        [pack_next[0:1]] + [from_next(map_own, d) for d in range(1, NROW)], axis=0
    ).astype(jnp.int32)

    copies, rhs_target = prepare(right_sides, section_blocks, slab)
    partner = jnp.arange(PRT * B, dtype=jnp.int32)
    hots = (partner[None, :, None] == maps_next[:, None, :]).astype(BF)
    hot_next = (maps_next[0][:, None] == partner[None, :]).astype(BF)

    start = gather(copies)
    lst = make_lists(tile_rows, tile_cols, col)
    tiles = load_tiles(front_tiles[0], start[0])
    start, hots, hot_next, coef_next, rhs_target, lst, tiles = lax.optimization_barrier(
        (start, hots, hot_next, coef_next, rhs_target, lst, tiles)
    )
    acc, msg = first_apply(lst, row, start, hots, tiles)
    pairs = []
    for step, active in enumerate(ORDER[: NSLAB - 1]):
        rcv = exchange(msg, active - 1)
        pairs.append(gather(combine(down_kernel, rcv, (rhs_target, interface_coef), TGT, "down")))
        acc, msg = down_step(lst, slab, row, pairs[-1], start, hots, tiles, acc, step)
    for s in range(NSLAB - 2, -1, -1):
        rcv = exchange(msg, s)
        pairs.append(gather(combine(up_kernel, rcv, (coef_next, hot_next), PRT, "up")))
        if s > 0:
            acc, msg = up_step(lst, slab, pairs[-1], start, tiles, acc, 2 * NSLAB - 3 - s)
    msg = last_apply(lst, slab, tiles, start, pairs, acc)
    return finish(section_blocks, lax.all_to_all(msg, "row", 0, 0, tiled=True))


def solution(mesh):
    placed = (
        P("slab", None, ("col", "row")),
        P("slab", ("col", "row"), None, None),
        P("slab", ("col", "row")),
        P("slab", ("col", "row")),
        P("slab"),
        P("slab", ("col", "row")),
        P("slab", ("col", "row")),
    )
    return jax.shard_map(
        body, mesh=mesh, in_specs=placed, out_specs=P("slab", None, ("col", "row")), check_vma=False
    )
```

```python
import functools

import jax
import jax.numpy as jnp
from jax import lax
from jax.experimental import pallas as pl
from jax.experimental.pallas import tpu as pltpu
from jax.sharding import PartitionSpec as P

B = 128
BLK = 8
NROW = 4
NCOL = 16
NSLAB = 4
W = 32
NT = 128
UNROLL = 8
TGT = 2
PRT = 4
BF = jnp.bfloat16
F32 = jnp.float32


def smem():
    return pl.BlockSpec(memory_space=pltpu.SMEM)


def vmem():
    return pl.BlockSpec(memory_space=pltpu.VMEM)


PARAMS = pltpu.CompilerParams(vmem_limit_bytes=24 * 2**20)
ACC = (NROW * BLK + 1, W, B)
LISTS = 9
V0AB, V0C, TC, TAB, LA, LBC = 0, 1, 2, 3, 5, 7
CHUNK = 3
ORDER = (1, 2, 3, 2, 1)
HALF = NCOL // 2


def shr(x, n):
    return lax.shift_right_logical(x, jnp.int32(n))


def product(v, tile):
    return lax.dot_general(v, tile, (((1,), (1,)), ((), ())), preferred_element_type=F32)


def picked(side, own_ref, other_ref, at):
    return jnp.where(side == 0, own_ref[at], other_ref[at])


def helper_kernel(
    col_index, rows_hbm, cols_hbm, map_hbm, coef_hbm, out_ref, pack_ref,
    rows_ref, cols_ref, map_ref, coef_ref, sems,
):
    ins = (rows_hbm, cols_hbm, map_hbm, coef_hbm)
    copies = [
        pltpu.make_async_copy(src, dst, sems.at[k])
        for k, (src, dst) in enumerate(zip(ins, (rows_ref, cols_ref, map_ref, coef_ref)))
    ]
    for copy in copies:
        copy.start()
    for copy in copies:
        copy.wait()
    pack_ref[0:1, :] = map_ref[...].astype(F32)
    pack_ref[1:2, :] = coef_ref[...]
    lane = lax.broadcasted_iota(jnp.int32, (1, NT), 1)
    down = lax.broadcasted_iota(jnp.int32, (NT, NT), 0)
    across = lax.broadcasted_iota(jnp.int32, (NT, NT), 1)
    before = jnp.where(down < across, 1.0, 0.0).astype(BF)
    row = rows_ref[...] - col_index[0] * (NROW * BLK)
    col = cols_ref[...]
    part = shr(col, 5)
    half = shr(part, 1)
    side = (part & 1) ^ (col_index[0] & 1)
    blk = col & (BLK - 1)
    out = row & (BLK - 1)
    early = out < PRT
    target = blk < TGT
    low = blk < PRT
    own = side == 0
    other = side == 1
    member = (
        (BLK, early),
        (BLK, out >= PRT),
        (TGT, target & (out >= PRT)),
        (TGT, target & early & own),
        (TGT, target & early & other),
        (PRT, low & (out < TGT) & own),
        (PRT, low & (out < TGT) & other),
        (PRT, low & (out >= TGT) & own),
        (PRT, low & (out >= TGT) & other),
    )
    sizes = jnp.zeros((1, NT), jnp.int32)
    for k, (width, belongs) in enumerate(member):
        one = jnp.where(belongs, 1.0, 0.0)
        count = jnp.sum(one, axis=1, keepdims=True).astype(jnp.int32)
        rank = jnp.dot(
            jnp.broadcast_to(one, (8, NT)).astype(BF), before, preferred_element_type=F32
        )[0:1].astype(jnp.int32)
        rank = jnp.where(belongs, rank, -1)
        place = jnp.where(jnp.broadcast_to(rank, (NT, NT)) == down, 1.0, 0.0).astype(BF)
        upper = half * width + blk + side * 64
        digits = jnp.concatenate(
            [x.astype(F32) for x in (lane, row, upper, upper, upper, upper, upper, upper)], axis=0
        ).astype(BF)
        moved = lax.dot_general(
            digits, place, (((1,), (1,)), ((), ())), preferred_element_type=F32
        ).astype(jnp.int32)
        entry = moved[0:1] + moved[1:2] * NT + moved[2:3] * 8192
        out_ref[k : k + 1, :] = jnp.where(lane < count, entry, NROW * BLK * NT)
        sizes = jnp.where(lane == k, shr(count + UNROLL - 1, 3), sizes)
    for k in range(LISTS, 16):
        out_ref[k : k + 1, :] = sizes


def helper(col_index, tile_rows, tile_cols, plane_map, interface_coef):
    ins = (tile_rows, tile_cols, plane_map, interface_coef)
    return pl.pallas_call(
        helper_kernel,
        out_shape=(
            jax.ShapeDtypeStruct((16, NT), jnp.int32),
            jax.ShapeDtypeStruct((2, TGT * B), F32),
        ),
        in_specs=[smem()] + [pl.BlockSpec(memory_space=pltpu.HBM)] * 4,
        out_specs=(vmem(), vmem()),
        scratch_shapes=[pltpu.VMEM(x.shape, x.dtype) for x in ins] + [pltpu.SemaphoreType.DMA((4,))],
        compiler_params=PARAMS,
        name="helper",
    )(col_index, *[pltpu.with_memory_space_constraint(x, pltpu.HBM) for x in ins])


def load_kernel(tiles_hbm, own_ref, tiles_ref, sem):
    copy = pltpu.make_async_copy(tiles_hbm, tiles_ref, sem)
    copy.start()
    copy.wait()


def load_tiles(tiles, own):
    return pl.pallas_call(
        load_kernel,
        out_shape=jax.ShapeDtypeStruct(tiles.shape, BF),
        in_specs=[pl.BlockSpec(memory_space=pltpu.HBM), vmem()],
        out_specs=vmem(),
        scratch_shapes=[pltpu.SemaphoreType.DMA],
        compiler_params=PARAMS,
        name="load",
    )(pltpu.with_memory_space_constraint(tiles, pltpu.HBM), own)


def apply_list(lst, which, sources, tiles_ref, acc, low=0, most=NT):
    def group(g, _):
        rows, done = [], []
        for u in range(UNROLL):
            e = lst[which, g * UNROLL + u]
            at = shr(e, 13) & 63
            v = sources[0][at] if len(sources) == 1 else picked(shr(e, 19), *sources, at)
            rows.append(shr(e, 7) & 63)
            done.append(product(v, tiles_ref[e & 127]))
        for r, d in zip(rows, done):
            acc[r] += d
        return 0

    groups = lst[LISTS, which]
    lax.fori_loop(low, jnp.minimum(groups, low + most), group, 0)


def late_start(slab, step):
    used = jnp.int32(step)
    for active in ORDER[:step]:
        used = used - jnp.where(slab[0] == active, jnp.int32(1), jnp.int32(0))
    return used * CHUNK


def write_down(acc, row, hot_ref, msg_ref):
    for d in range(NROW):
        r = (row[0] + d) & (NROW - 1)
        values = jnp.concatenate([acc[r * BLK + b].astype(BF) for b in range(PRT)], axis=1)
        part = jnp.dot(values, hot_ref[d], preferred_element_type=F32).astype(BF)
        for b in range(TGT):
            for s in range(2):
                msg_ref[s * NROW + r, b] = part[:, b * B : (b + 1) * B]


def write_up(acc, msg_ref):
    for r in range(NROW):
        for b in range(TGT):
            part = acc[r * BLK + b].astype(BF)
            for s in range(2):
                msg_ref[s * NROW + r, b] = part


MESSAGE = jax.ShapeDtypeStruct((2 * NROW, TGT, W, B), BF)


def first_kernel(lst, row, own_ref, other_ref, hot_ref, tiles_ref, acc, msg_ref):
    acc[...] = jnp.zeros(ACC, F32)
    apply_list(lst, V0AB, (own_ref, other_ref), tiles_ref, acc)
    write_down(acc, row, hot_ref, msg_ref)


def first_apply(lst, row, pair, hots, tiles):
    return pl.pallas_call(
        first_kernel,
        out_shape=(jax.ShapeDtypeStruct(ACC, F32), MESSAGE),
        in_specs=[smem(), smem()] + [vmem()] * 4,
        out_specs=(vmem(), vmem()),
        compiler_params=PARAMS,
        name="first",
    )(lst, row, *pair, hots, tiles)


def own_kernel(lst, slab, own_ref, own0, other0, tiles_ref, acc_in, acc, *, which, step):
    @pl.when(slab[0] == ORDER[step])
    def _():
        apply_list(lst, which, (own_ref,), tiles_ref, acc)

    @pl.when(slab[0] != ORDER[step])
    def _():
        apply_list(lst, V0C, (own0, other0), tiles_ref, acc, late_start(slab, step), CHUNK)


def own_apply(lst, slab, which, own, first_pair, tiles, acc, step):
    return pl.pallas_call(
        functools.partial(own_kernel, which=which, step=step),
        out_shape=jax.ShapeDtypeStruct(ACC, F32),
        in_specs=[smem(), smem()] + [vmem()] * 5,
        out_specs=vmem(),
        input_output_aliases={6: 0},
        compiler_params=PARAMS,
        name="own",
    )(lst, slab, own, *first_pair, tiles, acc)


def other_kernel(lst, slab, row, other_ref, hot_ref, tiles_ref, acc_in, acc, msg_ref, *, which, step):
    @pl.when(slab[0] == ORDER[step])
    def _():
        apply_list(lst, which + 1, (other_ref,), tiles_ref, acc)

    if step + 1 < len(ORDER) and ORDER[step] < ORDER[step + 1]:
        write_down(acc, row, hot_ref, msg_ref)
    else:
        write_up(acc, msg_ref)


def other_apply(lst, slab, row, which, other, hots, tiles, acc, step):
    return pl.pallas_call(
        functools.partial(other_kernel, which=which, step=step),
        out_shape=(jax.ShapeDtypeStruct(ACC, F32), MESSAGE),
        in_specs=[smem(), smem(), smem()] + [vmem()] * 4,
        out_specs=(vmem(), vmem()),
        input_output_aliases={6: 0},
        compiler_params=PARAMS,
        name="other",
    )(lst, slab, row, other, hots, tiles, acc)


def step_apply(lst, slab, row, which, pair, first_pair, hots, tiles, acc, step):
    acc = own_apply(lst, slab, which, pair[0], first_pair, tiles, acc, step)
    return other_apply(lst, slab, row, which, pair[1], hots, tiles, acc, step)


def last_own_kernel(lst, slab, tiles_ref, own0, other0, *refs):
    gathered, acc = refs[:11], refs[12]
    for k, s in enumerate((1, 2, 3, 2, 1, 0)):
        @pl.when(slab[0] == s)
        def _(k=k, s=s):
            if s == 0:
                apply_list(lst, LA, gathered[2 * k : 2 * k + 1], tiles_ref, acc)
            if k < NSLAB - 1:
                apply_list(lst, TC, gathered[2 * k : 2 * k + 2], tiles_ref, acc)
            else:
                apply_list(lst, LBC, gathered[2 * k : 2 * k + 1], tiles_ref, acc)
                if s > 0:
                    apply_list(lst, LBC + 1, gathered[2 * k + 1 : 2 * k + 2], tiles_ref, acc)

    apply_list(lst, V0C, (own0, other0), tiles_ref, acc, late_start(slab, len(ORDER)))


def last_other_kernel(lst, slab, tiles_ref, other_ref, acc_in, acc, msg_ref):
    @pl.when(slab[0] == 0)
    def _():
        apply_list(lst, LA + 1, (other_ref,), tiles_ref, acc)
        apply_list(lst, LBC + 1, (other_ref,), tiles_ref, acc)

    for r in range(NROW):
        for b in range(BLK):
            msg_ref[r, b] = acc[r * BLK + b].astype(BF)


def last_apply(lst, slab, tiles, first_pair, pairs, acc):
    flat = [ref for pair in pairs for ref in pair]
    whole = jax.ShapeDtypeStruct(ACC, F32)
    acc = pl.pallas_call(
        last_own_kernel,
        out_shape=whole,
        in_specs=[smem(), smem()] + [vmem()] * 15,
        out_specs=vmem(),
        input_output_aliases={16: 0},
        compiler_params=PARAMS,
        name="last_own",
    )(lst, slab, tiles, *first_pair, *flat[:-1], acc)
    return pl.pallas_call(
        last_other_kernel,
        out_shape=(whole, jax.ShapeDtypeStruct((NROW, BLK, W, B), BF)),
        in_specs=[smem(), smem()] + [vmem()] * 3,
        out_specs=(vmem(), vmem()),
        input_output_aliases={4: 0},
        compiler_params=PARAMS,
        name="last_other",
    )(lst, slab, tiles, flat[-1], acc)[1]


def split(x):
    high = x.astype(BF)
    rest = x - high.astype(F32)
    return jnp.concatenate([high, rest.astype(BF)], axis=0)


def row_total(rcv_ref, place, b):
    part = rcv_ref[place * NROW, b].astype(F32)
    for r in range(1, NROW):
        part = part + rcv_ref[place * NROW + r, b].astype(F32)
    return part


def down_kernel(rcv_ref, rhs_ref, coef_ref, out_ref):
    for b in range(TGT):
        pulled = row_total(rcv_ref, 0, b) * coef_ref[:, b * B : (b + 1) * B]
        value = (rhs_ref[b] - pulled).astype(BF)
        for z in range(HALF):
            out_ref[z, b] = value


def up_kernel(rcv_ref, coef_ref, hot_ref, out_ref):
    values = jnp.concatenate(
        [
            split(row_total(rcv_ref, 1, b) * coef_ref[:, b * B : (b + 1) * B])
            for b in range(TGT)
        ],
        axis=1,
    )
    total = jnp.dot(values, hot_ref[...], preferred_element_type=F32)
    lifted = -(total[:W] + total[W:])
    for b in range(PRT):
        value = lifted[:, b * B : (b + 1) * B].astype(BF)
        for z in range(HALF):
            out_ref[z, b] = value


def combine(kernel, received, others, blocks, name):
    return pl.pallas_call(
        kernel,
        out_shape=jax.ShapeDtypeStruct((HALF, blocks, W, B), BF),
        in_specs=[vmem()] * (1 + len(others)),
        out_specs=vmem(),
        compiler_params=PARAMS,
        name=name,
    )(received, *others)


def prepare_kernel(count, slab, rhs_hbm, out_ref, target_ref, rhs_ref, sems):
    wide = 2 * B
    copies = [
        pltpu.make_async_copy(
            rhs_hbm.at[0, :, pl.ds(k * wide, wide)], rhs_ref.at[k], sems.at[k]
        )
        for k in range(BLK // 2)
    ]
    for copy in copies:
        copy.start()
    for b in range(BLK):
        if b % 2 == 0:
            copies[b // 2].wait()
        value = rhs_ref[b // 2, :, b % 2 * B : (b % 2 + 1) * B]
        if b < TGT:
            target_ref[b] = value
            value = jnp.where(slab[0] == 0, value, 0.0)
        value = jnp.where(b < count[0], value, 0.0).astype(BF)
        for z in range(HALF):
            out_ref[z, b] = value


def prepare(right_sides, section_blocks, slab):
    return pl.pallas_call(
        prepare_kernel,
        out_shape=(
            jax.ShapeDtypeStruct((HALF, BLK, W, B), BF),
            jax.ShapeDtypeStruct((TGT, W, B), F32),
        ),
        in_specs=[smem(), smem(), pl.BlockSpec(memory_space=pltpu.HBM)],
        out_specs=(vmem(), vmem()),
        scratch_shapes=[
            pltpu.VMEM((BLK // 2, W, 2 * B), F32),
            pltpu.SemaphoreType.DMA((BLK // 2,)),
        ],
        compiler_params=PARAMS,
        name="prepare",
    )(section_blocks, slab, pltpu.with_memory_space_constraint(right_sides, pltpu.HBM))


def finish_kernel(count, parts_ref, out_ref):
    for b in range(BLK):
        total = parts_ref[0, b].astype(F32)
        for r in range(1, NROW):
            total = total + parts_ref[r, b].astype(F32)
        out_ref[0, :, b * B : (b + 1) * B] = jnp.where(b < count[0], total, 0.0)


def finish(section_blocks, parts):
    return pl.pallas_call(
        finish_kernel,
        out_shape=jax.ShapeDtypeStruct((1, W, BLK * B), F32),
        in_specs=[smem(), vmem()],
        out_specs=vmem(),
        compiler_params=PARAMS,
        name="finish",
    )(section_blocks, parts)


Z_GROUPS = [[2 * z + k for z in range(HALF)] for k in range(2)]


def gather(copies):
    own = lax.all_to_all(copies, "col", 0, 0, tiled=True, axis_index_groups=Z_GROUPS)
    own = own.reshape(HALF * copies.shape[1], W, B)
    return own, lax.ppermute(own, "col", [(c, c ^ 1) for c in range(NCOL)])


def exchange(message, low):
    groups = [
        [(s + k) % NSLAB * NROW + r for k in range(2) for r in range(NROW)]
        for s in (low, low + 2)
    ]
    return lax.all_to_all(message, ("slab", "row"), 0, 0, tiled=True, axis_index_groups=groups)


def from_next(value, turn):
    pairs = [
        ((s + 1) * NROW + (r + turn) % NROW, s * NROW + r)
        for s in range(NSLAB - 1)
        for r in range(NROW)
    ]
    return lax.ppermute(value, ("slab", "row"), pairs)


def body(right_sides, front_tiles, tile_rows, tile_cols, section_blocks, plane_map, interface_coef):
    slab = lax.axis_index("slab").astype(jnp.int32)
    row = lax.axis_index("row").astype(jnp.int32)
    col = lax.axis_index("col").astype(jnp.int32)
    slab = slab.reshape(1)
    row = row.reshape(1)
    col = col.reshape(1)
    lst, pack = helper(col, tile_rows, tile_cols, plane_map, interface_coef)
    packs = [from_next(pack, d) for d in range(NROW)]
    coef_next = packs[0][1:2]
    maps_next = jnp.concatenate([p[0:1] for p in packs], axis=0).astype(jnp.int32)

    copies, rhs_target = prepare(right_sides, section_blocks, slab)
    partner = jnp.arange(PRT * B, dtype=jnp.int32)
    hots = (partner[None, :, None] == maps_next[:, None, :]).astype(BF)
    hot_next = (maps_next[0][:, None] == partner[None, :]).astype(BF)

    start = gather(copies)
    tiles = load_tiles(front_tiles[0], start[0])
    start, hots, hot_next, coef_next, rhs_target, lst, tiles = lax.optimization_barrier(
        (start, hots, hot_next, coef_next, rhs_target, lst, tiles)
    )
    acc, msg = first_apply(lst, row, start, hots, tiles)
    pairs = []
    for step in range(2 * NSLAB - 2):
        if step < NSLAB - 1:
            rcv = exchange(msg, step)
            value = combine(down_kernel, rcv, (rhs_target, interface_coef), TGT, "down")
        else:
            rcv = exchange(msg, 2 * NSLAB - 3 - step)
            value = combine(up_kernel, rcv, (coef_next, hot_next), PRT, "up")
        pairs.append(gather(value))
        if step < len(ORDER):
            which = TAB if step < NSLAB - 1 else LA
            acc, msg = step_apply(lst, slab, row, which, pairs[-1], start, hots, tiles, acc, step)
    msg = last_apply(lst, slab, tiles, start, pairs, acc)
    return finish(section_blocks, lax.all_to_all(msg, "row", 0, 0, tiled=True))


def solution(mesh):
    placed = (
        P("slab", None, ("col", "row")),
        P("slab", ("col", "row"), None, None),
        P("slab", ("col", "row")),
        P("slab", ("col", "row")),
        P("slab"),
        P("slab", ("col", "row")),
        P("slab", ("col", "row")),
    )
    return jax.shard_map(
        body, mesh=mesh, in_specs=placed, out_specs=P("slab", None, ("col", "row")), check_vma=False
    )
```

```python
import functools

import jax
import jax.numpy as jnp
from jax import lax
from jax.experimental import pallas as pl
from jax.experimental.pallas import tpu as pltpu
from jax.sharding import PartitionSpec as P

B = 128
BLK = 8
NROW = 4
NCOL = 16
NSLAB = 4
W = 32
NT = 128
UNROLL = 8
TGT = 2
PRT = 4
BF = jnp.bfloat16
F32 = jnp.float32


def smem():
    return pl.BlockSpec(memory_space=pltpu.SMEM)


def vmem():
    return pl.BlockSpec(memory_space=pltpu.VMEM)


PARAMS = pltpu.CompilerParams(vmem_limit_bytes=24 * 2**20)
ACC = (NROW * BLK + 1, W, B)
LISTS = 9
V0AB, V0C, TC, TAB, LA, LBC = 0, 1, 2, 3, 5, 7
CHUNK = 4
ORDER = (1, 2, 3, 2, 1)
HALF = NCOL // 2


def shr(x, n):
    return lax.shift_right_logical(x, jnp.int32(n))


def product(v, tile):
    return lax.dot_general(v, tile, (((1,), (1,)), ((), ())), preferred_element_type=F32)


def picked(side, own_ref, other_ref, at):
    return jnp.where(side == 0, own_ref[at], other_ref[at])


def helper_kernel(
    col_index, rows_hbm, cols_hbm, map_hbm, coef_hbm, out_ref, pack_ref,
    rows_ref, cols_ref, map_ref, coef_ref, sems,
):
    ins = (rows_hbm, cols_hbm, map_hbm, coef_hbm)
    copies = [
        pltpu.make_async_copy(src, dst, sems.at[k])
        for k, (src, dst) in enumerate(zip(ins, (rows_ref, cols_ref, map_ref, coef_ref)))
    ]
    for copy in copies:
        copy.start()
    for copy in copies:
        copy.wait()
    pack_ref[0:1, :] = map_ref[...].astype(F32)
    pack_ref[1:2, :] = coef_ref[...]
    lane = lax.broadcasted_iota(jnp.int32, (1, NT), 1)
    down = lax.broadcasted_iota(jnp.int32, (NT, NT), 0)
    across = lax.broadcasted_iota(jnp.int32, (NT, NT), 1)
    before = jnp.where(down < across, 1.0, 0.0).astype(BF)
    row = rows_ref[...] - col_index[0] * (NROW * BLK)
    col = cols_ref[...]
    part = shr(col, 5)
    half = shr(part, 1)
    side = (part & 1) ^ (col_index[0] & 1)
    blk = col & (BLK - 1)
    out = row & (BLK - 1)
    early = out < PRT
    target = blk < TGT
    low = blk < PRT
    own = side == 0
    other = side == 1
    member = (
        (BLK, early),
        (BLK, out >= PRT),
        (TGT, target & (out >= PRT)),
        (TGT, target & early & own),
        (TGT, target & early & other),
        (PRT, low & (out < TGT) & own),
        (PRT, low & (out < TGT) & other),
        (PRT, low & (out >= TGT) & own),
        (PRT, low & (out >= TGT) & other),
    )
    sizes = jnp.zeros((1, NT), jnp.int32)
    for k, (width, belongs) in enumerate(member):
        one = jnp.where(belongs, 1.0, 0.0)
        count = jnp.sum(one, axis=1, keepdims=True).astype(jnp.int32)
        rank = jnp.dot(
            jnp.broadcast_to(one, (8, NT)).astype(BF), before, preferred_element_type=F32
        )[0:1].astype(jnp.int32)
        rank = jnp.where(belongs, rank, -1)
        place = jnp.where(jnp.broadcast_to(rank, (NT, NT)) == down, 1.0, 0.0).astype(BF)
        upper = half * width + blk + side * 64
        digits = jnp.concatenate(
            [x.astype(F32) for x in (lane, row, upper, upper, upper, upper, upper, upper)], axis=0
        ).astype(BF)
        moved = lax.dot_general(
            digits, place, (((1,), (1,)), ((), ())), preferred_element_type=F32
        ).astype(jnp.int32)
        entry = moved[0:1] + moved[1:2] * NT + moved[2:3] * 8192
        out_ref[k : k + 1, :] = jnp.where(lane < count, entry, NROW * BLK * NT)
        sizes = jnp.where(lane == k, shr(count + UNROLL - 1, 3), sizes)
    for k in range(LISTS, 16):
        out_ref[k : k + 1, :] = sizes


def helper(col_index, tile_rows, tile_cols, plane_map, interface_coef):
    ins = (tile_rows, tile_cols, plane_map, interface_coef)
    return pl.pallas_call(
        helper_kernel,
        out_shape=(
            jax.ShapeDtypeStruct((16, NT), jnp.int32),
            jax.ShapeDtypeStruct((2, TGT * B), F32),
        ),
        in_specs=[smem()] + [pl.BlockSpec(memory_space=pltpu.HBM)] * 4,
        out_specs=(vmem(), vmem()),
        scratch_shapes=[pltpu.VMEM(x.shape, x.dtype) for x in ins] + [pltpu.SemaphoreType.DMA((4,))],
        compiler_params=PARAMS,
        name="helper",
    )(col_index, *[pltpu.with_memory_space_constraint(x, pltpu.HBM) for x in ins])


SPLIT = NT // 2


def half_load(tiles_hbm, tiles_ref, sem, k):
    at = pl.ds(k * SPLIT, SPLIT)
    return pltpu.make_async_copy(tiles_hbm.at[at], tiles_ref.at[at], sem)


def load_kernel(tiles_hbm, own_ref, tiles_ref, sem):
    copy = half_load(tiles_hbm, tiles_ref, sem, 0)
    copy.start()
    copy.wait()


def load_tiles(tiles, own):
    return pl.pallas_call(
        load_kernel,
        out_shape=jax.ShapeDtypeStruct(tiles.shape, BF),
        in_specs=[pl.BlockSpec(memory_space=pltpu.HBM), vmem()],
        out_specs=vmem(),
        scratch_shapes=[pltpu.SemaphoreType.DMA],
        compiler_params=PARAMS,
        name="load",
    )(pltpu.with_memory_space_constraint(tiles, pltpu.HBM), own)


def apply_group(lst, which, g, sources, tiles_ref, acc):
    rows, done = [], []
    for u in range(UNROLL):
        e = lst[which, g * UNROLL + u]
        at = shr(e, 13) & 63
        v = sources[0][at] if len(sources) == 1 else picked(shr(e, 19), *sources, at)
        rows.append(shr(e, 7) & 63)
        done.append(product(v, tiles_ref[e & 127]))
    for r, d in zip(rows, done):
        acc[r] += d


def apply_list(lst, which, sources, tiles_ref, acc, low=0, most=NT):
    def group(g, _):
        apply_group(lst, which, g, sources, tiles_ref, acc)
        return 0

    groups = lst[LISTS, which]
    lax.fori_loop(low, jnp.minimum(groups, low + most), group, 0)


def late_start(slab, step):
    used = jnp.int32(step)
    for j in range(step):
        busy = slab[0] == ORDER[j]
        if 0 < j < NSLAB:
            busy = busy | (slab[0] == ORDER[j - 1])
        used = used - jnp.where(busy, jnp.int32(1), jnp.int32(0))
    return used * CHUNK


def write_down(acc, row, hot_ref, msg_ref):
    for d in range(NROW):
        r = (row[0] + d) & (NROW - 1)
        values = jnp.concatenate([acc[r * BLK + b].astype(BF) for b in range(PRT)], axis=1)
        part = jnp.dot(values, hot_ref[d], preferred_element_type=F32).astype(BF)
        for b in range(TGT):
            for s in range(2):
                msg_ref[s * NROW + r, b] = part[:, b * B : (b + 1) * B]


def write_up(acc, msg_ref):
    for r in range(NROW):
        for b in range(TGT):
            part = acc[r * BLK + b].astype(BF)
            for s in range(2):
                msg_ref[s * NROW + r, b] = part


MESSAGE = jax.ShapeDtypeStruct((2 * NROW, TGT, W, B), BF)


def first_kernel(lst, row, own_ref, other_ref, hot_ref, tiles_hbm, tiles_in, acc, tiles_ref, msg_ref, sem):
    rest = half_load(tiles_hbm, tiles_ref, sem, 1)
    rest.start()
    acc[...] = jnp.zeros(ACC, F32)

    def group(g, loaded):
        late = lst[V0AB, g * UNROLL] & SPLIT
        for u in range(1, UNROLL):
            late = late | (lst[V0AB, g * UNROLL + u] & SPLIT)

        @pl.when((late > 0) & (loaded == 0))
        def _():
            rest.wait()

        apply_group(lst, V0AB, g, (own_ref, other_ref), tiles_ref, acc)
        return loaded | late

    loaded = lax.fori_loop(0, lst[LISTS, V0AB], group, jnp.int32(0))

    @pl.when(loaded == 0)
    def _():
        rest.wait()

    write_down(acc, row, hot_ref, msg_ref)


def first_apply(lst, row, pair, hots, front, tiles):
    return pl.pallas_call(
        first_kernel,
        out_shape=(
            jax.ShapeDtypeStruct(ACC, F32),
            jax.ShapeDtypeStruct(tiles.shape, BF),
            MESSAGE,
        ),
        in_specs=[smem(), smem()] + [vmem()] * 3 + [pl.BlockSpec(memory_space=pltpu.HBM), vmem()],
        out_specs=(vmem(), vmem(), vmem()),
        scratch_shapes=[pltpu.SemaphoreType.DMA],
        input_output_aliases={6: 1},
        compiler_params=PARAMS,
        name="first",
    )(lst, row, *pair, hots, pltpu.with_memory_space_constraint(front, pltpu.HBM), tiles)


def own_kernel(lst, slab, own_ref, own0, other0, tiles_ref, *refs, which, step):
    before, acc = refs[:-2], refs[-1]
    active = slab[0] == ORDER[step]
    after = slab[0] == ORDER[step - 1] if before else slab[0] < 0

    @pl.when(active)
    def _():
        apply_list(lst, which, (own_ref,), tiles_ref, acc)

    if before:
        @pl.when(after)
        def _():
            apply_list(lst, TC, before, tiles_ref, acc)

    @pl.when(jnp.logical_not(active | after))
    def _():
        apply_list(lst, V0C, (own0, other0), tiles_ref, acc, late_start(slab, step), CHUNK)


def own_apply(lst, slab, which, own, before, first_pair, tiles, acc, step):
    ins = (own, *first_pair, tiles, *before, acc)
    return pl.pallas_call(
        functools.partial(own_kernel, which=which, step=step),
        out_shape=jax.ShapeDtypeStruct(ACC, F32),
        in_specs=[smem(), smem()] + [vmem()] * len(ins),
        out_specs=vmem(),
        input_output_aliases={1 + len(ins): 0},
        compiler_params=PARAMS,
        name="own",
    )(lst, slab, *ins)


def other_kernel(lst, slab, row, other_ref, hot_ref, tiles_ref, acc_in, acc, msg_ref, *, which, step):
    @pl.when(slab[0] == ORDER[step])
    def _():
        apply_list(lst, which + 1, (other_ref,), tiles_ref, acc)

    if step + 1 < len(ORDER) and ORDER[step] < ORDER[step + 1]:
        write_down(acc, row, hot_ref, msg_ref)
    else:
        write_up(acc, msg_ref)


def other_apply(lst, slab, row, which, other, hots, tiles, acc, step):
    return pl.pallas_call(
        functools.partial(other_kernel, which=which, step=step),
        out_shape=(jax.ShapeDtypeStruct(ACC, F32), MESSAGE),
        in_specs=[smem(), smem(), smem()] + [vmem()] * 4,
        out_specs=(vmem(), vmem()),
        input_output_aliases={6: 0},
        compiler_params=PARAMS,
        name="other",
    )(lst, slab, row, other, hots, tiles, acc)


def step_apply(lst, slab, row, which, pairs, first_pair, hots, tiles, acc, step):
    own, other = pairs[-1]
    before = pairs[-2] if 0 < step < NSLAB else ()
    acc = own_apply(lst, slab, which, own, before, first_pair, tiles, acc, step)
    return other_apply(lst, slab, row, which, other, hots, tiles, acc, step)


def last_own_kernel(lst, slab, tiles_ref, own0, other0, *refs):
    gathered, acc = refs[:5], refs[6]
    for s in range(NSLAB - 1):
        at = 2 * (NSLAB - 2 - s)

        @pl.when(slab[0] == s)
        def _(s=s, at=at):
            if s == 0:
                apply_list(lst, LA, gathered[at : at + 1], tiles_ref, acc)
            apply_list(lst, LBC, gathered[at : at + 1], tiles_ref, acc)
            if s > 0:
                apply_list(lst, LBC + 1, gathered[at + 1 : at + 2], tiles_ref, acc)

    apply_list(lst, V0C, (own0, other0), tiles_ref, acc, late_start(slab, len(ORDER)))


def last_other_kernel(lst, slab, tiles_ref, other_ref, acc_in, acc, msg_ref):
    @pl.when(slab[0] == 0)
    def _():
        apply_list(lst, LA + 1, (other_ref,), tiles_ref, acc)
        apply_list(lst, LBC + 1, (other_ref,), tiles_ref, acc)

    for r in range(NROW):
        for b in range(BLK):
            msg_ref[r, b] = acc[r * BLK + b].astype(BF)


def last_apply(lst, slab, tiles, first_pair, pairs, acc):
    flat = [ref for pair in pairs[NSLAB - 1 :] for ref in pair]
    whole = jax.ShapeDtypeStruct(ACC, F32)
    acc = pl.pallas_call(
        last_own_kernel,
        out_shape=whole,
        in_specs=[smem(), smem()] + [vmem()] * 9,
        out_specs=vmem(),
        input_output_aliases={10: 0},
        compiler_params=PARAMS,
        name="last_own",
    )(lst, slab, tiles, *first_pair, *flat[:-1], acc)
    return pl.pallas_call(
        last_other_kernel,
        out_shape=(whole, jax.ShapeDtypeStruct((NROW, BLK, W, B), BF)),
        in_specs=[smem(), smem()] + [vmem()] * 3,
        out_specs=(vmem(), vmem()),
        input_output_aliases={4: 0},
        compiler_params=PARAMS,
        name="last_other",
    )(lst, slab, tiles, flat[-1], acc)[1]


def split(x):
    high = x.astype(BF)
    rest = x - high.astype(F32)
    return jnp.concatenate([high, rest.astype(BF)], axis=0)


def row_total(rcv_ref, place, b):
    part = rcv_ref[place * NROW, b].astype(F32)
    for r in range(1, NROW):
        part = part + rcv_ref[place * NROW + r, b].astype(F32)
    return part


def down_kernel(rcv_ref, rhs_ref, coef_ref, out_ref):
    for b in range(TGT):
        pulled = row_total(rcv_ref, 0, b) * coef_ref[:, b * B : (b + 1) * B]
        value = (rhs_ref[b] - pulled).astype(BF)
        for z in range(HALF):
            out_ref[z, b] = value


def up_kernel(rcv_ref, coef_ref, hot_ref, out_ref):
    values = jnp.concatenate(
        [
            split(row_total(rcv_ref, 1, b) * coef_ref[:, b * B : (b + 1) * B])
            for b in range(TGT)
        ],
        axis=1,
    )
    total = jnp.dot(values, hot_ref[...], preferred_element_type=F32)
    lifted = -(total[:W] + total[W:])
    for b in range(PRT):
        value = lifted[:, b * B : (b + 1) * B].astype(BF)
        for z in range(HALF):
            out_ref[z, b] = value


def combine(kernel, received, others, blocks, name):
    return pl.pallas_call(
        kernel,
        out_shape=jax.ShapeDtypeStruct((HALF, blocks, W, B), BF),
        in_specs=[vmem()] * (1 + len(others)),
        out_specs=vmem(),
        compiler_params=PARAMS,
        name=name,
    )(received, *others)


def prepare_kernel(count, slab, rhs_hbm, out_ref, target_ref, rhs_ref, sems):
    wide = 2 * B
    copies = [
        pltpu.make_async_copy(
            rhs_hbm.at[0, :, pl.ds(k * wide, wide)], rhs_ref.at[k], sems.at[k]
        )
        for k in range(BLK // 2)
    ]
    for copy in copies:
        copy.start()
    for b in range(BLK):
        if b % 2 == 0:
            copies[b // 2].wait()
        value = rhs_ref[b // 2, :, b % 2 * B : (b % 2 + 1) * B]
        if b < TGT:
            target_ref[b] = value
            value = jnp.where(slab[0] == 0, value, 0.0)
        value = jnp.where(b < count[0], value, 0.0).astype(BF)
        for z in range(HALF):
            out_ref[z, b] = value


def prepare(right_sides, section_blocks, slab):
    return pl.pallas_call(
        prepare_kernel,
        out_shape=(
            jax.ShapeDtypeStruct((HALF, BLK, W, B), BF),
            jax.ShapeDtypeStruct((TGT, W, B), F32),
        ),
        in_specs=[smem(), smem(), pl.BlockSpec(memory_space=pltpu.HBM)],
        out_specs=(vmem(), vmem()),
        scratch_shapes=[
            pltpu.VMEM((BLK // 2, W, 2 * B), F32),
            pltpu.SemaphoreType.DMA((BLK // 2,)),
        ],
        compiler_params=PARAMS,
        name="prepare",
    )(section_blocks, slab, pltpu.with_memory_space_constraint(right_sides, pltpu.HBM))


def finish_kernel(count, parts_ref, out_ref):
    for b in range(BLK):
        total = parts_ref[0, b].astype(F32)
        for r in range(1, NROW):
            total = total + parts_ref[r, b].astype(F32)
        out_ref[0, :, b * B : (b + 1) * B] = jnp.where(b < count[0], total, 0.0)


def finish(section_blocks, parts):
    return pl.pallas_call(
        finish_kernel,
        out_shape=jax.ShapeDtypeStruct((1, W, BLK * B), F32),
        in_specs=[smem(), vmem()],
        out_specs=vmem(),
        compiler_params=PARAMS,
        name="finish",
    )(section_blocks, parts)


Z_GROUPS = [[2 * z + k for z in range(HALF)] for k in range(2)]


def gather(copies):
    own = lax.all_to_all(copies, "col", 0, 0, tiled=True, axis_index_groups=Z_GROUPS)
    own = own.reshape(HALF * copies.shape[1], W, B)
    return own, lax.ppermute(own, "col", [(c, c ^ 1) for c in range(NCOL)])


def exchange(message, low):
    groups = [
        [(s + k) % NSLAB * NROW + r for k in range(2) for r in range(NROW)]
        for s in (low, low + 2)
    ]
    return lax.all_to_all(message, ("slab", "row"), 0, 0, tiled=True, axis_index_groups=groups)


def from_next(value, turn):
    pairs = [
        ((s + 1) * NROW + (r + turn) % NROW, s * NROW + r)
        for s in range(NSLAB - 1)
        for r in range(NROW)
    ]
    return lax.ppermute(value, ("slab", "row"), pairs)


def body(right_sides, front_tiles, tile_rows, tile_cols, section_blocks, plane_map, interface_coef):
    slab = lax.axis_index("slab").astype(jnp.int32)
    row = lax.axis_index("row").astype(jnp.int32)
    col = lax.axis_index("col").astype(jnp.int32)
    slab = slab.reshape(1)
    row = row.reshape(1)
    col = col.reshape(1)
    lst, pack = helper(col, tile_rows, tile_cols, plane_map, interface_coef)
    packs = [from_next(pack, d) for d in range(NROW)]
    coef_next = packs[0][1:2]
    maps_next = jnp.concatenate([p[0:1] for p in packs], axis=0).astype(jnp.int32)

    copies, rhs_target = prepare(right_sides, section_blocks, slab)
    partner = jnp.arange(PRT * B, dtype=jnp.int32)
    hots = (partner[None, :, None] == maps_next[:, None, :]).astype(BF)
    hot_next = (maps_next[0][:, None] == partner[None, :]).astype(BF)

    start = gather(copies)
    tiles = load_tiles(front_tiles[0], start[0])
    start, hots, hot_next, coef_next, rhs_target, lst, tiles = lax.optimization_barrier(
        (start, hots, hot_next, coef_next, rhs_target, lst, tiles)
    )
    acc, tiles, msg = first_apply(lst, row, start, hots, front_tiles[0], tiles)
    pairs = []
    for step in range(2 * NSLAB - 2):
        if step < NSLAB - 1:
            rcv = exchange(msg, step)
            value = combine(down_kernel, rcv, (rhs_target, interface_coef), TGT, "down")
        else:
            rcv = exchange(msg, 2 * NSLAB - 3 - step)
            value = combine(up_kernel, rcv, (coef_next, hot_next), PRT, "up")
        pairs.append(gather(value))
        if step < len(ORDER):
            which = TAB if step < NSLAB - 1 else LA
            acc, msg = step_apply(lst, slab, row, which, pairs, start, hots, tiles, acc, step)
    msg = last_apply(lst, slab, tiles, start, pairs, acc)
    return finish(section_blocks, lax.all_to_all(msg, "row", 0, 0, tiled=True))


def solution(mesh):
    placed = (
        P("slab", None, ("col", "row")),
        P("slab", ("col", "row"), None, None),
        P("slab", ("col", "row")),
        P("slab", ("col", "row")),
        P("slab"),
        P("slab", ("col", "row")),
        P("slab", ("col", "row")),
    )
    return jax.shard_map(
        body, mesh=mesh, in_specs=placed, out_specs=P("slab", None, ("col", "row")), check_vma=False
    )
```

```python
import functools

import jax
import jax.numpy as jnp
from jax import lax
from jax.experimental import pallas as pl
from jax.experimental.pallas import tpu as pltpu
from jax.sharding import PartitionSpec as P


B = 128
BLK = 8
NROW = 4
NCOL = 16
NSLAB = 4
W = 32
NT = 128
UNROLL = 8
TGT = 2
PRT = 4
BF = jnp.bfloat16
F32 = jnp.float32


def smem():
    return pl.BlockSpec(memory_space=pltpu.SMEM)


def vmem():
    return pl.BlockSpec(memory_space=pltpu.VMEM)


PARAMS = pltpu.CompilerParams(vmem_limit_bytes=24 * 2**20)
ACC = (NROW * BLK + 1, W, B)
LISTS = 9
V0AB, V0C, TC, TAB, LA, LBC = 0, 1, 2, 3, 5, 7
CHUNK = 3
ORDER = (1, 2, 3, 2, 1)
HALF = NCOL // 2


def shr(x, n):
    return lax.shift_right_logical(x, jnp.int32(n))


def product(v, tile):
    return lax.dot_general(v, tile, (((1,), (1,)), ((), ())), preferred_element_type=F32)


def picked(side, own_ref, other_ref, at):
    return jnp.where(side == 0, own_ref[at], other_ref[at])


def helper_kernel(
    col_index, rows_hbm, cols_hbm, map_hbm, coef_hbm, out_ref, pack_ref,
    rows_ref, cols_ref, map_ref, coef_ref, sems,
):
    ins = (rows_hbm, cols_hbm, map_hbm, coef_hbm)
    copies = [
        pltpu.make_async_copy(src, dst, sems.at[k])
        for k, (src, dst) in enumerate(zip(ins, (rows_ref, cols_ref, map_ref, coef_ref)))
    ]
    for copy in copies:
        copy.start()
    for copy in copies:
        copy.wait()
    pack_ref[0:1, :] = map_ref[...].astype(F32)
    pack_ref[1:2, :] = coef_ref[...]
    lane = lax.broadcasted_iota(jnp.int32, (1, NT), 1)
    down = lax.broadcasted_iota(jnp.int32, (NT, NT), 0)
    across = lax.broadcasted_iota(jnp.int32, (NT, NT), 1)
    before = jnp.where(down < across, 1.0, 0.0).astype(BF)
    row = rows_ref[...] - col_index[0] * (NROW * BLK)
    col = cols_ref[...]
    part = shr(col, 5)
    half = shr(part, 1)
    side = (part & 1) ^ (col_index[0] & 1)
    blk = col & (BLK - 1)
    out = row & (BLK - 1)
    early = out < PRT
    target = blk < TGT
    low = blk < PRT
    own = side == 0
    other = side == 1
    member = (
        (BLK, early),
        (BLK, out >= PRT),
        (TGT, target & (out >= PRT)),
        (TGT, target & early & own),
        (TGT, target & early & other),
        (PRT, low & (out < TGT) & own),
        (PRT, low & (out < TGT) & other),
        (PRT, low & (out >= TGT) & own),
        (PRT, low & (out >= TGT) & other),
    )
    sizes = jnp.zeros((1, NT), jnp.int32)
    for k, (width, belongs) in enumerate(member):
        one = jnp.where(belongs, 1.0, 0.0)
        count = jnp.sum(one, axis=1, keepdims=True).astype(jnp.int32)
        rank = jnp.dot(
            jnp.broadcast_to(one, (8, NT)).astype(BF), before, preferred_element_type=F32
        )[0:1].astype(jnp.int32)
        rank = jnp.where(belongs, rank, -1)
        place = jnp.where(jnp.broadcast_to(rank, (NT, NT)) == down, 1.0, 0.0).astype(BF)
        upper = half * width + blk + side * 64
        digits = jnp.concatenate(
            [x.astype(F32) for x in (lane, row, upper, upper, upper, upper, upper, upper)], axis=0
        ).astype(BF)
        moved = lax.dot_general(
            digits, place, (((1,), (1,)), ((), ())), preferred_element_type=F32
        ).astype(jnp.int32)
        entry = moved[0:1] + moved[1:2] * NT + moved[2:3] * 8192
        out_ref[k : k + 1, :] = jnp.where(lane < count, entry, NROW * BLK * NT)
        sizes = jnp.where(lane == k, shr(count + UNROLL - 1, 3), sizes)
    for k in range(LISTS, 16):
        out_ref[k : k + 1, :] = sizes


def helper(col_index, tile_rows, tile_cols, plane_map, interface_coef):
    ins = (tile_rows, tile_cols, plane_map, interface_coef)
    return pl.pallas_call(
        helper_kernel,
        out_shape=(
            jax.ShapeDtypeStruct((16, NT), jnp.int32),
            jax.ShapeDtypeStruct((2, TGT * B), F32),
        ),
        in_specs=[smem()] + [pl.BlockSpec(memory_space=pltpu.HBM)] * 4,
        out_specs=(vmem(), vmem()),
        scratch_shapes=[pltpu.VMEM(x.shape, x.dtype) for x in ins] + [pltpu.SemaphoreType.DMA((4,))],
        compiler_params=PARAMS,
        name="helper",
    )(col_index, *[pltpu.with_memory_space_constraint(x, pltpu.HBM) for x in ins])


def load_kernel(tiles_hbm, own_ref, tiles_ref, sem):
    copy = pltpu.make_async_copy(tiles_hbm, tiles_ref, sem)
    copy.start()
    copy.wait()


def load_tiles(tiles, own):
    return pl.pallas_call(
        load_kernel,
        out_shape=jax.ShapeDtypeStruct(tiles.shape, BF),
        in_specs=[pl.BlockSpec(memory_space=pltpu.HBM), vmem()],
        out_specs=vmem(),
        scratch_shapes=[pltpu.SemaphoreType.DMA],
        compiler_params=PARAMS,
        name="load",
    )(pltpu.with_memory_space_constraint(tiles, pltpu.HBM), own)


def apply_group(lst, which, g, sources, tiles_ref, acc):
    rows, done = [], []
    for u in range(UNROLL):
        e = lst[which, g * UNROLL + u]
        at = shr(e, 13) & 63
        v = sources[0][at] if len(sources) == 1 else picked(shr(e, 19), *sources, at)
        rows.append(shr(e, 7) & 63)
        done.append(product(v, tiles_ref[e & 127]))
    for r, d in zip(rows, done):
        acc[r] += d


def apply_list(lst, which, sources, tiles_ref, acc, low=0, most=NT):
    def group(g, _):
        apply_group(lst, which, g, sources, tiles_ref, acc)
        return 0

    groups = lst[LISTS, which]
    lax.fori_loop(low, jnp.minimum(groups, low + most), group, 0)


def late_start(slab, step):
    used = jnp.int32(step)
    for j in range(step):
        busy = slab[0] == ORDER[j]
        if 0 < j < NSLAB:
            busy = busy | (slab[0] == ORDER[j - 1])
        used = used - jnp.where(busy, jnp.int32(1), jnp.int32(0))
    return used * CHUNK


def write_down(acc, row, hot_ref, msg_ref):
    for d in range(NROW):
        r = (row[0] + d) & (NROW - 1)
        values = jnp.concatenate([acc[r * BLK + b].astype(BF) for b in range(PRT)], axis=1)
        part = jnp.dot(values, hot_ref[d], preferred_element_type=F32).astype(BF)
        for b in range(TGT):
            for s in range(2):
                msg_ref[s * NROW + r, b] = part[:, b * B : (b + 1) * B]


def write_up(acc, msg_ref):
    for r in range(NROW):
        for b in range(TGT):
            part = acc[r * BLK + b].astype(BF)
            for s in range(2):
                msg_ref[s * NROW + r, b] = part


MESSAGE = jax.ShapeDtypeStruct((2 * NROW, TGT, W, B), BF)


def first_kernel(lst, row, own_ref, other_ref, hot_ref, tiles_ref, acc, msg_ref):
    acc[...] = jnp.zeros(ACC, F32)
    apply_list(lst, V0AB, (own_ref, other_ref), tiles_ref, acc)
    write_down(acc, row, hot_ref, msg_ref)


def first_apply(lst, row, pair, hots, tiles):
    return pl.pallas_call(
        first_kernel,
        out_shape=(jax.ShapeDtypeStruct(ACC, F32), MESSAGE),
        in_specs=[smem(), smem()] + [vmem()] * 4,
        out_specs=(vmem(), vmem()),
        compiler_params=PARAMS,
        name="first",
    )(lst, row, *pair, hots, tiles)


def own_kernel(lst, slab, own_ref, own0, other0, tiles_ref, *refs, which, step):
    before, acc = refs[:-2], refs[-1]
    active = slab[0] == ORDER[step]
    after = slab[0] == ORDER[step - 1] if before else slab[0] < 0

    @pl.when(active)
    def _():
        apply_list(lst, which, (own_ref,), tiles_ref, acc)

    if before:
        @pl.when(after)
        def _():
            apply_list(lst, TC, before, tiles_ref, acc)

    @pl.when(jnp.logical_not(active | after))
    def _():
        apply_list(lst, V0C, (own0, other0), tiles_ref, acc, late_start(slab, step), CHUNK)


def own_apply(lst, slab, which, own, before, first_pair, tiles, acc, step):
    ins = (own, *first_pair, tiles, *before, acc)
    return pl.pallas_call(
        functools.partial(own_kernel, which=which, step=step),
        out_shape=jax.ShapeDtypeStruct(ACC, F32),
        in_specs=[smem(), smem()] + [vmem()] * len(ins),
        out_specs=vmem(),
        input_output_aliases={1 + len(ins): 0},
        compiler_params=PARAMS,
        name="own",
    )(lst, slab, *ins)


def other_kernel(lst, slab, row, other_ref, hot_ref, tiles_ref, acc_in, acc, msg_ref, *, which, step):
    @pl.when(slab[0] == ORDER[step])
    def _():
        apply_list(lst, which + 1, (other_ref,), tiles_ref, acc)

    if step + 1 < len(ORDER) and ORDER[step] < ORDER[step + 1]:
        write_down(acc, row, hot_ref, msg_ref)
    else:
        write_up(acc, msg_ref)


def other_apply(lst, slab, row, which, other, hots, tiles, acc, step):
    return pl.pallas_call(
        functools.partial(other_kernel, which=which, step=step),
        out_shape=(jax.ShapeDtypeStruct(ACC, F32), MESSAGE),
        in_specs=[smem(), smem(), smem()] + [vmem()] * 4,
        out_specs=(vmem(), vmem()),
        input_output_aliases={6: 0},
        compiler_params=PARAMS,
        name="other",
    )(lst, slab, row, other, hots, tiles, acc)


def step_apply(lst, slab, row, which, pairs, first_pair, hots, tiles, acc, step):
    own, other = pairs[-1]
    before = pairs[-2] if 0 < step < NSLAB else ()
    acc = own_apply(lst, slab, which, own, before, first_pair, tiles, acc, step)
    return other_apply(lst, slab, row, which, other, hots, tiles, acc, step)


def last_own_kernel(lst, slab, tiles_ref, own0, other0, *refs):
    gathered, acc = refs[:5], refs[6]
    for s in range(NSLAB - 1):
        at = 2 * (NSLAB - 2 - s)

        @pl.when(slab[0] == s)
        def _(s=s, at=at):
            if s == 0:
                apply_list(lst, LA, gathered[at : at + 1], tiles_ref, acc)
            apply_list(lst, LBC, gathered[at : at + 1], tiles_ref, acc)
            if s > 0:
                apply_list(lst, LBC + 1, gathered[at + 1 : at + 2], tiles_ref, acc)

    apply_list(lst, V0C, (own0, other0), tiles_ref, acc, late_start(slab, len(ORDER)))


def last_other_kernel(lst, slab, tiles_ref, other_ref, acc_in, acc, msg_ref):
    @pl.when(slab[0] == 0)
    def _():
        apply_list(lst, LA + 1, (other_ref,), tiles_ref, acc)
        apply_list(lst, LBC + 1, (other_ref,), tiles_ref, acc)

    for r in range(NROW):
        for b in range(BLK):
            msg_ref[r, b] = acc[r * BLK + b].astype(BF)


def last_apply(lst, slab, tiles, first_pair, pairs, acc):
    flat = [ref for pair in pairs[NSLAB - 1 :] for ref in pair]
    whole = jax.ShapeDtypeStruct(ACC, F32)
    acc = pl.pallas_call(
        last_own_kernel,
        out_shape=whole,
        in_specs=[smem(), smem()] + [vmem()] * 9,
        out_specs=vmem(),
        input_output_aliases={10: 0},
        compiler_params=PARAMS,
        name="last_own",
    )(lst, slab, tiles, *first_pair, *flat[:-1], acc)
    return pl.pallas_call(
        last_other_kernel,
        out_shape=(whole, jax.ShapeDtypeStruct((NROW, BLK, W, B), BF)),
        in_specs=[smem(), smem()] + [vmem()] * 3,
        out_specs=(vmem(), vmem()),
        input_output_aliases={4: 0},
        compiler_params=PARAMS,
        name="last_other",
    )(lst, slab, tiles, flat[-1], acc)[1]


def split(x):
    high = x.astype(BF)
    rest = x - high.astype(F32)
    return jnp.concatenate([high, rest.astype(BF)], axis=0)


def row_total(rcv_ref, place, b):
    part = rcv_ref[place * NROW, b].astype(F32)
    for r in range(1, NROW):
        part = part + rcv_ref[place * NROW + r, b].astype(F32)
    return part


def down_kernel(rcv_ref, rhs_ref, coef_ref, out_ref):
    for b in range(TGT):
        pulled = row_total(rcv_ref, 0, b) * coef_ref[:, b * B : (b + 1) * B]
        value = (rhs_ref[b] - pulled).astype(BF)
        for z in range(HALF):
            out_ref[z, b] = value


def up_kernel(rcv_ref, coef_ref, hot_ref, out_ref):
    values = jnp.concatenate(
        [
            split(row_total(rcv_ref, 1, b) * coef_ref[:, b * B : (b + 1) * B])
            for b in range(TGT)
        ],
        axis=1,
    )
    total = jnp.dot(values, hot_ref[...], preferred_element_type=F32)
    lifted = -(total[:W] + total[W:])
    for b in range(PRT):
        value = lifted[:, b * B : (b + 1) * B].astype(BF)
        for z in range(HALF):
            out_ref[z, b] = value


def combine(kernel, received, others, blocks):
    return pl.pallas_call(
        kernel,
        out_shape=jax.ShapeDtypeStruct((HALF, blocks, W, B), BF),
        in_specs=[vmem()] * (1 + len(others)),
        out_specs=vmem(),
        compiler_params=PARAMS,
    )(received, *others)


def prepare_kernel(count, slab, rhs_hbm, out_ref, target_ref, rhs_ref, sems):
    wide = 2 * B
    copies = [
        pltpu.make_async_copy(
            rhs_hbm.at[0, :, pl.ds(k * wide, wide)], rhs_ref.at[k], sems.at[k]
        )
        for k in range(BLK // 2)
    ]
    for copy in copies:
        copy.start()
    for b in range(BLK):
        if b % 2 == 0:
            copies[b // 2].wait()
        value = rhs_ref[b // 2, :, b % 2 * B : (b % 2 + 1) * B]
        if b < TGT:
            target_ref[b] = value
            value = jnp.where(slab[0] == 0, value, 0.0)
        value = jnp.where(b < count[0], value, 0.0).astype(BF)
        for z in range(HALF):
            out_ref[z, b] = value


def prepare(right_sides, section_blocks, slab):
    return pl.pallas_call(
        prepare_kernel,
        out_shape=(
            jax.ShapeDtypeStruct((HALF, BLK, W, B), BF),
            jax.ShapeDtypeStruct((TGT, W, B), F32),
        ),
        in_specs=[smem(), smem(), pl.BlockSpec(memory_space=pltpu.HBM)],
        out_specs=(vmem(), vmem()),
        scratch_shapes=[
            pltpu.VMEM((BLK // 2, W, 2 * B), F32),
            pltpu.SemaphoreType.DMA((BLK // 2,)),
        ],
        compiler_params=PARAMS,
        name="prepare",
    )(section_blocks, slab, pltpu.with_memory_space_constraint(right_sides, pltpu.HBM))


def finish_kernel(count, parts_ref, out_ref):
    for b in range(BLK):
        total = parts_ref[0, b].astype(F32)
        for r in range(1, NROW):
            total = total + parts_ref[r, b].astype(F32)
        out_ref[0, :, b * B : (b + 1) * B] = jnp.where(b < count[0], total, 0.0)


def finish(section_blocks, parts):
    return pl.pallas_call(
        finish_kernel,
        out_shape=jax.ShapeDtypeStruct((1, W, BLK * B), F32),
        in_specs=[smem(), vmem()],
        out_specs=vmem(),
        compiler_params=PARAMS,
        name="finish",
    )(section_blocks, parts)


Z_GROUPS = [[2 * z + k for z in range(HALF)] for k in range(2)]


def gather(copies):
    own = lax.all_to_all(copies, "col", 0, 0, tiled=True, axis_index_groups=Z_GROUPS)
    own = own.reshape(HALF * copies.shape[1], W, B)
    return own, lax.ppermute(own, "col", [(c, c ^ 1) for c in range(NCOL)])


def exchange(message, low):
    groups = [
        [(s + k) % NSLAB * NROW + r for k in range(2) for r in range(NROW)]
        for s in (low, low + 2)
    ]
    return lax.all_to_all(message, ("slab", "row"), 0, 0, tiled=True, axis_index_groups=groups)


def from_next(value, turn):
    pairs = [
        ((s + 1) * NROW + (r + turn) % NROW, s * NROW + r)
        for s in range(NSLAB - 1)
        for r in range(NROW)
    ]
    return lax.ppermute(value, ("slab", "row"), pairs)


def body(right_sides, front_tiles, tile_rows, tile_cols, section_blocks, plane_map, interface_coef):
    slab = lax.axis_index("slab").astype(jnp.int32)
    row = lax.axis_index("row").astype(jnp.int32)
    col = lax.axis_index("col").astype(jnp.int32)
    slab = slab.reshape(1)
    row = row.reshape(1)
    col = col.reshape(1)
    others = [from_next(plane_map, d) for d in range(1, NROW)]
    lst, pack = helper(col, tile_rows, tile_cols, plane_map, interface_coef)
    pack_next = from_next(pack, 0)
    coef_next = pack_next[1:2]
    maps_next = jnp.concatenate([pack_next[0:1].astype(jnp.int32)] + others, axis=0)

    copies, rhs_target = prepare(right_sides, section_blocks, slab)
    partner = jnp.arange(PRT * B, dtype=jnp.int32)
    hots = (partner[None, :, None] == maps_next[:, None, :]).astype(BF)
    hot_next = (maps_next[0][:, None] == partner[None, :]).astype(BF)

    start = gather(copies)
    tiles = load_tiles(front_tiles[0], start[0])
    start, hots, hot_next, coef_next, rhs_target, lst, tiles = lax.optimization_barrier(
        (start, hots, hot_next, coef_next, rhs_target, lst, tiles)
    )
    acc, msg = first_apply(lst, row, start, hots, tiles)
    pairs = []
    for step in range(2 * NSLAB - 2):
        if step < NSLAB - 1:
            rcv = exchange(msg, step)
            value = combine(down_kernel, rcv, (rhs_target, interface_coef), TGT)
        else:
            rcv = exchange(msg, 2 * NSLAB - 3 - step)
            value = combine(up_kernel, rcv, (coef_next, hot_next), PRT)
        pairs.append(gather(value))
        if step < len(ORDER):
            which = TAB if step < NSLAB - 1 else LA
            acc, msg = step_apply(lst, slab, row, which, pairs, start, hots, tiles, acc, step)
    msg = last_apply(lst, slab, tiles, start, pairs, acc)
    return finish(section_blocks, lax.all_to_all(msg, "row", 0, 0, tiled=True))


def solution(mesh):
    placed = (
        P("slab", None, ("col", "row")),
        P("slab", ("col", "row"), None, None),
        P("slab", ("col", "row")),
        P("slab", ("col", "row")),
        P("slab"),
        P("slab", ("col", "row")),
        P("slab", ("col", "row")),
    )
    return jax.shard_map(
        body, mesh=mesh, in_specs=placed, out_specs=P("slab", None, ("col", "row")), check_vma=False
    )
```

```python
import functools

import jax
import jax.numpy as jnp
from jax import lax
from jax.experimental import pallas as pl
from jax.experimental.pallas import tpu as pltpu
from jax.sharding import PartitionSpec as P


B = 128
BLK = 8
NROW = 4
NCOL = 16
NSLAB = 4
W = 32
NT = 128
UNROLL = 8
TGT = 2
PRT = 4
BF = jnp.bfloat16
F32 = jnp.float32


def smem():
    return pl.BlockSpec(memory_space=pltpu.SMEM)


def vmem():
    return pl.BlockSpec(memory_space=pltpu.VMEM)


PARAMS = pltpu.CompilerParams(vmem_limit_bytes=24 * 2**20)
ACC = (NROW * BLK + 1, W, B)
LISTS = 9
V0AB, V0C, TC, TAB, LA, LBC = 0, 1, 2, 3, 5, 7
CHUNK = 3
EXTRA = 2
ORDER = (1, 2, 3, 2, 1)
HALF = NCOL // 2


def shr(x, n):
    return lax.shift_right_logical(x, jnp.int32(n))


def product(v, tile):
    return lax.dot_general(v, tile, (((1,), (1,)), ((), ())), preferred_element_type=F32)


def picked(side, own_ref, other_ref, at):
    return jnp.where(side == 0, own_ref[at], other_ref[at])


def helper_kernel(col_index, rows_hbm, cols_hbm, out_ref, rows_ref, cols_ref, sems):
    copies = [
        pltpu.make_async_copy(rows_hbm, rows_ref, sems.at[0]),
        pltpu.make_async_copy(cols_hbm, cols_ref, sems.at[1]),
    ]
    for copy in copies:
        copy.start()
    for copy in copies:
        copy.wait()
    lane = lax.broadcasted_iota(jnp.int32, (1, NT), 1)
    down = lax.broadcasted_iota(jnp.int32, (NT, NT), 0)
    across = lax.broadcasted_iota(jnp.int32, (NT, NT), 1)
    before = jnp.where(down < across, 1.0, 0.0).astype(BF)
    row = rows_ref[...] - col_index[0] * (NROW * BLK)
    col = cols_ref[...]
    part = shr(col, 5)
    half = shr(part, 1)
    side = (part & 1) ^ (col_index[0] & 1)
    blk = col & (BLK - 1)
    out = row & (BLK - 1)
    early = out < PRT
    target = blk < TGT
    low = blk < PRT
    own = side == 0
    other = side == 1
    member = (
        (BLK, early),
        (BLK, out >= PRT),
        (TGT, target & (out >= PRT)),
        (TGT, target & early & own),
        (TGT, target & early & other),
        (PRT, low & (out < TGT) & own),
        (PRT, low & (out < TGT) & other),
        (PRT, low & (out >= TGT) & own),
        (PRT, low & (out >= TGT) & other),
    )
    sizes = jnp.zeros((1, NT), jnp.int32)
    for k, (width, belongs) in enumerate(member):
        one = jnp.where(belongs, 1.0, 0.0)
        count = jnp.sum(one, axis=1, keepdims=True).astype(jnp.int32)
        rank = jnp.dot(
            jnp.broadcast_to(one, (8, NT)).astype(BF), before, preferred_element_type=F32
        )[0:1].astype(jnp.int32)
        rank = jnp.where(belongs, rank, -1)
        place = jnp.where(jnp.broadcast_to(rank, (NT, NT)) == down, 1.0, 0.0).astype(BF)
        upper = half * width + blk + side * 64
        digits = jnp.concatenate(
            [x.astype(F32) for x in (lane, row, upper, upper, upper, upper, upper, upper)], axis=0
        ).astype(BF)
        moved = lax.dot_general(
            digits, place, (((1,), (1,)), ((), ())), preferred_element_type=F32
        ).astype(jnp.int32)
        entry = moved[0:1] + moved[1:2] * NT + moved[2:3] * 8192
        out_ref[k : k + 1, :] = jnp.where(lane < count, entry, NROW * BLK * NT)
        sizes = jnp.where(lane == k, shr(count + UNROLL - 1, 3), sizes)
    for k in range(LISTS, 16):
        out_ref[k : k + 1, :] = sizes


def helper(col_index, tile_rows, tile_cols):
    ins = (tile_rows, tile_cols)
    return pl.pallas_call(
        helper_kernel,
        out_shape=jax.ShapeDtypeStruct((16, NT), jnp.int32),
        in_specs=[smem()] + [pl.BlockSpec(memory_space=pltpu.HBM)] * 2,
        out_specs=vmem(),
        scratch_shapes=[pltpu.VMEM(x.shape, x.dtype) for x in ins] + [pltpu.SemaphoreType.DMA((2,))],
        compiler_params=PARAMS,
        name="helper",
    )(col_index, *[pltpu.with_memory_space_constraint(x, pltpu.HBM) for x in ins])


def load_kernel(tiles_hbm, own_ref, tiles_ref, sem):
    copy = pltpu.make_async_copy(tiles_hbm, tiles_ref, sem)
    copy.start()
    copy.wait()


def load_tiles(tiles, own):
    return pl.pallas_call(
        load_kernel,
        out_shape=jax.ShapeDtypeStruct(tiles.shape, BF),
        in_specs=[pl.BlockSpec(memory_space=pltpu.HBM), vmem()],
        out_specs=vmem(),
        scratch_shapes=[pltpu.SemaphoreType.DMA],
        compiler_params=PARAMS,
        name="load",
    )(pltpu.with_memory_space_constraint(tiles, pltpu.HBM), own)


def apply_group(lst, which, g, sources, tiles_ref, acc):
    rows, done = [], []
    for u in range(UNROLL):
        e = lst[which, g * UNROLL + u]
        at = shr(e, 13) & 63
        v = sources[0][at] if len(sources) == 1 else picked(shr(e, 19), *sources, at)
        rows.append(shr(e, 7) & 63)
        done.append(product(v, tiles_ref[e & 127]))
    for r, d in zip(rows, done):
        acc[r] += d


def apply_list(lst, which, sources, tiles_ref, acc, low=0, most=NT):
    def group(g, _):
        apply_group(lst, which, g, sources, tiles_ref, acc)
        return 0

    groups = lst[LISTS, which]
    lax.fori_loop(low, jnp.minimum(groups, low + most), group, 0)


def late_start(slab, step):
    used = jnp.int32(step)
    for j in range(step):
        busy = slab[0] == ORDER[j]
        if 0 < j < NSLAB:
            busy = busy | (slab[0] == ORDER[j - 1])
        used = used - jnp.where(busy, jnp.int32(1), jnp.int32(0))
    return used * (CHUNK + EXTRA)


def write_down(acc, row, hot_ref, msg_ref):
    for d in range(NROW):
        r = (row[0] + d) & (NROW - 1)
        values = jnp.concatenate([acc[r * BLK + b].astype(BF) for b in range(PRT)], axis=1)
        part = jnp.dot(values, hot_ref[d], preferred_element_type=F32).astype(BF)
        for b in range(TGT):
            for s in range(2):
                msg_ref[s * NROW + r, b] = part[:, b * B : (b + 1) * B]


def write_up(acc, msg_ref):
    for r in range(NROW):
        for b in range(TGT):
            part = acc[r * BLK + b].astype(BF)
            for s in range(2):
                msg_ref[s * NROW + r, b] = part


MESSAGE = jax.ShapeDtypeStruct((2 * NROW, TGT, W, B), BF)


def first_kernel(lst, row, own_ref, other_ref, hot_ref, tiles_ref, acc, msg_ref):
    acc[...] = jnp.zeros(ACC, F32)
    apply_list(lst, V0AB, (own_ref, other_ref), tiles_ref, acc)
    write_down(acc, row, hot_ref, msg_ref)


def first_apply(lst, row, pair, hots, tiles):
    return pl.pallas_call(
        first_kernel,
        out_shape=(jax.ShapeDtypeStruct(ACC, F32), MESSAGE),
        in_specs=[smem(), smem()] + [vmem()] * 4,
        out_specs=(vmem(), vmem()),
        compiler_params=PARAMS,
        name="first",
    )(lst, row, *pair, hots, tiles)


def own_kernel(lst, slab, own_ref, own0, other0, tiles_ref, *refs, which, step):
    before, acc = refs[:-2], refs[-1]
    active = slab[0] == ORDER[step]
    after = slab[0] == ORDER[step - 1] if before else slab[0] < 0

    @pl.when(active)
    def _():
        apply_list(lst, which, (own_ref,), tiles_ref, acc)

    if before:
        @pl.when(after)
        def _():
            apply_list(lst, TC, before, tiles_ref, acc)

    @pl.when(jnp.logical_not(active | after))
    def _():
        apply_list(lst, V0C, (own0, other0), tiles_ref, acc, late_start(slab, step), CHUNK)


def own_apply(lst, slab, which, own, before, first_pair, tiles, acc, step):
    ins = (own, *first_pair, tiles, *before, acc)
    return pl.pallas_call(
        functools.partial(own_kernel, which=which, step=step),
        out_shape=jax.ShapeDtypeStruct(ACC, F32),
        in_specs=[smem(), smem()] + [vmem()] * len(ins),
        out_specs=vmem(),
        input_output_aliases={1 + len(ins): 0},
        compiler_params=PARAMS,
        name="own",
    )(lst, slab, *ins)


def other_kernel(
    lst, slab, row, other_ref, own0, other0, hot_ref, tiles_ref, acc_in, acc, msg_ref, *, which, step
):
    active = slab[0] == ORDER[step]
    after = slab[0] == ORDER[step - 1] if 0 < step < NSLAB else slab[0] < 0

    @pl.when(active)
    def _():
        apply_list(lst, which + 1, (other_ref,), tiles_ref, acc)

    @pl.when(jnp.logical_not(active | after))
    def _():
        apply_list(lst, V0C, (own0, other0), tiles_ref, acc, late_start(slab, step) + CHUNK, EXTRA)

    if step + 1 < len(ORDER) and ORDER[step] < ORDER[step + 1]:
        write_down(acc, row, hot_ref, msg_ref)
    else:
        write_up(acc, msg_ref)


def other_apply(lst, slab, row, which, other, first_pair, hots, tiles, acc, step):
    return pl.pallas_call(
        functools.partial(other_kernel, which=which, step=step),
        out_shape=(jax.ShapeDtypeStruct(ACC, F32), MESSAGE),
        in_specs=[smem(), smem(), smem()] + [vmem()] * 6,
        out_specs=(vmem(), vmem()),
        input_output_aliases={8: 0},
        compiler_params=PARAMS,
        name="other",
    )(lst, slab, row, other, *first_pair, hots, tiles, acc)


def step_apply(lst, slab, row, which, pairs, first_pair, hots, tiles, acc, step):
    own, other = pairs[-1]
    before = pairs[-2] if 0 < step < NSLAB else ()
    acc = own_apply(lst, slab, which, own, before, first_pair, tiles, acc, step)
    return other_apply(lst, slab, row, which, other, first_pair, hots, tiles, acc, step)


def last_own_kernel(lst, slab, tiles_ref, own0, other0, *refs):
    gathered, acc = refs[:5], refs[6]
    for s in range(NSLAB - 1):
        at = 2 * (NSLAB - 2 - s)

        @pl.when(slab[0] == s)
        def _(s=s, at=at):
            if s == 0:
                apply_list(lst, LA, gathered[at : at + 1], tiles_ref, acc)
            apply_list(lst, LBC, gathered[at : at + 1], tiles_ref, acc)
            if s > 0:
                apply_list(lst, LBC + 1, gathered[at + 1 : at + 2], tiles_ref, acc)

    apply_list(lst, V0C, (own0, other0), tiles_ref, acc, late_start(slab, len(ORDER)))


def last_other_kernel(lst, slab, tiles_ref, other_ref, acc_in, acc, msg_ref):
    @pl.when(slab[0] == 0)
    def _():
        apply_list(lst, LA + 1, (other_ref,), tiles_ref, acc)
        apply_list(lst, LBC + 1, (other_ref,), tiles_ref, acc)

    for r in range(NROW):
        for b in range(BLK):
            msg_ref[r, b] = acc[r * BLK + b].astype(BF)


def last_apply(lst, slab, tiles, first_pair, pairs, acc):
    flat = [ref for pair in pairs[NSLAB - 1 :] for ref in pair]
    whole = jax.ShapeDtypeStruct(ACC, F32)
    acc = pl.pallas_call(
        last_own_kernel,
        out_shape=whole,
        in_specs=[smem(), smem()] + [vmem()] * 9,
        out_specs=vmem(),
        input_output_aliases={10: 0},
        compiler_params=PARAMS,
        name="last_own",
    )(lst, slab, tiles, *first_pair, *flat[:-1], acc)
    return pl.pallas_call(
        last_other_kernel,
        out_shape=(whole, jax.ShapeDtypeStruct((NROW, BLK, W, B), BF)),
        in_specs=[smem(), smem()] + [vmem()] * 3,
        out_specs=(vmem(), vmem()),
        input_output_aliases={4: 0},
        compiler_params=PARAMS,
        name="last_other",
    )(lst, slab, tiles, flat[-1], acc)[1]


def split(x):
    high = x.astype(BF)
    rest = x - high.astype(F32)
    return jnp.concatenate([high, rest.astype(BF)], axis=0)


def row_total(rcv_ref, place, b):
    part = rcv_ref[place * NROW, b].astype(F32)
    for r in range(1, NROW):
        part = part + rcv_ref[place * NROW + r, b].astype(F32)
    return part


def down_kernel(rcv_ref, rhs_ref, coef_ref, out_ref):
    for b in range(TGT):
        pulled = row_total(rcv_ref, 0, b) * coef_ref[:, b * B : (b + 1) * B]
        value = (rhs_ref[b] - pulled).astype(BF)
        for z in range(HALF):
            out_ref[z, b] = value


def up_kernel(rcv_ref, coef_ref, hot_ref, out_ref):
    values = jnp.concatenate(
        [
            split(row_total(rcv_ref, 1, b) * coef_ref[:, b * B : (b + 1) * B])
            for b in range(TGT)
        ],
        axis=1,
    )
    total = jnp.dot(values, hot_ref[...], preferred_element_type=F32)
    lifted = -(total[:W] + total[W:])
    for b in range(PRT):
        value = lifted[:, b * B : (b + 1) * B].astype(BF)
        for z in range(HALF):
            out_ref[z, b] = value


def combine(kernel, received, others, blocks):
    return pl.pallas_call(
        kernel,
        out_shape=jax.ShapeDtypeStruct((HALF, blocks, W, B), BF),
        in_specs=[vmem()] * (1 + len(others)),
        out_specs=vmem(),
        compiler_params=PARAMS,
    )(received, *others)


def prepare_kernel(count, slab, rhs_hbm, out_ref, target_ref, rhs_ref, sems):
    wide = 2 * B
    copies = [
        pltpu.make_async_copy(
            rhs_hbm.at[0, :, pl.ds(k * wide, wide)], rhs_ref.at[k], sems.at[k]
        )
        for k in range(BLK // 2)
    ]
    for copy in copies:
        copy.start()
    for b in range(BLK):
        if b % 2 == 0:
            copies[b // 2].wait()
        value = rhs_ref[b // 2, :, b % 2 * B : (b % 2 + 1) * B]
        if b < TGT:
            target_ref[b] = value
            value = jnp.where(slab[0] == 0, value, 0.0)
        value = jnp.where(b < count[0], value, 0.0).astype(BF)
        for z in range(HALF):
            out_ref[z, b] = value


def prepare(right_sides, section_blocks, slab):
    return pl.pallas_call(
        prepare_kernel,
        out_shape=(
            jax.ShapeDtypeStruct((HALF, BLK, W, B), BF),
            jax.ShapeDtypeStruct((TGT, W, B), F32),
        ),
        in_specs=[smem(), smem(), pl.BlockSpec(memory_space=pltpu.HBM)],
        out_specs=(vmem(), vmem()),
        scratch_shapes=[
            pltpu.VMEM((BLK // 2, W, 2 * B), F32),
            pltpu.SemaphoreType.DMA((BLK // 2,)),
        ],
        compiler_params=PARAMS,
        name="prepare",
    )(section_blocks, slab, pltpu.with_memory_space_constraint(right_sides, pltpu.HBM))


def finish_kernel(count, parts_ref, out_ref):
    for b in range(BLK):
        total = parts_ref[0, b].astype(F32)
        for r in range(1, NROW):
            total = total + parts_ref[r, b].astype(F32)
        out_ref[0, :, b * B : (b + 1) * B] = jnp.where(b < count[0], total, 0.0)


def finish(section_blocks, parts):
    return pl.pallas_call(
        finish_kernel,
        out_shape=jax.ShapeDtypeStruct((1, W, BLK * B), F32),
        in_specs=[smem(), vmem()],
        out_specs=vmem(),
        compiler_params=PARAMS,
        name="finish",
    )(section_blocks, parts)


Z_GROUPS = [[2 * z + k for z in range(HALF)] for k in range(2)]


def gather(copies):
    own = lax.all_to_all(copies, "col", 0, 0, tiled=True, axis_index_groups=Z_GROUPS)
    own = own.reshape(HALF * copies.shape[1], W, B)
    return own, lax.ppermute(own, "col", [(c, c ^ 1) for c in range(NCOL)])


def exchange(message, low):
    groups = [
        [(s + k) % NSLAB * NROW + r for k in range(2) for r in range(NROW)]
        for s in (low, low + 2)
    ]
    return lax.all_to_all(message, ("slab", "row"), 0, 0, tiled=True, axis_index_groups=groups)


def from_next(value, turn):
    pairs = [
        ((s + 1) * NROW + (r + turn) % NROW, s * NROW + r)
        for s in range(NSLAB - 1)
        for r in range(NROW)
    ]
    return lax.ppermute(value, ("slab", "row"), pairs)


def body(right_sides, front_tiles, tile_rows, tile_cols, section_blocks, plane_map, interface_coef):
    slab = lax.axis_index("slab").astype(jnp.int32)
    row = lax.axis_index("row").astype(jnp.int32)
    col = lax.axis_index("col").astype(jnp.int32)
    slab = slab.reshape(1)
    row = row.reshape(1)
    col = col.reshape(1)
    maps = [from_next(plane_map, d) for d in range(NROW)]
    coef_next = from_next(interface_coef, 0)
    lst = helper(col, tile_rows, tile_cols)
    maps_next = jnp.concatenate(maps, axis=0)

    copies, rhs_target = prepare(right_sides, section_blocks, slab)
    partner = jnp.arange(PRT * B, dtype=jnp.int32)
    hots = (partner[None, :, None] == maps_next[:, None, :]).astype(BF)
    hot_next = (maps_next[0][:, None] == partner[None, :]).astype(BF)

    start = gather(copies)
    tiles = load_tiles(front_tiles[0], start[0])
    start, hots, hot_next, coef_next, rhs_target, lst, tiles = lax.optimization_barrier(
        (start, hots, hot_next, coef_next, rhs_target, lst, tiles)
    )
    acc, msg = first_apply(lst, row, start, hots, tiles)
    pairs = []
    for step in range(2 * NSLAB - 2):
        if step < NSLAB - 1:
            rcv = exchange(msg, step)
            value = combine(down_kernel, rcv, (rhs_target, interface_coef), TGT)
        else:
            rcv = exchange(msg, 2 * NSLAB - 3 - step)
            value = combine(up_kernel, rcv, (coef_next, hot_next), PRT)
        pairs.append(gather(value))
        if step < len(ORDER):
            which = TAB if step < NSLAB - 1 else LA
            acc, msg = step_apply(lst, slab, row, which, pairs, start, hots, tiles, acc, step)
    msg = last_apply(lst, slab, tiles, start, pairs, acc)
    return finish(section_blocks, lax.all_to_all(msg, "row", 0, 0, tiled=True))


def solution(mesh):
    placed = (
        P("slab", None, ("col", "row")),
        P("slab", ("col", "row"), None, None),
        P("slab", ("col", "row")),
        P("slab", ("col", "row")),
        P("slab"),
        P("slab", ("col", "row")),
        P("slab", ("col", "row")),
    )
    return jax.shard_map(
        body, mesh=mesh, in_specs=placed, out_specs=P("slab", None, ("col", "row")), check_vma=False
    )
```

```python
import functools

import jax
import jax.numpy as jnp
from jax import lax
from jax.experimental import pallas as pl
from jax.experimental.pallas import tpu as pltpu
from jax.sharding import PartitionSpec as P


B = 128
BLK = 8
NROW = 4
NCOL = 16
NSLAB = 4
W = 32
NT = 128
UNROLL = 8
TGT = 2
PRT = 4
BF = jnp.bfloat16
F32 = jnp.float32


def smem():
    return pl.BlockSpec(memory_space=pltpu.SMEM)


def vmem():
    return pl.BlockSpec(memory_space=pltpu.VMEM)


PARAMS = pltpu.CompilerParams(vmem_limit_bytes=24 * 2**20)
ACC = (NROW * BLK + 1, W, B)
LISTS = 9
V0AB, V0C, TC, TAB, LA, LBC = 0, 1, 2, 3, 5, 7
CHUNK = 3
ORDER = (1, 2, 3, 2, 1)
HALF = NCOL // 2


def shr(x, n):
    return lax.shift_right_logical(x, jnp.int32(n))


def product(v, tile):
    return lax.dot_general(v, tile, (((1,), (1,)), ((), ())), preferred_element_type=F32)


def picked(side, own_ref, other_ref, at):
    return jnp.where(side == 0, own_ref[at], other_ref[at])


def helper_kernel(col_index, rows_ref, cols_ref, out_ref):
    lane = lax.broadcasted_iota(jnp.int32, (1, NT), 1)
    down = lax.broadcasted_iota(jnp.int32, (NT, NT), 0)
    across = lax.broadcasted_iota(jnp.int32, (NT, NT), 1)
    before = jnp.where(down < across, 1.0, 0.0).astype(BF)
    row = rows_ref[...] - col_index[0] * (NROW * BLK)
    col = cols_ref[...]
    part = shr(col, 5)
    half = shr(part, 1)
    side = (part & 1) ^ (col_index[0] & 1)
    blk = col & (BLK - 1)
    out = row & (BLK - 1)
    early = out < PRT
    target = blk < TGT
    low = blk < PRT
    own = side == 0
    other = side == 1
    member = (
        (BLK, early),
        (BLK, out >= PRT),
        (TGT, target & (out >= PRT)),
        (TGT, target & early & own),
        (TGT, target & early & other),
        (PRT, low & (out < TGT) & own),
        (PRT, low & (out < TGT) & other),
        (PRT, low & (out >= TGT) & own),
        (PRT, low & (out >= TGT) & other),
    )
    sizes = jnp.zeros((1, NT), jnp.int32)
    for k, (width, belongs) in enumerate(member):
        one = jnp.where(belongs, 1.0, 0.0)
        count = jnp.sum(one, axis=1, keepdims=True).astype(jnp.int32)
        rank = jnp.dot(
            jnp.broadcast_to(one, (8, NT)).astype(BF), before, preferred_element_type=F32
        )[0:1].astype(jnp.int32)
        rank = jnp.where(belongs, rank, -1)
        place = jnp.where(jnp.broadcast_to(rank, (NT, NT)) == down, 1.0, 0.0).astype(BF)
        upper = half * width + blk + side * 64
        digits = jnp.concatenate(
            [x.astype(F32) for x in (lane, row, upper, upper, upper, upper, upper, upper)], axis=0
        ).astype(BF)
        moved = lax.dot_general(
            digits, place, (((1,), (1,)), ((), ())), preferred_element_type=F32
        ).astype(jnp.int32)
        entry = moved[0:1] + moved[1:2] * NT + moved[2:3] * 8192
        out_ref[k : k + 1, :] = jnp.where(lane < count, entry, NROW * BLK * NT)
        sizes = jnp.where(lane == k, shr(count + UNROLL - 1, 3), sizes)
    for k in range(LISTS, 16):
        out_ref[k : k + 1, :] = sizes


def helper(col_index, tile_rows, tile_cols):
    return pl.pallas_call(
        helper_kernel,
        out_shape=jax.ShapeDtypeStruct((16, NT), jnp.int32),
        in_specs=[smem(), vmem(), vmem()],
        out_specs=vmem(),
        compiler_params=PARAMS,
        name="helper",
    )(col_index, tile_rows, tile_cols)


def load_kernel(tiles_hbm, own_ref, tiles_ref, sem):
    copy = pltpu.make_async_copy(tiles_hbm, tiles_ref, sem)
    copy.start()
    copy.wait()


def load_tiles(tiles, own):
    return pl.pallas_call(
        load_kernel,
        out_shape=jax.ShapeDtypeStruct(tiles.shape, BF),
        in_specs=[pl.BlockSpec(memory_space=pltpu.HBM), vmem()],
        out_specs=vmem(),
        scratch_shapes=[pltpu.SemaphoreType.DMA],
        compiler_params=PARAMS,
        name="load",
    )(pltpu.with_memory_space_constraint(tiles, pltpu.HBM), own)


def products(pairs):
    out = []
    for (va, ta), (vb, tb) in zip(pairs[::2], pairs[1::2]):
        both = product(jnp.concatenate([va, vb], axis=0), jnp.concatenate([ta, tb], axis=0))
        out += [both[:W, :B], both[W:, B:]]
    return out


def apply_list(lst, which, sources, tiles_ref, acc, low=0, most=NT):
    def group(g, _):
        rows, done = [], []
        for u in range(UNROLL):
            e = lst[which, g * UNROLL + u]
            at = shr(e, 13) & 63
            v = sources[0][at] if len(sources) == 1 else picked(shr(e, 19), *sources, at)
            rows.append(shr(e, 7) & 63)
            done.append((v, tiles_ref[e & 127]))
        for r, d in zip(rows, products(done)):
            acc[r] += d
        return 0

    groups = lst[LISTS, which]
    lax.fori_loop(low, jnp.minimum(groups, low + most), group, 0)


def late_start(slab, step):
    used = jnp.int32(step)
    for active in ORDER[:step]:
        used = used - jnp.where(slab[0] == active, jnp.int32(1), jnp.int32(0))
    return used * CHUNK


def write_down(acc, row, hot_ref, msg_ref):
    for d in range(NROW):
        r = (row[0] + d) & (NROW - 1)
        values = jnp.concatenate([acc[r * BLK + b].astype(BF) for b in range(PRT)], axis=1)
        part = jnp.dot(values, hot_ref[d], preferred_element_type=F32).astype(BF)
        for b in range(TGT):
            for s in range(2):
                msg_ref[s * NROW + r, b] = part[:, b * B : (b + 1) * B]


def write_up(acc, msg_ref):
    for r in range(NROW):
        for b in range(TGT):
            part = acc[r * BLK + b].astype(BF)
            for s in range(2):
                msg_ref[s * NROW + r, b] = part


MESSAGE = jax.ShapeDtypeStruct((2 * NROW, TGT, W, B), BF)


def first_kernel(lst, row, own_ref, other_ref, hot_ref, tiles_ref, acc, msg_ref):
    acc[...] = jnp.zeros(ACC, F32)
    apply_list(lst, V0AB, (own_ref, other_ref), tiles_ref, acc)
    write_down(acc, row, hot_ref, msg_ref)


def first_apply(lst, row, pair, hots, tiles):
    return pl.pallas_call(
        first_kernel,
        out_shape=(jax.ShapeDtypeStruct(ACC, F32), MESSAGE),
        in_specs=[smem(), smem()] + [vmem()] * 4,
        out_specs=(vmem(), vmem()),
        compiler_params=PARAMS,
        name="first",
    )(lst, row, *pair, hots, tiles)


def own_kernel(lst, slab, own_ref, own0, other0, tiles_ref, acc_in, acc, *, which, step):
    @pl.when(slab[0] == ORDER[step])
    def _():
        apply_list(lst, which, (own_ref,), tiles_ref, acc)

    @pl.when(slab[0] != ORDER[step])
    def _():
        apply_list(lst, V0C, (own0, other0), tiles_ref, acc, late_start(slab, step), CHUNK)


def own_apply(lst, slab, which, own, first_pair, tiles, acc, step):
    return pl.pallas_call(
        functools.partial(own_kernel, which=which, step=step),
        out_shape=jax.ShapeDtypeStruct(ACC, F32),
        in_specs=[smem(), smem()] + [vmem()] * 5,
        out_specs=vmem(),
        input_output_aliases={6: 0},
        compiler_params=PARAMS,
        name="own",
    )(lst, slab, own, *first_pair, tiles, acc)


def other_kernel(lst, slab, row, other_ref, hot_ref, tiles_ref, acc_in, acc, msg_ref, *, which, step):
    @pl.when(slab[0] == ORDER[step])
    def _():
        apply_list(lst, which + 1, (other_ref,), tiles_ref, acc)

    if step + 1 < len(ORDER) and ORDER[step] < ORDER[step + 1]:
        write_down(acc, row, hot_ref, msg_ref)
    else:
        write_up(acc, msg_ref)


def other_apply(lst, slab, row, which, other, hots, tiles, acc, step):
    return pl.pallas_call(
        functools.partial(other_kernel, which=which, step=step),
        out_shape=(jax.ShapeDtypeStruct(ACC, F32), MESSAGE),
        in_specs=[smem(), smem(), smem()] + [vmem()] * 4,
        out_specs=(vmem(), vmem()),
        input_output_aliases={6: 0},
        compiler_params=PARAMS,
        name="other",
    )(lst, slab, row, other, hots, tiles, acc)


def step_apply(lst, slab, row, which, pair, first_pair, hots, tiles, acc, step):
    acc = own_apply(lst, slab, which, pair[0], first_pair, tiles, acc, step)
    return other_apply(lst, slab, row, which, pair[1], hots, tiles, acc, step)


def last_own_kernel(lst, slab, tiles_ref, own0, other0, *refs):
    gathered, acc = refs[:11], refs[12]
    for k, s in enumerate((1, 2, 3, 2, 1, 0)):
        @pl.when(slab[0] == s)
        def _(k=k, s=s):
            if s == 0:
                apply_list(lst, LA, gathered[2 * k : 2 * k + 1], tiles_ref, acc)
            if k < NSLAB - 1:
                apply_list(lst, TC, gathered[2 * k : 2 * k + 2], tiles_ref, acc)
            else:
                apply_list(lst, LBC, gathered[2 * k : 2 * k + 1], tiles_ref, acc)
                if s > 0:
                    apply_list(lst, LBC + 1, gathered[2 * k + 1 : 2 * k + 2], tiles_ref, acc)

    apply_list(lst, V0C, (own0, other0), tiles_ref, acc, late_start(slab, len(ORDER)))


def last_other_kernel(lst, slab, tiles_ref, other_ref, acc_in, acc, msg_ref):
    @pl.when(slab[0] == 0)
    def _():
        apply_list(lst, LA + 1, (other_ref,), tiles_ref, acc)
        apply_list(lst, LBC + 1, (other_ref,), tiles_ref, acc)

    for r in range(NROW):
        for b in range(BLK):
            msg_ref[r, b] = acc[r * BLK + b].astype(BF)


def last_apply(lst, slab, tiles, first_pair, pairs, acc):
    flat = [ref for pair in pairs for ref in pair]
    whole = jax.ShapeDtypeStruct(ACC, F32)
    acc = pl.pallas_call(
        last_own_kernel,
        out_shape=whole,
        in_specs=[smem(), smem()] + [vmem()] * 15,
        out_specs=vmem(),
        input_output_aliases={16: 0},
        compiler_params=PARAMS,
        name="last_own",
    )(lst, slab, tiles, *first_pair, *flat[:-1], acc)
    return pl.pallas_call(
        last_other_kernel,
        out_shape=(whole, jax.ShapeDtypeStruct((NROW, BLK, W, B), BF)),
        in_specs=[smem(), smem()] + [vmem()] * 3,
        out_specs=(vmem(), vmem()),
        input_output_aliases={4: 0},
        compiler_params=PARAMS,
        name="last_other",
    )(lst, slab, tiles, flat[-1], acc)[1]


def split(x):
    high = x.astype(BF)
    rest = x - high.astype(F32)
    return jnp.concatenate([high, rest.astype(BF)], axis=0)


def row_total(rcv_ref, place, b):
    part = rcv_ref[place * NROW, b].astype(F32)
    for r in range(1, NROW):
        part = part + rcv_ref[place * NROW + r, b].astype(F32)
    return part


def down_kernel(rcv_ref, rhs_ref, coef_ref, out_ref):
    for b in range(TGT):
        pulled = row_total(rcv_ref, 0, b) * coef_ref[:, b * B : (b + 1) * B]
        value = (rhs_ref[b] - pulled).astype(BF)
        for z in range(HALF):
            out_ref[z, b] = value


def up_kernel(rcv_ref, coef_ref, hot_ref, out_ref):
    values = jnp.concatenate(
        [
            split(row_total(rcv_ref, 1, b) * coef_ref[:, b * B : (b + 1) * B])
            for b in range(TGT)
        ],
        axis=1,
    )
    total = jnp.dot(values, hot_ref[...], preferred_element_type=F32)
    lifted = -(total[:W] + total[W:])
    for b in range(PRT):
        value = lifted[:, b * B : (b + 1) * B].astype(BF)
        for z in range(HALF):
            out_ref[z, b] = value


def combine(kernel, received, others, blocks):
    return pl.pallas_call(
        kernel,
        out_shape=jax.ShapeDtypeStruct((HALF, blocks, W, B), BF),
        in_specs=[vmem()] * (1 + len(others)),
        out_specs=vmem(),
        compiler_params=PARAMS,
    )(received, *others)


def prepare_kernel(
    count, slab, rhs_hbm, rows_hbm, cols_hbm, map_hbm, coef_hbm,
    out_ref, target_ref, rows_ref, cols_ref, pack_ref,
    rhs_ref, map_ref, coef_ref, sems,
):
    wide = 2 * B
    copies = [
        pltpu.make_async_copy(
            rhs_hbm.at[0, :, pl.ds(k * wide, wide)], rhs_ref.at[k], sems.at[k]
        )
        for k in range(BLK // 2)
    ]
    small = [
        pltpu.make_async_copy(src, dst, sems.at[BLK // 2 + k])
        for k, (src, dst) in enumerate(
            ((rows_hbm, rows_ref), (cols_hbm, cols_ref), (map_hbm, map_ref), (coef_hbm, coef_ref))
        )
    ]
    for copy in copies + small:
        copy.start()
    for b in range(BLK):
        if b % 2 == 0:
            copies[b // 2].wait()
        value = rhs_ref[b // 2, :, b % 2 * B : (b % 2 + 1) * B]
        if b < TGT:
            target_ref[b] = value
            value = jnp.where(slab[0] == 0, value, 0.0)
        value = jnp.where(b < count[0], value, 0.0).astype(BF)
        for z in range(HALF):
            out_ref[z, b] = value
    for copy in small:
        copy.wait()
    pack_ref[0:1, :] = map_ref[...].astype(F32)
    pack_ref[1:2, :] = coef_ref[...]


def prepare(right_sides, section_blocks, slab, tile_rows, tile_cols, plane_map, interface_coef):
    ins = (right_sides, tile_rows, tile_cols, plane_map, interface_coef)
    return pl.pallas_call(
        prepare_kernel,
        out_shape=(
            jax.ShapeDtypeStruct((HALF, BLK, W, B), BF),
            jax.ShapeDtypeStruct((TGT, W, B), F32),
            jax.ShapeDtypeStruct(tile_rows.shape, jnp.int32),
            jax.ShapeDtypeStruct(tile_cols.shape, jnp.int32),
            jax.ShapeDtypeStruct((2, TGT * B), F32),
        ),
        in_specs=[smem(), smem()] + [pl.BlockSpec(memory_space=pltpu.HBM)] * 5,
        out_specs=(vmem(),) * 5,
        scratch_shapes=[
            pltpu.VMEM((BLK // 2, W, 2 * B), F32),
            pltpu.VMEM((1, TGT * B), jnp.int32),
            pltpu.VMEM((1, TGT * B), F32),
            pltpu.SemaphoreType.DMA((BLK // 2 + 4,)),
        ],
        compiler_params=PARAMS,
        name="prepare",
    )(section_blocks, slab, *[pltpu.with_memory_space_constraint(x, pltpu.HBM) for x in ins])


def finish_kernel(count, parts_ref, out_ref):
    for b in range(BLK):
        total = parts_ref[0, b].astype(F32)
        for r in range(1, NROW):
            total = total + parts_ref[r, b].astype(F32)
        out_ref[0, :, b * B : (b + 1) * B] = jnp.where(b < count[0], total, 0.0)


def finish(section_blocks, parts):
    return pl.pallas_call(
        finish_kernel,
        out_shape=jax.ShapeDtypeStruct((1, W, BLK * B), F32),
        in_specs=[smem(), vmem()],
        out_specs=vmem(),
        compiler_params=PARAMS,
        name="finish",
    )(section_blocks, parts)


Z_GROUPS = [[2 * z + k for z in range(HALF)] for k in range(2)]


def gather(copies):
    own = lax.all_to_all(copies, "col", 0, 0, tiled=True, axis_index_groups=Z_GROUPS)
    own = own.reshape(HALF * copies.shape[1], W, B)
    return own, lax.ppermute(own, "col", [(c, c ^ 1) for c in range(NCOL)])


def exchange(message, low):
    groups = [
        [(s + k) % NSLAB * NROW + r for k in range(2) for r in range(NROW)]
        for s in (low, low + 2)
    ]
    return lax.all_to_all(message, ("slab", "row"), 0, 0, tiled=True, axis_index_groups=groups)


def from_next(value, turn):
    pairs = [
        ((s + 1) * NROW + (r + turn) % NROW, s * NROW + r)
        for s in range(NSLAB - 1)
        for r in range(NROW)
    ]
    return lax.ppermute(value, ("slab", "row"), pairs)


def body(right_sides, front_tiles, tile_rows, tile_cols, section_blocks, plane_map, interface_coef):
    slab = lax.axis_index("slab").astype(jnp.int32)
    row = lax.axis_index("row").astype(jnp.int32)
    col = lax.axis_index("col").astype(jnp.int32)
    slab = slab.reshape(1)
    row = row.reshape(1)
    col = col.reshape(1)
    copies, rhs_target, rows, cols, pack = prepare(
        right_sides, section_blocks, slab, tile_rows, tile_cols, plane_map, interface_coef
    )
    packs = [from_next(pack, d) for d in range(NROW)]
    lst = helper(col, rows, cols)
    coef_next = packs[0][1:2]
    maps_next = jnp.concatenate([p[0:1] for p in packs], axis=0).astype(jnp.int32)

    partner = jnp.arange(PRT * B, dtype=jnp.int32)
    hots = (partner[None, :, None] == maps_next[:, None, :]).astype(BF)
    hot_next = (maps_next[0][:, None] == partner[None, :]).astype(BF)

    start = gather(copies)
    tiles = load_tiles(front_tiles[0], start[0])
    start, hots, hot_next, coef_next, rhs_target, lst, tiles = lax.optimization_barrier(
        (start, hots, hot_next, coef_next, rhs_target, lst, tiles)
    )
    acc, msg = first_apply(lst, row, start, hots, tiles)
    pairs = []
    for step in range(2 * NSLAB - 2):
        if step < NSLAB - 1:
            rcv = exchange(msg, step)
            value = combine(down_kernel, rcv, (rhs_target, interface_coef), TGT)
        else:
            rcv = exchange(msg, 2 * NSLAB - 3 - step)
            value = combine(up_kernel, rcv, (coef_next, hot_next), PRT)
        pairs.append(gather(value))
        if step < len(ORDER):
            which = TAB if step < NSLAB - 1 else LA
            acc, msg = step_apply(lst, slab, row, which, pairs[-1], start, hots, tiles, acc, step)
    msg = last_apply(lst, slab, tiles, start, pairs, acc)
    return finish(section_blocks, lax.all_to_all(msg, "row", 0, 0, tiled=True))


def solution(mesh):
    placed = (
        P("slab", None, ("col", "row")),
        P("slab", ("col", "row"), None, None),
        P("slab", ("col", "row")),
        P("slab", ("col", "row")),
        P("slab"),
        P("slab", ("col", "row")),
        P("slab", ("col", "row")),
    )
    return jax.shard_map(
        body, mesh=mesh, in_specs=placed, out_specs=P("slab", None, ("col", "row")), check_vma=False
    )
```

```python
import functools

import jax
import jax.numpy as jnp
from jax import lax
from jax.experimental import pallas as pl
from jax.experimental.pallas import tpu as pltpu
from jax.sharding import PartitionSpec as P


B = 128
BLK = 8
NROW = 4
NCOL = 16
NSLAB = 4
W = 32
NT = 128
UNROLL = 8
TGT = 2
PRT = 4
BF = jnp.bfloat16
F32 = jnp.float32


def smem():
    return pl.BlockSpec(memory_space=pltpu.SMEM)


def vmem():
    return pl.BlockSpec(memory_space=pltpu.VMEM)


PARAMS = pltpu.CompilerParams(vmem_limit_bytes=24 * 2**20)
ACC = (NROW * BLK + 1, W, B)
LISTS = 9
V0AB, V0C, TC, TAB, LA, LBC = 0, 1, 2, 3, 5, 7
CHUNK = 3
ORDER = (1, 2, 3, 2, 1)
HALF = NCOL // 2


def shr(x, n):
    return lax.shift_right_logical(x, jnp.int32(n))


def product(v, tile):
    return lax.dot_general(v, tile, (((1,), (1,)), ((), ())), preferred_element_type=F32)


def picked(side, own_ref, other_ref, at):
    return jnp.where(side == 0, own_ref[at], other_ref[at])


def helper_kernel(col_index, rows_ref, cols_ref, out_ref):
    lane = lax.broadcasted_iota(jnp.int32, (1, NT), 1)
    down = lax.broadcasted_iota(jnp.int32, (NT, NT), 0)
    across = lax.broadcasted_iota(jnp.int32, (NT, NT), 1)
    before = jnp.where(down < across, 1.0, 0.0).astype(BF)
    row = rows_ref[...] - col_index[0] * (NROW * BLK)
    col = cols_ref[...]
    part = shr(col, 5)
    half = shr(part, 1)
    side = (part & 1) ^ (col_index[0] & 1)
    blk = col & (BLK - 1)
    out = row & (BLK - 1)
    early = out < PRT
    target = blk < TGT
    low = blk < PRT
    own = side == 0
    other = side == 1
    member = (
        (BLK, early),
        (BLK, out >= PRT),
        (TGT, target & (out >= PRT)),
        (TGT, target & early & own),
        (TGT, target & early & other),
        (PRT, low & (out < TGT) & own),
        (PRT, low & (out < TGT) & other),
        (PRT, low & (out >= TGT) & own),
        (PRT, low & (out >= TGT) & other),
    )
    sizes = jnp.zeros((1, NT), jnp.int32)
    for k, (width, belongs) in enumerate(member):
        one = jnp.where(belongs, 1.0, 0.0)
        count = jnp.sum(one, axis=1, keepdims=True).astype(jnp.int32)
        rank = jnp.dot(
            jnp.broadcast_to(one, (8, NT)).astype(BF), before, preferred_element_type=F32
        )[0:1].astype(jnp.int32)
        rank = jnp.where(belongs, rank, -1)
        place = jnp.where(jnp.broadcast_to(rank, (NT, NT)) == down, 1.0, 0.0).astype(BF)
        upper = half * width + blk + side * 64
        digits = jnp.concatenate(
            [x.astype(F32) for x in (lane, row, upper, upper, upper, upper, upper, upper)], axis=0
        ).astype(BF)
        moved = lax.dot_general(
            digits, place, (((1,), (1,)), ((), ())), preferred_element_type=F32
        ).astype(jnp.int32)
        entry = moved[0:1] + moved[1:2] * NT + moved[2:3] * 8192
        out_ref[k : k + 1, :] = jnp.where(lane < count, entry, NROW * BLK * NT)
        sizes = jnp.where(lane == k, shr(count + UNROLL - 1, 3), sizes)
    for k in range(LISTS, 16):
        out_ref[k : k + 1, :] = sizes


def helper(col_index, tile_rows, tile_cols):
    return pl.pallas_call(
        helper_kernel,
        out_shape=jax.ShapeDtypeStruct((16, NT), jnp.int32),
        in_specs=[smem(), vmem(), vmem()],
        out_specs=vmem(),
        compiler_params=PARAMS,
        name="helper",
    )(col_index, tile_rows, tile_cols)


def load_kernel(tiles_hbm, own_ref, tiles_ref, sem):
    copy = pltpu.make_async_copy(tiles_hbm, tiles_ref, sem)
    copy.start()
    copy.wait()


def load_tiles(tiles, own):
    return pl.pallas_call(
        load_kernel,
        out_shape=jax.ShapeDtypeStruct(tiles.shape, BF),
        in_specs=[pl.BlockSpec(memory_space=pltpu.HBM), vmem()],
        out_specs=vmem(),
        scratch_shapes=[pltpu.SemaphoreType.DMA],
        compiler_params=PARAMS,
        name="load",
    )(pltpu.with_memory_space_constraint(tiles, pltpu.HBM), own)


def products(pairs):
    out = []
    for (va, ta), (vb, tb) in zip(pairs[::2], pairs[1::2]):
        both = product(jnp.concatenate([va, vb], axis=0), jnp.concatenate([ta, tb], axis=0))
        out += [both[:W, :B], both[W:, B:]]
    return out


def apply_list(lst, which, sources, tiles_ref, acc, low=0, most=NT):
    def group(g, _):
        rows, done = [], []
        for u in range(UNROLL):
            e = lst[which, g * UNROLL + u]
            at = shr(e, 13) & 63
            v = sources[0][at] if len(sources) == 1 else picked(shr(e, 19), *sources, at)
            rows.append(shr(e, 7) & 63)
            done.append((v, tiles_ref[e & 127]))
        for r, d in zip(rows, products(done)):
            acc[r] += d
        return 0

    groups = lst[LISTS, which]
    lax.fori_loop(low, jnp.minimum(groups, low + most), group, 0)


def late_start(slab, step):
    used = jnp.int32(step)
    for j in range(step):
        busy = slab[0] == ORDER[j]
        if 0 < j < NSLAB:
            busy = busy | (slab[0] == ORDER[j - 1])
        used = used - jnp.where(busy, jnp.int32(1), jnp.int32(0))
    return used * CHUNK


def write_down(acc, row, hot_ref, msg_ref):
    for d in range(NROW):
        r = (row[0] + d) & (NROW - 1)
        values = jnp.concatenate([acc[r * BLK + b].astype(BF) for b in range(PRT)], axis=1)
        part = jnp.dot(values, hot_ref[d], preferred_element_type=F32).astype(BF)
        for b in range(TGT):
            for s in range(2):
                msg_ref[s * NROW + r, b] = part[:, b * B : (b + 1) * B]


def write_up(acc, msg_ref):
    for r in range(NROW):
        for b in range(TGT):
            part = acc[r * BLK + b].astype(BF)
            for s in range(2):
                msg_ref[s * NROW + r, b] = part


MESSAGE = jax.ShapeDtypeStruct((2 * NROW, TGT, W, B), BF)


def first_kernel(lst, row, own_ref, other_ref, hot_ref, tiles_ref, acc, msg_ref):
    acc[...] = jnp.zeros(ACC, F32)
    apply_list(lst, V0AB, (own_ref, other_ref), tiles_ref, acc)
    write_down(acc, row, hot_ref, msg_ref)


def first_apply(lst, row, pair, hots, tiles):
    return pl.pallas_call(
        first_kernel,
        out_shape=(jax.ShapeDtypeStruct(ACC, F32), MESSAGE),
        in_specs=[smem(), smem()] + [vmem()] * 4,
        out_specs=(vmem(), vmem()),
        compiler_params=PARAMS,
        name="first",
    )(lst, row, *pair, hots, tiles)


def own_kernel(lst, slab, own_ref, own0, other0, tiles_ref, *refs, which, step):
    before, acc = refs[:-2], refs[-1]
    active = slab[0] == ORDER[step]
    after = slab[0] == ORDER[step - 1] if before else slab[0] < 0

    @pl.when(active)
    def _():
        apply_list(lst, which, (own_ref,), tiles_ref, acc)

    if before:
        @pl.when(after)
        def _():
            apply_list(lst, TC, before, tiles_ref, acc)

    @pl.when(jnp.logical_not(active | after))
    def _():
        apply_list(lst, V0C, (own0, other0), tiles_ref, acc, late_start(slab, step), CHUNK)


def own_apply(lst, slab, which, own, before, first_pair, tiles, acc, step):
    ins = (own, *first_pair, tiles, *before, acc)
    return pl.pallas_call(
        functools.partial(own_kernel, which=which, step=step),
        out_shape=jax.ShapeDtypeStruct(ACC, F32),
        in_specs=[smem(), smem()] + [vmem()] * len(ins),
        out_specs=vmem(),
        input_output_aliases={1 + len(ins): 0},
        compiler_params=PARAMS,
        name="own",
    )(lst, slab, *ins)


def other_kernel(lst, slab, row, other_ref, hot_ref, tiles_ref, acc_in, acc, msg_ref, *, which, step):
    @pl.when(slab[0] == ORDER[step])
    def _():
        apply_list(lst, which + 1, (other_ref,), tiles_ref, acc)

    if step + 1 < len(ORDER) and ORDER[step] < ORDER[step + 1]:
        write_down(acc, row, hot_ref, msg_ref)
    else:
        write_up(acc, msg_ref)


def other_apply(lst, slab, row, which, other, hots, tiles, acc, step):
    return pl.pallas_call(
        functools.partial(other_kernel, which=which, step=step),
        out_shape=(jax.ShapeDtypeStruct(ACC, F32), MESSAGE),
        in_specs=[smem(), smem(), smem()] + [vmem()] * 4,
        out_specs=(vmem(), vmem()),
        input_output_aliases={6: 0},
        compiler_params=PARAMS,
        name="other",
    )(lst, slab, row, other, hots, tiles, acc)


def step_apply(lst, slab, row, which, pairs, first_pair, hots, tiles, acc, step):
    own, other = pairs[-1]
    before = pairs[-2] if 0 < step < NSLAB else ()
    acc = own_apply(lst, slab, which, own, before, first_pair, tiles, acc, step)
    return other_apply(lst, slab, row, which, other, hots, tiles, acc, step)


def last_own_kernel(lst, slab, tiles_ref, own0, other0, *refs):
    gathered, acc = refs[:5], refs[6]
    for s in range(NSLAB - 1):
        at = 2 * (NSLAB - 2 - s)

        @pl.when(slab[0] == s)
        def _(s=s, at=at):
            if s == 0:
                apply_list(lst, LA, gathered[at : at + 1], tiles_ref, acc)
            apply_list(lst, LBC, gathered[at : at + 1], tiles_ref, acc)
            if s > 0:
                apply_list(lst, LBC + 1, gathered[at + 1 : at + 2], tiles_ref, acc)

    apply_list(lst, V0C, (own0, other0), tiles_ref, acc, late_start(slab, len(ORDER)))


def last_other_kernel(lst, slab, tiles_ref, other_ref, acc_in, acc, msg_ref):
    @pl.when(slab[0] == 0)
    def _():
        apply_list(lst, LA + 1, (other_ref,), tiles_ref, acc)
        apply_list(lst, LBC + 1, (other_ref,), tiles_ref, acc)

    for r in range(NROW):
        for b in range(BLK):
            msg_ref[r, b] = acc[r * BLK + b].astype(BF)


def last_apply(lst, slab, tiles, first_pair, pairs, acc):
    flat = [ref for pair in pairs[NSLAB - 1 :] for ref in pair]
    whole = jax.ShapeDtypeStruct(ACC, F32)
    acc = pl.pallas_call(
        last_own_kernel,
        out_shape=whole,
        in_specs=[smem(), smem()] + [vmem()] * 9,
        out_specs=vmem(),
        input_output_aliases={10: 0},
        compiler_params=PARAMS,
        name="last_own",
    )(lst, slab, tiles, *first_pair, *flat[:-1], acc)
    return pl.pallas_call(
        last_other_kernel,
        out_shape=(whole, jax.ShapeDtypeStruct((NROW, BLK, W, B), BF)),
        in_specs=[smem(), smem()] + [vmem()] * 3,
        out_specs=(vmem(), vmem()),
        input_output_aliases={4: 0},
        compiler_params=PARAMS,
        name="last_other",
    )(lst, slab, tiles, flat[-1], acc)[1]


def split(x):
    high = x.astype(BF)
    rest = x - high.astype(F32)
    return jnp.concatenate([high, rest.astype(BF)], axis=0)


def row_total(rcv_ref, place, b):
    part = rcv_ref[place * NROW, b].astype(F32)
    for r in range(1, NROW):
        part = part + rcv_ref[place * NROW + r, b].astype(F32)
    return part


def down_kernel(rcv_ref, rhs_ref, coef_ref, out_ref):
    for b in range(TGT):
        pulled = row_total(rcv_ref, 0, b) * coef_ref[:, b * B : (b + 1) * B]
        value = (rhs_ref[b] - pulled).astype(BF)
        for z in range(HALF):
            out_ref[z, b] = value


def up_kernel(rcv_ref, coef_ref, hot_ref, out_ref):
    values = jnp.concatenate(
        [
            split(row_total(rcv_ref, 1, b) * coef_ref[:, b * B : (b + 1) * B])
            for b in range(TGT)
        ],
        axis=1,
    )
    total = jnp.dot(values, hot_ref[...], preferred_element_type=F32)
    lifted = -(total[:W] + total[W:])
    for b in range(PRT):
        value = lifted[:, b * B : (b + 1) * B].astype(BF)
        for z in range(HALF):
            out_ref[z, b] = value


def combine(kernel, received, others, blocks):
    return pl.pallas_call(
        kernel,
        out_shape=jax.ShapeDtypeStruct((HALF, blocks, W, B), BF),
        in_specs=[vmem()] * (1 + len(others)),
        out_specs=vmem(),
        compiler_params=PARAMS,
    )(received, *others)


def prepare_kernel(
    count, slab, rhs_hbm, rows_hbm, cols_hbm, map_hbm, coef_hbm,
    out_ref, target_ref, rows_ref, cols_ref, pack_ref,
    rhs_ref, map_ref, coef_ref, sems,
):
    wide = 2 * B
    copies = [
        pltpu.make_async_copy(
            rhs_hbm.at[0, :, pl.ds(k * wide, wide)], rhs_ref.at[k], sems.at[k]
        )
        for k in range(BLK // 2)
    ]
    small = [
        pltpu.make_async_copy(src, dst, sems.at[BLK // 2 + k])
        for k, (src, dst) in enumerate(
            ((rows_hbm, rows_ref), (cols_hbm, cols_ref), (map_hbm, map_ref), (coef_hbm, coef_ref))
        )
    ]
    for copy in copies + small:
        copy.start()
    for b in range(BLK):
        if b % 2 == 0:
            copies[b // 2].wait()
        value = rhs_ref[b // 2, :, b % 2 * B : (b % 2 + 1) * B]
        if b < TGT:
            target_ref[b] = value
            value = jnp.where(slab[0] == 0, value, 0.0)
        value = jnp.where(b < count[0], value, 0.0).astype(BF)
        for z in range(HALF):
            out_ref[z, b] = value
    for copy in small:
        copy.wait()
    pack_ref[0:1, :] = map_ref[...].astype(F32)
    pack_ref[1:2, :] = coef_ref[...]


def prepare(right_sides, section_blocks, slab, tile_rows, tile_cols, plane_map, interface_coef):
    ins = (right_sides, tile_rows, tile_cols, plane_map, interface_coef)
    return pl.pallas_call(
        prepare_kernel,
        out_shape=(
            jax.ShapeDtypeStruct((HALF, BLK, W, B), BF),
            jax.ShapeDtypeStruct((TGT, W, B), F32),
            jax.ShapeDtypeStruct(tile_rows.shape, jnp.int32),
            jax.ShapeDtypeStruct(tile_cols.shape, jnp.int32),
            jax.ShapeDtypeStruct((2, TGT * B), F32),
        ),
        in_specs=[smem(), smem()] + [pl.BlockSpec(memory_space=pltpu.HBM)] * 5,
        out_specs=(vmem(),) * 5,
        scratch_shapes=[
            pltpu.VMEM((BLK // 2, W, 2 * B), F32),
            pltpu.VMEM((1, TGT * B), jnp.int32),
            pltpu.VMEM((1, TGT * B), F32),
            pltpu.SemaphoreType.DMA((BLK // 2 + 4,)),
        ],
        compiler_params=PARAMS,
        name="prepare",
    )(section_blocks, slab, *[pltpu.with_memory_space_constraint(x, pltpu.HBM) for x in ins])


def finish_kernel(count, parts_ref, out_ref):
    for b in range(BLK):
        total = parts_ref[0, b].astype(F32)
        for r in range(1, NROW):
            total = total + parts_ref[r, b].astype(F32)
        out_ref[0, :, b * B : (b + 1) * B] = jnp.where(b < count[0], total, 0.0)


def finish(section_blocks, parts):
    return pl.pallas_call(
        finish_kernel,
        out_shape=jax.ShapeDtypeStruct((1, W, BLK * B), F32),
        in_specs=[smem(), vmem()],
        out_specs=vmem(),
        compiler_params=PARAMS,
        name="finish",
    )(section_blocks, parts)


Z_GROUPS = [[2 * z + k for z in range(HALF)] for k in range(2)]


def gather(copies):
    own = lax.all_to_all(copies, "col", 0, 0, tiled=True, axis_index_groups=Z_GROUPS)
    own = own.reshape(HALF * copies.shape[1], W, B)
    return own, lax.ppermute(own, "col", [(c, c ^ 1) for c in range(NCOL)])


def exchange(message, low):
    groups = [
        [(s + k) % NSLAB * NROW + r for k in range(2) for r in range(NROW)]
        for s in (low, low + 2)
    ]
    return lax.all_to_all(message, ("slab", "row"), 0, 0, tiled=True, axis_index_groups=groups)


def from_next(value, turn):
    pairs = [
        ((s + 1) * NROW + (r + turn) % NROW, s * NROW + r)
        for s in range(NSLAB - 1)
        for r in range(NROW)
    ]
    return lax.ppermute(value, ("slab", "row"), pairs)


def body(right_sides, front_tiles, tile_rows, tile_cols, section_blocks, plane_map, interface_coef):
    slab = lax.axis_index("slab").astype(jnp.int32)
    row = lax.axis_index("row").astype(jnp.int32)
    col = lax.axis_index("col").astype(jnp.int32)
    slab = slab.reshape(1)
    row = row.reshape(1)
    col = col.reshape(1)
    copies, rhs_target, rows, cols, pack = prepare(
        right_sides, section_blocks, slab, tile_rows, tile_cols, plane_map, interface_coef
    )
    packs = [from_next(pack, d) for d in range(NROW)]
    lst = helper(col, rows, cols)
    coef_next = packs[0][1:2]
    maps_next = jnp.concatenate([p[0:1] for p in packs], axis=0).astype(jnp.int32)

    partner = jnp.arange(PRT * B, dtype=jnp.int32)
    hots = (partner[None, :, None] == maps_next[:, None, :]).astype(BF)
    hot_next = (maps_next[0][:, None] == partner[None, :]).astype(BF)

    start = gather(copies)
    tiles = load_tiles(front_tiles[0], start[0])
    start, hots, hot_next, coef_next, rhs_target, lst, tiles = lax.optimization_barrier(
        (start, hots, hot_next, coef_next, rhs_target, lst, tiles)
    )
    acc, msg = first_apply(lst, row, start, hots, tiles)
    pairs = []
    for step in range(2 * NSLAB - 2):
        if step < NSLAB - 1:
            rcv = exchange(msg, step)
            value = combine(down_kernel, rcv, (rhs_target, interface_coef), TGT)
        else:
            rcv = exchange(msg, 2 * NSLAB - 3 - step)
            value = combine(up_kernel, rcv, (coef_next, hot_next), PRT)
        pairs.append(gather(value))
        if step < len(ORDER):
            which = TAB if step < NSLAB - 1 else LA
            acc, msg = step_apply(lst, slab, row, which, pairs, start, hots, tiles, acc, step)
    msg = last_apply(lst, slab, tiles, start, pairs, acc)
    return finish(section_blocks, lax.all_to_all(msg, "row", 0, 0, tiled=True))


def solution(mesh):
    placed = (
        P("slab", None, ("col", "row")),
        P("slab", ("col", "row"), None, None),
        P("slab", ("col", "row")),
        P("slab", ("col", "row")),
        P("slab"),
        P("slab", ("col", "row")),
        P("slab", ("col", "row")),
    )
    return jax.shard_map(
        body, mesh=mesh, in_specs=placed, out_specs=P("slab", None, ("col", "row")), check_vma=False
    )
```

```python
import functools

import jax
import jax.numpy as jnp
from jax import lax
from jax.experimental import pallas as pl
from jax.experimental.pallas import tpu as pltpu
from jax.sharding import PartitionSpec as P


B = 128
BLK = 8
NROW = 4
NCOL = 16
NSLAB = 4
W = 32
NT = 128
UNROLL = 8
TGT = 2
PRT = 4
BF = jnp.bfloat16
F32 = jnp.float32


def smem():
    return pl.BlockSpec(memory_space=pltpu.SMEM)


def vmem():
    return pl.BlockSpec(memory_space=pltpu.VMEM)


PARAMS = pltpu.CompilerParams(vmem_limit_bytes=24 * 2**20)
ACC = (NROW * BLK + 1, W, B)
LISTS = 9
V0AB, V0C, TC, TAB, LA, LBC = 0, 1, 2, 3, 5, 7
CHUNK = 3
EXTRA = 2
ORDER = (1, 2, 3, 2, 1)
HALF = NCOL // 2


def shr(x, n):
    return lax.shift_right_logical(x, jnp.int32(n))


def product(v, tile):
    return lax.dot_general(v, tile, (((1,), (1,)), ((), ())), preferred_element_type=F32)


def picked(side, own_ref, other_ref, at):
    return jnp.where(side == 0, own_ref[at], other_ref[at])


def helper_kernel(col_index, rows_ref, cols_ref, out_ref):
    lane = lax.broadcasted_iota(jnp.int32, (1, NT), 1)
    down = lax.broadcasted_iota(jnp.int32, (NT, NT), 0)
    across = lax.broadcasted_iota(jnp.int32, (NT, NT), 1)
    before = jnp.where(down < across, 1.0, 0.0).astype(BF)
    row = rows_ref[...] - col_index[0] * (NROW * BLK)
    col = cols_ref[...]
    part = shr(col, 5)
    half = shr(part, 1)
    side = (part & 1) ^ (col_index[0] & 1)
    blk = col & (BLK - 1)
    out = row & (BLK - 1)
    early = out < PRT
    target = blk < TGT
    low = blk < PRT
    own = side == 0
    other = side == 1
    member = (
        (BLK, early),
        (BLK, out >= PRT),
        (TGT, target & (out >= PRT)),
        (TGT, target & early & own),
        (TGT, target & early & other),
        (PRT, low & (out < TGT) & own),
        (PRT, low & (out < TGT) & other),
        (PRT, low & (out >= TGT) & own),
        (PRT, low & (out >= TGT) & other),
    )
    sizes = jnp.zeros((1, NT), jnp.int32)
    for k, (width, belongs) in enumerate(member):
        one = jnp.where(belongs, 1.0, 0.0)
        count = jnp.sum(one, axis=1, keepdims=True).astype(jnp.int32)
        rank = jnp.dot(
            jnp.broadcast_to(one, (8, NT)).astype(BF), before, preferred_element_type=F32
        )[0:1].astype(jnp.int32)
        rank = jnp.where(belongs, rank, -1)
        place = jnp.where(jnp.broadcast_to(rank, (NT, NT)) == down, 1.0, 0.0).astype(BF)
        upper = half * width + blk + side * 64
        digits = jnp.concatenate(
            [x.astype(F32) for x in (lane, row, upper, upper, upper, upper, upper, upper)], axis=0
        ).astype(BF)
        moved = lax.dot_general(
            digits, place, (((1,), (1,)), ((), ())), preferred_element_type=F32
        ).astype(jnp.int32)
        entry = moved[0:1] + moved[1:2] * NT + moved[2:3] * 8192
        out_ref[k : k + 1, :] = jnp.where(lane < count, entry, NROW * BLK * NT)
        sizes = jnp.where(lane == k, shr(count + UNROLL - 1, 3), sizes)
    for k in range(LISTS, 16):
        out_ref[k : k + 1, :] = sizes


def helper(col_index, tile_rows, tile_cols):
    return pl.pallas_call(
        helper_kernel,
        out_shape=jax.ShapeDtypeStruct((16, NT), jnp.int32),
        in_specs=[smem(), vmem(), vmem()],
        out_specs=vmem(),
        compiler_params=PARAMS,
        name="helper",
    )(col_index, tile_rows, tile_cols)


def load_kernel(tiles_hbm, own_ref, tiles_ref, sem):
    copy = pltpu.make_async_copy(tiles_hbm, tiles_ref, sem)
    copy.start()
    copy.wait()


def load_tiles(tiles, own):
    return pl.pallas_call(
        load_kernel,
        out_shape=jax.ShapeDtypeStruct(tiles.shape, BF),
        in_specs=[pl.BlockSpec(memory_space=pltpu.HBM), vmem()],
        out_specs=vmem(),
        scratch_shapes=[pltpu.SemaphoreType.DMA],
        compiler_params=PARAMS,
        name="load",
    )(pltpu.with_memory_space_constraint(tiles, pltpu.HBM), own)


def products(pairs):
    out = []
    for (va, ta), (vb, tb) in zip(pairs[::2], pairs[1::2]):
        both = product(jnp.concatenate([va, vb], axis=0), jnp.concatenate([ta, tb], axis=0))
        out += [both[:W, :B], both[W:, B:]]
    return out


def apply_list(lst, which, sources, tiles_ref, acc, low=0, most=NT):
    def group(g, _):
        rows, done = [], []
        for u in range(UNROLL):
            e = lst[which, g * UNROLL + u]
            at = shr(e, 13) & 63
            v = sources[0][at] if len(sources) == 1 else picked(shr(e, 19), *sources, at)
            rows.append(shr(e, 7) & 63)
            done.append((v, tiles_ref[e & 127]))
        for r, d in zip(rows, products(done)):
            acc[r] += d
        return 0

    groups = lst[LISTS, which]
    lax.fori_loop(low, jnp.minimum(groups, low + most), group, 0)


def late_start(slab, step):
    used = jnp.int32(step)
    for j in range(step):
        busy = slab[0] == ORDER[j]
        if 0 < j < NSLAB:
            busy = busy | (slab[0] == ORDER[j - 1])
        used = used - jnp.where(busy, jnp.int32(1), jnp.int32(0))
    return used * (CHUNK + EXTRA)


def write_down(acc, row, hot_ref, msg_ref):
    for d in range(NROW):
        r = (row[0] + d) & (NROW - 1)
        values = jnp.concatenate([acc[r * BLK + b].astype(BF) for b in range(PRT)], axis=1)
        part = jnp.dot(values, hot_ref[d], preferred_element_type=F32).astype(BF)
        for b in range(TGT):
            for s in range(2):
                msg_ref[s * NROW + r, b] = part[:, b * B : (b + 1) * B]


def write_up(acc, msg_ref):
    for r in range(NROW):
        for b in range(TGT):
            part = acc[r * BLK + b].astype(BF)
            for s in range(2):
                msg_ref[s * NROW + r, b] = part


MESSAGE = jax.ShapeDtypeStruct((2 * NROW, TGT, W, B), BF)


def first_kernel(lst, row, own_ref, other_ref, hot_ref, tiles_ref, acc, msg_ref):
    acc[...] = jnp.zeros(ACC, F32)
    apply_list(lst, V0AB, (own_ref, other_ref), tiles_ref, acc)
    write_down(acc, row, hot_ref, msg_ref)


def first_apply(lst, row, pair, hots, tiles):
    return pl.pallas_call(
        first_kernel,
        out_shape=(jax.ShapeDtypeStruct(ACC, F32), MESSAGE),
        in_specs=[smem(), smem()] + [vmem()] * 4,
        out_specs=(vmem(), vmem()),
        compiler_params=PARAMS,
        name="first",
    )(lst, row, *pair, hots, tiles)


def own_kernel(lst, slab, own_ref, own0, other0, tiles_ref, *refs, which, step):
    before, acc = refs[:-2], refs[-1]
    active = slab[0] == ORDER[step]
    after = slab[0] == ORDER[step - 1] if before else slab[0] < 0

    @pl.when(active)
    def _():
        apply_list(lst, which, (own_ref,), tiles_ref, acc)

    if before:
        @pl.when(after)
        def _():
            apply_list(lst, TC, before, tiles_ref, acc)

    @pl.when(jnp.logical_not(active | after))
    def _():
        apply_list(lst, V0C, (own0, other0), tiles_ref, acc, late_start(slab, step), CHUNK)


def own_apply(lst, slab, which, own, before, first_pair, tiles, acc, step):
    ins = (own, *first_pair, tiles, *before, acc)
    return pl.pallas_call(
        functools.partial(own_kernel, which=which, step=step),
        out_shape=jax.ShapeDtypeStruct(ACC, F32),
        in_specs=[smem(), smem()] + [vmem()] * len(ins),
        out_specs=vmem(),
        input_output_aliases={1 + len(ins): 0},
        compiler_params=PARAMS,
        name="own",
    )(lst, slab, *ins)


def other_kernel(
    lst, slab, row, other_ref, own0, other0, hot_ref, tiles_ref, acc_in, acc, msg_ref, *, which, step
):
    active = slab[0] == ORDER[step]
    after = slab[0] == ORDER[step - 1] if 0 < step < NSLAB else slab[0] < 0

    @pl.when(active)
    def _():
        apply_list(lst, which + 1, (other_ref,), tiles_ref, acc)

    @pl.when(jnp.logical_not(active | after))
    def _():
        apply_list(lst, V0C, (own0, other0), tiles_ref, acc, late_start(slab, step) + CHUNK, EXTRA)

    if step + 1 < len(ORDER) and ORDER[step] < ORDER[step + 1]:
        write_down(acc, row, hot_ref, msg_ref)
    else:
        write_up(acc, msg_ref)


def other_apply(lst, slab, row, which, other, first_pair, hots, tiles, acc, step):
    return pl.pallas_call(
        functools.partial(other_kernel, which=which, step=step),
        out_shape=(jax.ShapeDtypeStruct(ACC, F32), MESSAGE),
        in_specs=[smem(), smem(), smem()] + [vmem()] * 6,
        out_specs=(vmem(), vmem()),
        input_output_aliases={8: 0},
        compiler_params=PARAMS,
        name="other",
    )(lst, slab, row, other, *first_pair, hots, tiles, acc)


def step_apply(lst, slab, row, which, pairs, first_pair, hots, tiles, acc, step):
    own, other = pairs[-1]
    before = pairs[-2] if 0 < step < NSLAB else ()
    acc = own_apply(lst, slab, which, own, before, first_pair, tiles, acc, step)
    return other_apply(lst, slab, row, which, other, first_pair, hots, tiles, acc, step)


def last_own_kernel(lst, slab, tiles_ref, own0, other0, *refs):
    gathered, acc = refs[:5], refs[6]
    for s in range(NSLAB - 1):
        at = 2 * (NSLAB - 2 - s)

        @pl.when(slab[0] == s)
        def _(s=s, at=at):
            if s == 0:
                apply_list(lst, LA, gathered[at : at + 1], tiles_ref, acc)
            apply_list(lst, LBC, gathered[at : at + 1], tiles_ref, acc)
            if s > 0:
                apply_list(lst, LBC + 1, gathered[at + 1 : at + 2], tiles_ref, acc)

    apply_list(lst, V0C, (own0, other0), tiles_ref, acc, late_start(slab, len(ORDER)))


def last_other_kernel(lst, slab, tiles_ref, other_ref, acc_in, acc, msg_ref):
    @pl.when(slab[0] == 0)
    def _():
        apply_list(lst, LA + 1, (other_ref,), tiles_ref, acc)
        apply_list(lst, LBC + 1, (other_ref,), tiles_ref, acc)

    for r in range(NROW):
        for b in range(BLK):
            msg_ref[r, b] = acc[r * BLK + b].astype(BF)


def last_apply(lst, slab, tiles, first_pair, pairs, acc):
    flat = [ref for pair in pairs[NSLAB - 1 :] for ref in pair]
    whole = jax.ShapeDtypeStruct(ACC, F32)
    acc = pl.pallas_call(
        last_own_kernel,
        out_shape=whole,
        in_specs=[smem(), smem()] + [vmem()] * 9,
        out_specs=vmem(),
        input_output_aliases={10: 0},
        compiler_params=PARAMS,
        name="last_own",
    )(lst, slab, tiles, *first_pair, *flat[:-1], acc)
    return pl.pallas_call(
        last_other_kernel,
        out_shape=(whole, jax.ShapeDtypeStruct((NROW, BLK, W, B), BF)),
        in_specs=[smem(), smem()] + [vmem()] * 3,
        out_specs=(vmem(), vmem()),
        input_output_aliases={4: 0},
        compiler_params=PARAMS,
        name="last_other",
    )(lst, slab, tiles, flat[-1], acc)[1]


def split(x):
    high = x.astype(BF)
    rest = x - high.astype(F32)
    return jnp.concatenate([high, rest.astype(BF)], axis=0)


def row_total(rcv_ref, place, b):
    part = rcv_ref[place * NROW, b].astype(F32)
    for r in range(1, NROW):
        part = part + rcv_ref[place * NROW + r, b].astype(F32)
    return part


def down_kernel(rcv_ref, rhs_ref, coef_ref, out_ref):
    for b in range(TGT):
        pulled = row_total(rcv_ref, 0, b) * coef_ref[:, b * B : (b + 1) * B]
        value = (rhs_ref[b] - pulled).astype(BF)
        for z in range(HALF):
            out_ref[z, b] = value


def up_kernel(rcv_ref, coef_ref, hot_ref, out_ref):
    values = jnp.concatenate(
        [
            split(row_total(rcv_ref, 1, b) * coef_ref[:, b * B : (b + 1) * B])
            for b in range(TGT)
        ],
        axis=1,
    )
    total = jnp.dot(values, hot_ref[...], preferred_element_type=F32)
    lifted = -(total[:W] + total[W:])
    for b in range(PRT):
        value = lifted[:, b * B : (b + 1) * B].astype(BF)
        for z in range(HALF):
            out_ref[z, b] = value


def combine(kernel, received, others, blocks):
    return pl.pallas_call(
        kernel,
        out_shape=jax.ShapeDtypeStruct((HALF, blocks, W, B), BF),
        in_specs=[vmem()] * (1 + len(others)),
        out_specs=vmem(),
        compiler_params=PARAMS,
    )(received, *others)


def prepare_kernel(
    count, slab, rhs_hbm, rows_hbm, cols_hbm, map_hbm, coef_hbm,
    out_ref, target_ref, rows_ref, cols_ref, pack_ref,
    rhs_ref, map_ref, coef_ref, sems,
):
    wide = 2 * B
    copies = [
        pltpu.make_async_copy(
            rhs_hbm.at[0, :, pl.ds(k * wide, wide)], rhs_ref.at[k], sems.at[k]
        )
        for k in range(BLK // 2)
    ]
    small = [
        pltpu.make_async_copy(src, dst, sems.at[BLK // 2 + k])
        for k, (src, dst) in enumerate(
            ((rows_hbm, rows_ref), (cols_hbm, cols_ref), (map_hbm, map_ref), (coef_hbm, coef_ref))
        )
    ]
    for copy in copies + small:
        copy.start()
    for b in range(BLK):
        if b % 2 == 0:
            copies[b // 2].wait()
        value = rhs_ref[b // 2, :, b % 2 * B : (b % 2 + 1) * B]
        if b < TGT:
            target_ref[b] = value
            value = jnp.where(slab[0] == 0, value, 0.0)
        value = jnp.where(b < count[0], value, 0.0).astype(BF)
        for z in range(HALF):
            out_ref[z, b] = value
    for copy in small:
        copy.wait()
    pack_ref[0:1, :] = map_ref[...].astype(F32)
    pack_ref[1:2, :] = coef_ref[...]


def prepare(right_sides, section_blocks, slab, tile_rows, tile_cols, plane_map, interface_coef):
    ins = (right_sides, tile_rows, tile_cols, plane_map, interface_coef)
    return pl.pallas_call(
        prepare_kernel,
        out_shape=(
            jax.ShapeDtypeStruct((HALF, BLK, W, B), BF),
            jax.ShapeDtypeStruct((TGT, W, B), F32),
            jax.ShapeDtypeStruct(tile_rows.shape, jnp.int32),
            jax.ShapeDtypeStruct(tile_cols.shape, jnp.int32),
            jax.ShapeDtypeStruct((2, TGT * B), F32),
        ),
        in_specs=[smem(), smem()] + [pl.BlockSpec(memory_space=pltpu.HBM)] * 5,
        out_specs=(vmem(),) * 5,
        scratch_shapes=[
            pltpu.VMEM((BLK // 2, W, 2 * B), F32),
            pltpu.VMEM((1, TGT * B), jnp.int32),
            pltpu.VMEM((1, TGT * B), F32),
            pltpu.SemaphoreType.DMA((BLK // 2 + 4,)),
        ],
        compiler_params=PARAMS,
        name="prepare",
    )(section_blocks, slab, *[pltpu.with_memory_space_constraint(x, pltpu.HBM) for x in ins])


def finish_kernel(count, parts_ref, out_ref):
    for b in range(BLK):
        total = parts_ref[0, b].astype(F32)
        for r in range(1, NROW):
            total = total + parts_ref[r, b].astype(F32)
        out_ref[0, :, b * B : (b + 1) * B] = jnp.where(b < count[0], total, 0.0)


def finish(section_blocks, parts):
    return pl.pallas_call(
        finish_kernel,
        out_shape=jax.ShapeDtypeStruct((1, W, BLK * B), F32),
        in_specs=[smem(), vmem()],
        out_specs=vmem(),
        compiler_params=PARAMS,
        name="finish",
    )(section_blocks, parts)


Z_GROUPS = [[2 * z + k for z in range(HALF)] for k in range(2)]


def gather(copies):
    own = lax.all_to_all(copies, "col", 0, 0, tiled=True, axis_index_groups=Z_GROUPS)
    own = own.reshape(HALF * copies.shape[1], W, B)
    return own, lax.ppermute(own, "col", [(c, c ^ 1) for c in range(NCOL)])


def exchange(message, low):
    groups = [
        [(s + k) % NSLAB * NROW + r for k in range(2) for r in range(NROW)]
        for s in (low, low + 2)
    ]
    return lax.all_to_all(message, ("slab", "row"), 0, 0, tiled=True, axis_index_groups=groups)


def from_next(value, turn):
    pairs = [
        ((s + 1) * NROW + (r + turn) % NROW, s * NROW + r)
        for s in range(NSLAB - 1)
        for r in range(NROW)
    ]
    return lax.ppermute(value, ("slab", "row"), pairs)


def body(right_sides, front_tiles, tile_rows, tile_cols, section_blocks, plane_map, interface_coef):
    slab = lax.axis_index("slab").astype(jnp.int32)
    row = lax.axis_index("row").astype(jnp.int32)
    col = lax.axis_index("col").astype(jnp.int32)
    slab = slab.reshape(1)
    row = row.reshape(1)
    col = col.reshape(1)
    copies, rhs_target, rows, cols, pack = prepare(
        right_sides, section_blocks, slab, tile_rows, tile_cols, plane_map, interface_coef
    )
    packs = [from_next(pack, d) for d in range(NROW)]
    lst = helper(col, rows, cols)
    coef_next = packs[0][1:2]
    maps_next = jnp.concatenate([p[0:1] for p in packs], axis=0).astype(jnp.int32)

    partner = jnp.arange(PRT * B, dtype=jnp.int32)
    hots = (partner[None, :, None] == maps_next[:, None, :]).astype(BF)
    hot_next = (maps_next[0][:, None] == partner[None, :]).astype(BF)

    start = gather(copies)
    tiles = load_tiles(front_tiles[0], start[0])
    start, hots, hot_next, coef_next, rhs_target, lst, tiles = lax.optimization_barrier(
        (start, hots, hot_next, coef_next, rhs_target, lst, tiles)
    )
    acc, msg = first_apply(lst, row, start, hots, tiles)
    pairs = []
    for step in range(2 * NSLAB - 2):
        if step < NSLAB - 1:
            rcv = exchange(msg, step)
            value = combine(down_kernel, rcv, (rhs_target, interface_coef), TGT)
        else:
            rcv = exchange(msg, 2 * NSLAB - 3 - step)
            value = combine(up_kernel, rcv, (coef_next, hot_next), PRT)
        pairs.append(gather(value))
        if step < len(ORDER):
            which = TAB if step < NSLAB - 1 else LA
            acc, msg = step_apply(lst, slab, row, which, pairs, start, hots, tiles, acc, step)
    msg = last_apply(lst, slab, tiles, start, pairs, acc)
    return finish(section_blocks, lax.all_to_all(msg, "row", 0, 0, tiled=True))


def solution(mesh):
    placed = (
        P("slab", None, ("col", "row")),
        P("slab", ("col", "row"), None, None),
        P("slab", ("col", "row")),
        P("slab", ("col", "row")),
        P("slab"),
        P("slab", ("col", "row")),
        P("slab", ("col", "row")),
    )
    return jax.shard_map(
        body, mesh=mesh, in_specs=placed, out_specs=P("slab", None, ("col", "row")), check_vma=False
    )
```

```python
import functools

import jax
import jax.numpy as jnp
from jax import lax
from jax.experimental import pallas as pl
from jax.experimental.pallas import tpu as pltpu
from jax.sharding import PartitionSpec as P


B = 128
BLK = 8
NROW = 4
NCOL = 16
NSLAB = 4
W = 32
NT = 128
UNROLL = 8
TGT = 2
PRT = 4
BF = jnp.bfloat16
F32 = jnp.float32


def smem():
    return pl.BlockSpec(memory_space=pltpu.SMEM)


def vmem():
    return pl.BlockSpec(memory_space=pltpu.VMEM)


PARAMS = pltpu.CompilerParams(vmem_limit_bytes=24 * 2**20)
ACC = (NROW * BLK + 1, W, B)
LISTS = 9
V0AB, V0C, TC, TAB, LA, LBC = 0, 1, 2, 3, 5, 7
CHUNK = 3
ORDER = (1, 2, 3, 2, 1)
HALF = NCOL // 2


def shr(x, n):
    return lax.shift_right_logical(x, jnp.int32(n))


def product(v, tile):
    return lax.dot_general(v, tile, (((1,), (1,)), ((), ())), preferred_element_type=F32)


def picked(side, own_ref, other_ref, at):
    return jnp.where(side == 0, own_ref[at], other_ref[at])


def helper_kernel(col_index, rows_ref, cols_ref, out_ref):
    lane = lax.broadcasted_iota(jnp.int32, (1, NT), 1)
    down = lax.broadcasted_iota(jnp.int32, (NT, NT), 0)
    across = lax.broadcasted_iota(jnp.int32, (NT, NT), 1)
    before = jnp.where(down < across, 1.0, 0.0).astype(BF)
    row = rows_ref[...] - col_index[0] * (NROW * BLK)
    col = cols_ref[...]
    part = shr(col, 5)
    half = shr(part, 1)
    side = (part & 1) ^ (col_index[0] & 1)
    blk = col & (BLK - 1)
    out = row & (BLK - 1)
    early = out < PRT
    target = blk < TGT
    low = blk < PRT
    own = side == 0
    other = side == 1
    member = (
        (BLK, early),
        (BLK, out >= PRT),
        (TGT, target & (out >= PRT)),
        (TGT, target & early & own),
        (TGT, target & early & other),
        (PRT, low & (out < TGT) & own),
        (PRT, low & (out < TGT) & other),
        (PRT, low & (out >= TGT) & own),
        (PRT, low & (out >= TGT) & other),
    )
    sizes = jnp.zeros((1, NT), jnp.int32)
    for k, (width, belongs) in enumerate(member):
        one = jnp.where(belongs, 1.0, 0.0)
        count = jnp.sum(one, axis=1, keepdims=True).astype(jnp.int32)
        rank = jnp.dot(
            jnp.broadcast_to(one, (8, NT)).astype(BF), before, preferred_element_type=F32
        )[0:1].astype(jnp.int32)
        rank = jnp.where(belongs, rank, -1)
        place = jnp.where(jnp.broadcast_to(rank, (NT, NT)) == down, 1.0, 0.0).astype(BF)
        upper = half * width + blk + side * 64
        digits = jnp.concatenate(
            [x.astype(F32) for x in (lane, row, upper, upper, upper, upper, upper, upper)], axis=0
        ).astype(BF)
        moved = lax.dot_general(
            digits, place, (((1,), (1,)), ((), ())), preferred_element_type=F32
        ).astype(jnp.int32)
        entry = moved[0:1] + moved[1:2] * NT + moved[2:3] * 8192
        out_ref[k : k + 1, :] = jnp.where(lane < count, entry, NROW * BLK * NT)
        sizes = jnp.where(lane == k, shr(count + UNROLL - 1, 3), sizes)
    for k in range(LISTS, 16):
        out_ref[k : k + 1, :] = sizes


def helper(col_index, tile_rows, tile_cols):
    return pl.pallas_call(
        helper_kernel,
        out_shape=jax.ShapeDtypeStruct((16, NT), jnp.int32),
        in_specs=[smem(), vmem(), vmem()],
        out_specs=vmem(),
        compiler_params=PARAMS,
        name="helper",
    )(col_index, tile_rows, tile_cols)


def load_kernel(tiles_hbm, own_ref, tiles_ref, sem):
    copy = pltpu.make_async_copy(tiles_hbm, tiles_ref, sem)
    copy.start()
    copy.wait()


def load_tiles(tiles, own):
    return pl.pallas_call(
        load_kernel,
        out_shape=jax.ShapeDtypeStruct(tiles.shape, BF),
        in_specs=[pl.BlockSpec(memory_space=pltpu.HBM), vmem()],
        out_specs=vmem(),
        scratch_shapes=[pltpu.SemaphoreType.DMA],
        compiler_params=PARAMS,
        name="load",
    )(pltpu.with_memory_space_constraint(tiles, pltpu.HBM), own)


def products(pairs):
    out = []
    for (va, ta), (vb, tb) in zip(pairs[::2], pairs[1::2]):
        zero = jnp.zeros_like(va)
        left = jnp.concatenate(
            [jnp.concatenate([va, zero], axis=1), jnp.concatenate([zero, vb], axis=1)], axis=0
        )
        both = product(left, jnp.concatenate([ta, tb], axis=1))
        out += [both[:W], both[W:]]
    return out


def apply_list(lst, which, sources, tiles_ref, acc, low=0, most=NT):
    def group(g, _):
        rows, done = [], []
        for u in range(UNROLL):
            e = lst[which, g * UNROLL + u]
            at = shr(e, 13) & 63
            v = sources[0][at] if len(sources) == 1 else picked(shr(e, 19), *sources, at)
            rows.append(shr(e, 7) & 63)
            done.append((v, tiles_ref[e & 127]))
        for r, d in zip(rows, products(done)):
            acc[r] += d
        return 0

    groups = lst[LISTS, which]
    lax.fori_loop(low, jnp.minimum(groups, low + most), group, 0)


def late_start(slab, step):
    used = jnp.int32(step)
    for j in range(step):
        busy = slab[0] == ORDER[j]
        if 0 < j < NSLAB:
            busy = busy | (slab[0] == ORDER[j - 1])
        used = used - jnp.where(busy, jnp.int32(1), jnp.int32(0))
    return used * CHUNK


def write_down(acc, row, hot_ref, msg_ref):
    for d in range(NROW):
        r = (row[0] + d) & (NROW - 1)
        values = jnp.concatenate([acc[r * BLK + b].astype(BF) for b in range(PRT)], axis=1)
        part = jnp.dot(values, hot_ref[d], preferred_element_type=F32).astype(BF)
        for b in range(TGT):
            for s in range(2):
                msg_ref[s * NROW + r, b] = part[:, b * B : (b + 1) * B]


def write_up(acc, msg_ref):
    for r in range(NROW):
        for b in range(TGT):
            part = acc[r * BLK + b].astype(BF)
            for s in range(2):
                msg_ref[s * NROW + r, b] = part


MESSAGE = jax.ShapeDtypeStruct((2 * NROW, TGT, W, B), BF)


def first_kernel(lst, row, own_ref, other_ref, hot_ref, tiles_ref, acc, msg_ref):
    acc[...] = jnp.zeros(ACC, F32)
    apply_list(lst, V0AB, (own_ref, other_ref), tiles_ref, acc)
    write_down(acc, row, hot_ref, msg_ref)


def first_apply(lst, row, pair, hots, tiles):
    return pl.pallas_call(
        first_kernel,
        out_shape=(jax.ShapeDtypeStruct(ACC, F32), MESSAGE),
        in_specs=[smem(), smem()] + [vmem()] * 4,
        out_specs=(vmem(), vmem()),
        compiler_params=PARAMS,
        name="first",
    )(lst, row, *pair, hots, tiles)


def own_kernel(lst, slab, own_ref, own0, other0, tiles_ref, *refs, which, step):
    before, acc = refs[:-2], refs[-1]
    active = slab[0] == ORDER[step]
    after = slab[0] == ORDER[step - 1] if before else slab[0] < 0

    @pl.when(active)
    def _():
        apply_list(lst, which, (own_ref,), tiles_ref, acc)

    if before:
        @pl.when(after)
        def _():
            apply_list(lst, TC, before, tiles_ref, acc)

    @pl.when(jnp.logical_not(active | after))
    def _():
        apply_list(lst, V0C, (own0, other0), tiles_ref, acc, late_start(slab, step), CHUNK)


def own_apply(lst, slab, which, own, before, first_pair, tiles, acc, step):
    ins = (own, *first_pair, tiles, *before, acc)
    return pl.pallas_call(
        functools.partial(own_kernel, which=which, step=step),
        out_shape=jax.ShapeDtypeStruct(ACC, F32),
        in_specs=[smem(), smem()] + [vmem()] * len(ins),
        out_specs=vmem(),
        input_output_aliases={1 + len(ins): 0},
        compiler_params=PARAMS,
        name="own",
    )(lst, slab, *ins)


def other_kernel(lst, slab, row, other_ref, hot_ref, tiles_ref, acc_in, acc, msg_ref, *, which, step):
    @pl.when(slab[0] == ORDER[step])
    def _():
        apply_list(lst, which + 1, (other_ref,), tiles_ref, acc)

    if step + 1 < len(ORDER) and ORDER[step] < ORDER[step + 1]:
        write_down(acc, row, hot_ref, msg_ref)
    else:
        write_up(acc, msg_ref)


def other_apply(lst, slab, row, which, other, hots, tiles, acc, step):
    return pl.pallas_call(
        functools.partial(other_kernel, which=which, step=step),
        out_shape=(jax.ShapeDtypeStruct(ACC, F32), MESSAGE),
        in_specs=[smem(), smem(), smem()] + [vmem()] * 4,
        out_specs=(vmem(), vmem()),
        input_output_aliases={6: 0},
        compiler_params=PARAMS,
        name="other",
    )(lst, slab, row, other, hots, tiles, acc)


def step_apply(lst, slab, row, which, pairs, first_pair, hots, tiles, acc, step):
    own, other = pairs[-1]
    before = pairs[-2] if 0 < step < NSLAB else ()
    acc = own_apply(lst, slab, which, own, before, first_pair, tiles, acc, step)
    return other_apply(lst, slab, row, which, other, hots, tiles, acc, step)


def last_own_kernel(lst, slab, tiles_ref, own0, other0, *refs):
    gathered, acc = refs[:5], refs[6]
    for s in range(NSLAB - 1):
        at = 2 * (NSLAB - 2 - s)

        @pl.when(slab[0] == s)
        def _(s=s, at=at):
            if s == 0:
                apply_list(lst, LA, gathered[at : at + 1], tiles_ref, acc)
            apply_list(lst, LBC, gathered[at : at + 1], tiles_ref, acc)
            if s > 0:
                apply_list(lst, LBC + 1, gathered[at + 1 : at + 2], tiles_ref, acc)

    apply_list(lst, V0C, (own0, other0), tiles_ref, acc, late_start(slab, len(ORDER)))


def last_other_kernel(lst, slab, tiles_ref, other_ref, acc_in, acc, msg_ref):
    @pl.when(slab[0] == 0)
    def _():
        apply_list(lst, LA + 1, (other_ref,), tiles_ref, acc)
        apply_list(lst, LBC + 1, (other_ref,), tiles_ref, acc)

    for r in range(NROW):
        for b in range(BLK):
            msg_ref[r, b] = acc[r * BLK + b].astype(BF)


def last_apply(lst, slab, tiles, first_pair, pairs, acc):
    flat = [ref for pair in pairs[NSLAB - 1 :] for ref in pair]
    whole = jax.ShapeDtypeStruct(ACC, F32)
    acc = pl.pallas_call(
        last_own_kernel,
        out_shape=whole,
        in_specs=[smem(), smem()] + [vmem()] * 9,
        out_specs=vmem(),
        input_output_aliases={10: 0},
        compiler_params=PARAMS,
        name="last_own",
    )(lst, slab, tiles, *first_pair, *flat[:-1], acc)
    return pl.pallas_call(
        last_other_kernel,
        out_shape=(whole, jax.ShapeDtypeStruct((NROW, BLK, W, B), BF)),
        in_specs=[smem(), smem()] + [vmem()] * 3,
        out_specs=(vmem(), vmem()),
        input_output_aliases={4: 0},
        compiler_params=PARAMS,
        name="last_other",
    )(lst, slab, tiles, flat[-1], acc)[1]


def split(x):
    high = x.astype(BF)
    rest = x - high.astype(F32)
    return jnp.concatenate([high, rest.astype(BF)], axis=0)


def row_total(rcv_ref, place, b):
    part = rcv_ref[place * NROW, b].astype(F32)
    for r in range(1, NROW):
        part = part + rcv_ref[place * NROW + r, b].astype(F32)
    return part


def down_kernel(rcv_ref, rhs_ref, coef_ref, out_ref):
    for b in range(TGT):
        pulled = row_total(rcv_ref, 0, b) * coef_ref[:, b * B : (b + 1) * B]
        value = (rhs_ref[b] - pulled).astype(BF)
        for z in range(HALF):
            out_ref[z, b] = value


def up_kernel(rcv_ref, coef_ref, hot_ref, out_ref):
    values = jnp.concatenate(
        [
            split(row_total(rcv_ref, 1, b) * coef_ref[:, b * B : (b + 1) * B])
            for b in range(TGT)
        ],
        axis=1,
    )
    total = jnp.dot(values, hot_ref[...], preferred_element_type=F32)
    lifted = -(total[:W] + total[W:])
    for b in range(PRT):
        value = lifted[:, b * B : (b + 1) * B].astype(BF)
        for z in range(HALF):
            out_ref[z, b] = value


def combine(kernel, received, others, blocks):
    return pl.pallas_call(
        kernel,
        out_shape=jax.ShapeDtypeStruct((HALF, blocks, W, B), BF),
        in_specs=[vmem()] * (1 + len(others)),
        out_specs=vmem(),
        compiler_params=PARAMS,
    )(received, *others)


def prepare_kernel(
    count, slab, rhs_hbm, rows_hbm, cols_hbm, map_hbm, coef_hbm,
    out_ref, target_ref, rows_ref, cols_ref, pack_ref,
    rhs_ref, map_ref, coef_ref, sems,
):
    wide = 2 * B
    copies = [
        pltpu.make_async_copy(
            rhs_hbm.at[0, :, pl.ds(k * wide, wide)], rhs_ref.at[k], sems.at[k]
        )
        for k in range(BLK // 2)
    ]
    small = [
        pltpu.make_async_copy(src, dst, sems.at[BLK // 2 + k])
        for k, (src, dst) in enumerate(
            ((rows_hbm, rows_ref), (cols_hbm, cols_ref), (map_hbm, map_ref), (coef_hbm, coef_ref))
        )
    ]
    for copy in copies + small:
        copy.start()
    for b in range(BLK):
        if b % 2 == 0:
            copies[b // 2].wait()
        value = rhs_ref[b // 2, :, b % 2 * B : (b % 2 + 1) * B]
        if b < TGT:
            target_ref[b] = value
            value = jnp.where(slab[0] == 0, value, 0.0)
        value = jnp.where(b < count[0], value, 0.0).astype(BF)
        for z in range(HALF):
            out_ref[z, b] = value
    for copy in small:
        copy.wait()
    pack_ref[0:1, :] = map_ref[...].astype(F32)
    pack_ref[1:2, :] = coef_ref[...]


def prepare(right_sides, section_blocks, slab, tile_rows, tile_cols, plane_map, interface_coef):
    ins = (right_sides, tile_rows, tile_cols, plane_map, interface_coef)
    return pl.pallas_call(
        prepare_kernel,
        out_shape=(
            jax.ShapeDtypeStruct((HALF, BLK, W, B), BF),
            jax.ShapeDtypeStruct((TGT, W, B), F32),
            jax.ShapeDtypeStruct(tile_rows.shape, jnp.int32),
            jax.ShapeDtypeStruct(tile_cols.shape, jnp.int32),
            jax.ShapeDtypeStruct((2, TGT * B), F32),
        ),
        in_specs=[smem(), smem()] + [pl.BlockSpec(memory_space=pltpu.HBM)] * 5,
        out_specs=(vmem(),) * 5,
        scratch_shapes=[
            pltpu.VMEM((BLK // 2, W, 2 * B), F32),
            pltpu.VMEM((1, TGT * B), jnp.int32),
            pltpu.VMEM((1, TGT * B), F32),
            pltpu.SemaphoreType.DMA((BLK // 2 + 4,)),
        ],
        compiler_params=PARAMS,
        name="prepare",
    )(section_blocks, slab, *[pltpu.with_memory_space_constraint(x, pltpu.HBM) for x in ins])


def finish_kernel(count, parts_ref, out_ref):
    for b in range(BLK):
        total = parts_ref[0, b].astype(F32)
        for r in range(1, NROW):
            total = total + parts_ref[r, b].astype(F32)
        out_ref[0, :, b * B : (b + 1) * B] = jnp.where(b < count[0], total, 0.0)


def finish(section_blocks, parts):
    return pl.pallas_call(
        finish_kernel,
        out_shape=jax.ShapeDtypeStruct((1, W, BLK * B), F32),
        in_specs=[smem(), vmem()],
        out_specs=vmem(),
        compiler_params=PARAMS,
        name="finish",
    )(section_blocks, parts)


Z_GROUPS = [[2 * z + k for z in range(HALF)] for k in range(2)]


def gather(copies):
    own = lax.all_to_all(copies, "col", 0, 0, tiled=True, axis_index_groups=Z_GROUPS)
    own = own.reshape(HALF * copies.shape[1], W, B)
    return own, lax.ppermute(own, "col", [(c, c ^ 1) for c in range(NCOL)])


def exchange(message, low):
    groups = [
        [(s + k) % NSLAB * NROW + r for k in range(2) for r in range(NROW)]
        for s in (low, low + 2)
    ]
    return lax.all_to_all(message, ("slab", "row"), 0, 0, tiled=True, axis_index_groups=groups)


def from_next(value, turn):
    pairs = [
        ((s + 1) * NROW + (r + turn) % NROW, s * NROW + r)
        for s in range(NSLAB - 1)
        for r in range(NROW)
    ]
    return lax.ppermute(value, ("slab", "row"), pairs)


def body(right_sides, front_tiles, tile_rows, tile_cols, section_blocks, plane_map, interface_coef):
    slab = lax.axis_index("slab").astype(jnp.int32)
    row = lax.axis_index("row").astype(jnp.int32)
    col = lax.axis_index("col").astype(jnp.int32)
    slab = slab.reshape(1)
    row = row.reshape(1)
    col = col.reshape(1)
    copies, rhs_target, rows, cols, pack = prepare(
        right_sides, section_blocks, slab, tile_rows, tile_cols, plane_map, interface_coef
    )
    packs = [from_next(pack, d) for d in range(NROW)]
    lst = helper(col, rows, cols)
    coef_next = packs[0][1:2]
    maps_next = jnp.concatenate([p[0:1] for p in packs], axis=0).astype(jnp.int32)

    partner = jnp.arange(PRT * B, dtype=jnp.int32)
    hots = (partner[None, :, None] == maps_next[:, None, :]).astype(BF)
    hot_next = (maps_next[0][:, None] == partner[None, :]).astype(BF)

    start = gather(copies)
    tiles = load_tiles(front_tiles[0], start[0])
    start, hots, hot_next, coef_next, rhs_target, lst, tiles = lax.optimization_barrier(
        (start, hots, hot_next, coef_next, rhs_target, lst, tiles)
    )
    acc, msg = first_apply(lst, row, start, hots, tiles)
    pairs = []
    for step in range(2 * NSLAB - 2):
        if step < NSLAB - 1:
            rcv = exchange(msg, step)
            value = combine(down_kernel, rcv, (rhs_target, interface_coef), TGT)
        else:
            rcv = exchange(msg, 2 * NSLAB - 3 - step)
            value = combine(up_kernel, rcv, (coef_next, hot_next), PRT)
        pairs.append(gather(value))
        if step < len(ORDER):
            which = TAB if step < NSLAB - 1 else LA
            acc, msg = step_apply(lst, slab, row, which, pairs, start, hots, tiles, acc, step)
    msg = last_apply(lst, slab, tiles, start, pairs, acc)
    return finish(section_blocks, lax.all_to_all(msg, "row", 0, 0, tiled=True))


def solution(mesh):
    placed = (
        P("slab", None, ("col", "row")),
        P("slab", ("col", "row"), None, None),
        P("slab", ("col", "row")),
        P("slab", ("col", "row")),
        P("slab"),
        P("slab", ("col", "row")),
        P("slab", ("col", "row")),
    )
    return jax.shard_map(
        body, mesh=mesh, in_specs=placed, out_specs=P("slab", None, ("col", "row")), check_vma=False
    )
```
